32 devices in a mesh: dp: 4 (over y, x), loop: 8 (over z, core).
Axes of the slice: x: 2, y: 2, z: 4, core: 2. Of those that a mesh axis runs over, the one named last changes fastest.
Arguments:
- features: bfloat16 [24, 7, 7, 2048], P('loop'), may hold values from -6 to 6
- image_ids: int32 [24], P('loop'), may hold values from 0 to 15
- text_embeds: bfloat16 [16, 1152], P('loop'), may hold values from -6 to 6
- text_ids: int32 [16], replicated, may hold values from 0 to 15, each once
- depth_kernel: bfloat16 [7, 7, 2048], replicated, may hold values from -0.875 to 0.875
- depth_bias: float32 [2048], replicated, may hold values from -3 to 3
- norm_gain: float32 [2048], replicated, may hold values from 0.5 to 2
- w_up: bfloat16 [2048, 4096], P(None, 'dp'), may hold values from -0.125 to 0.125
- w_down: bfloat16 [2048, 4096], P(None, 'dp'), may hold values from -0.09375 to 0.09375
- projection: bfloat16 [2048, 1152], replicated, may hold values from -0.125 to 0.125
- logit_scale: float32 [1], replicated, may hold values from 4 to 16
- logit_bias: float32 [1], replicated, may hold values from -4 to -1
Outputs:
- row_loss: float32 [24], P('loop')
- grad_texts: float32 [16, 1152], P('loop')
- grad_kernel: float32 [7, 7, 2048], replicated
- grad_bias: float32 [2048], replicated
- grad_gain: float32 [2048], replicated
- grad_up: float32 [2048, 4096], P('loop', 'dp')
- grad_down: float32 [2048, 4096], P('loop', 'dp')
- grad_proj: float32 [2048, 1152], P(('dp', 'loop'))
The draws below stay inside these ranges and needn't reach their ends.
Inputs may be any that keep to these rules, and one draw needn't show every extreme that they name: `image_ids`: each image's pair id names one text. `text_ids`: the 16 texts carry distinct pair ids.
All inputs are finite; a program needn't handle non-finite values.
Results may differ from the reference program's by a relative error of at most 0.0065.
Values sent between devices are 32-bit elements; how exact they have to be, the bound alone decides.
A program may use at most 192 MiB of HBM per device.

```python
import math
import jax
import jax.numpy as jnp
from jax import lax

C = 2048
HID = 4096
E = 1152
KERNEL = 7
GRID = 7
IMG_DEV = 3
IMAGES = 24
TEXTS = 16
N_LOOP = 8


def with_ends(array, own_key, low, top_value):
    extent = array.shape
    spot = [jax.random.randint(jax.random.fold_in(own_key, axis), (), 0, extent[axis]) for axis in range(len(extent))]
    array = array.at[tuple(spot)].set(low)
    longest = extent.index(max(extent))
    spot[longest] = (spot[longest] + 1) % extent[longest]
    return array.at[tuple(spot)].set(top_value)


def block_scale(rng, extent, pieces, low, high):
    loudness = 1.0
    for axis_at, parts in pieces:
        heights = jax.random.uniform(jax.random.fold_in(jax.random.fold_in(rng, 6), axis_at), (parts,), jnp.float32, low / len(pieces), high / len(pieces))
        loudness = loudness * jnp.repeat(jnp.exp(heights), extent[axis_at] // parts).reshape((-1,) + (1,) * (len(extent) - 1 - axis_at))
    return loudness


def gaussian(own_key, shape, scale, bound, shards=(), dtype=jnp.bfloat16):
    drawn = jax.random.normal(own_key, shape, jnp.float32) * scale
    if len(shards) > 0:
        drawn = block_scale(own_key, shape, shards, -0.22, 0.18) * drawn
    return jnp.clip(drawn, min=-bound, max=bound).astype(dtype)


def setup_inputs(seed: int = 0) -> dict:
    key_list = jax.random.split(jax.random.key(seed), 13)
    features = gaussian(key_list[0], (IMAGES, GRID, GRID, C), 1.0, 6.0, ((0, 8),))
    image_ids = with_ends(jax.random.randint(key_list[1], (IMAGES,), 0, TEXTS), jax.random.fold_in(key_list[1], 1), 0, TEXTS - 1).astype(jnp.int32)
    text_embeds = gaussian(key_list[2], (TEXTS, E), 1.0, 6.0, ((0, 8),))
    text_ids = jax.random.permutation(key_list[3], TEXTS).astype(jnp.int32)
    depth_kernel = gaussian(key_list[4], (KERNEL, KERNEL, C), (KERNEL * KERNEL) ** -0.5, 0.875)
    depth_bias = gaussian(key_list[5], (C,), 0.5, 3.0, (), jnp.float32)
    norm_gain = jnp.clip(jnp.exp(jax.random.uniform(key_list[6], (C,), jnp.float32, math.log(0.5), math.log(2.0))), 0.5, 2.0)
    w_up = gaussian(key_list[7], (C, HID), C ** -0.5, 0.125, ((1, 4),))
    w_down = gaussian(key_list[8], (C, HID), HID ** -0.5, 0.09375, ((1, 4),))
    projection = gaussian(key_list[9], (C, E), C ** -0.5, 0.125)
    logit_scale = jnp.clip(jnp.exp(jax.random.uniform(key_list[10], (1,), jnp.float32, math.log(4.0), math.log(16.0))), 4.0, 16.0)
    logit_bias = jnp.clip(jax.random.uniform(key_list[11], (1,), jnp.float32, -4.0, -1.0), -4.0, -1.0)
    return dict(features=features, image_ids=image_ids, text_embeds=text_embeds, text_ids=text_ids, depth_kernel=depth_kernel, depth_bias=depth_bias, norm_gain=norm_gain, w_up=w_up, w_down=w_down, projection=projection, logit_scale=logit_scale, logit_bias=logit_bias)


full_precision = lax.Precision.HIGHEST
half_root = 0.7071067811865476
density_factor = 0.3989422804014327

def gelu_value(values):
    return 0.5 * values * (1.0 + lax.erf(values * half_root))

def gelu_slope(values):
    cumulative = 0.5 * (1.0 + lax.erf(values * half_root))
    return cumulative + values * jnp.exp(-0.5 * values * values) * density_factor

def depthwise(images, kernel):
    side = kernel.shape[0]
    reach = (side - 1) // 2
    height = images.shape[1]
    width = images.shape[2]
    padded = jnp.pad(images, ((0, 0), (reach, reach), (reach, reach), (0, 0)))
    total = jnp.zeros(images.shape, jnp.float32)
    for row_off in range(side):
        for col_off in range(side):
            total = total + padded[:, row_off:row_off + height, col_off:col_off + width, :] * kernel[row_off, col_off]
    return total

def kernel_grad(images, grad_conv, side):
    reach = (side - 1) // 2
    height = images.shape[1]
    width = images.shape[2]
    padded = jnp.pad(images, ((0, 0), (reach, reach), (reach, reach), (0, 0)))
    rows_out = []
    for row_off in range(side):
        cols_out = []
        for col_off in range(side):
            window = padded[:, row_off:row_off + height, col_off:col_off + width, :]
            cols_out.append(lax.optimization_barrier(jnp.sum(window * grad_conv, axis=(0, 1, 2))))
        rows_out.append(jnp.stack(cols_out, axis=0))
    return jnp.stack(rows_out, axis=0)

def norm_parts(images, depth_kernel, depth_bias, norm_gain):
    conv_out = depthwise(images.astype(jnp.float32), depth_kernel.astype(jnp.float32)) + depth_bias
    centered = conv_out - lax.optimization_barrier(jnp.mean(conv_out, axis=3, keepdims=True))
    inv_std = lax.rsqrt(lax.optimization_barrier(jnp.mean(centered * centered, axis=3, keepdims=True)) + 1e-06)
    unit_part = centered * inv_std
    normed = (unit_part * norm_gain).astype(jnp.bfloat16)
    return (unit_part, inv_std, normed)

def unit_rows(values):
    inverse = lax.rsqrt(lax.optimization_barrier(jnp.sum(values * values, axis=1, keepdims=True)) + 1e-06)
    return (values * inverse, inverse)

def conv_grads(images, depth_kernel, unit_part, inv_std, norm_gain, grad_normed):
    grad_gain = lax.optimization_barrier(jnp.sum(grad_normed * unit_part, axis=(0, 1, 2)))
    grad_unit = grad_normed * norm_gain
    grad_conv = inv_std * (grad_unit - lax.optimization_barrier(jnp.mean(grad_unit, axis=3, keepdims=True)) - unit_part * lax.optimization_barrier(jnp.mean(grad_unit * unit_part, axis=3, keepdims=True)))
    grad_bias = lax.optimization_barrier(jnp.sum(grad_conv, axis=(0, 1, 2)))
    grad_kernel = kernel_grad(images.astype(jnp.float32), grad_conv, depth_kernel.shape[0])
    return (grad_kernel, grad_bias, grad_gain)

def reference(features, image_ids, text_embeds, text_ids, depth_kernel, depth_bias, norm_gain, w_up, w_down, projection, logit_scale, logit_bias):
    cell_count = GRID * GRID
    groups = features.reshape(N_LOOP, IMG_DEV, GRID, GRID, C)

    def forward_one(images):
        unit_part, inv_std, normed = norm_parts(images, depth_kernel, depth_bias, norm_gain)
        pre_act = jnp.dot(normed.reshape(-1, C), w_up, preferred_element_type=jnp.float32)
        hidden_mean = lax.optimization_barrier(jnp.mean(gelu_value(pre_act).reshape(IMG_DEV, cell_count, HID), axis=1)).astype(jnp.bfloat16)
        mlp_pool = lax.dot_general(hidden_mean, w_down, (((1,), (1,)), ((), ())), preferred_element_type=jnp.float32)
        pooled = (lax.optimization_barrier(jnp.mean(images.astype(jnp.float32), axis=(1, 2))) + mlp_pool).astype(jnp.bfloat16)
        return (pooled, hidden_mean)
    pooled, hidden_mean = lax.map(forward_one, groups)
    pooled = pooled.reshape(IMAGES, C)
    hidden_mean = hidden_mean.reshape(IMAGES, HID)
    embedding = jnp.dot(pooled, projection, preferred_element_type=jnp.float32)
    scale_value = logit_scale[0]
    bias_value = logit_bias[0]
    image_unit, image_inverse = unit_rows(embedding)
    text_unit, text_inverse = unit_rows(text_embeds.astype(jnp.float32))
    logits = scale_value * jnp.dot(image_unit, text_unit.T, precision=full_precision) + bias_value
    labels = jnp.where(image_ids[:, None] == text_ids[None, :], 1.0, -1.0).astype(jnp.float32)
    row_loss = -lax.optimization_barrier(jnp.sum(jax.nn.log_sigmoid(labels * logits), axis=1))
    coeffs = -scale_value * labels * jax.nn.sigmoid(-labels * logits)
    grad_image = jnp.dot(coeffs, text_unit, precision=full_precision)
    grad_text = jnp.dot(coeffs.T, image_unit, precision=full_precision)
    grad_texts = text_inverse * (grad_text - text_unit * lax.optimization_barrier(jnp.sum(text_unit * grad_text, axis=1, keepdims=True)))
    grad_embed = (image_inverse * (grad_image - image_unit * lax.optimization_barrier(jnp.sum(image_unit * grad_image, axis=1, keepdims=True)))).astype(jnp.bfloat16)
    grad_pooled = lax.dot_general(grad_embed, projection, (((1,), (1,)), ((), ())), preferred_element_type=jnp.float32).astype(jnp.bfloat16)
    grad_proj = lax.dot_general(pooled, grad_embed, (((0,), (0,)), ((), ())), preferred_element_type=jnp.float32)
    grad_down = lax.dot_general(grad_pooled, hidden_mean, (((0,), (0,)), ((), ())), preferred_element_type=jnp.float32)
    grad_groups = grad_pooled.reshape(N_LOOP, IMG_DEV, C)

    def backward_step(carry_state, inputs_pair):
        up_total, kernel_total, bias_total, gain_total = carry_state
        images, group_grad = inputs_pair
        unit_part, inv_std, normed = norm_parts(images, depth_kernel, depth_bias, norm_gain)
        normed_rows = normed.reshape(-1, C)
        pre_act = jnp.dot(normed_rows, w_up, preferred_element_type=jnp.float32)
        spread = jnp.dot(group_grad, w_down, preferred_element_type=jnp.float32) / cell_count
        grad_pre = (gelu_slope(pre_act).reshape(IMG_DEV, cell_count, HID) * spread[:, None, :]).reshape(-1, HID).astype(jnp.bfloat16)
        up_part = lax.dot_general(normed_rows, grad_pre, (((0,), (0,)), ((), ())), preferred_element_type=jnp.float32)
        grad_normed = lax.dot_general(grad_pre, w_up, (((1,), (1,)), ((), ())), preferred_element_type=jnp.float32).reshape(images.shape)
        kernel_part, bias_part, gain_part = conv_grads(images, depth_kernel, unit_part, inv_std, norm_gain, grad_normed)
        return ((up_total + up_part, kernel_total + kernel_part, bias_total + bias_part, gain_total + gain_part), jnp.zeros((), jnp.float32))
    start_state = (jnp.zeros((C, HID), jnp.float32), jnp.zeros((KERNEL, KERNEL, C), jnp.float32), jnp.zeros((C,), jnp.float32), jnp.zeros((C,), jnp.float32))
    totals, unused = lax.scan(backward_step, start_state, (groups, grad_groups))
    return (row_loss, grad_texts, totals[1], totals[2], totals[3], totals[0], grad_down, grad_proj)
```

```python
import functools
import jax
import jax.numpy as jnp
from jax import lax
from jax.experimental import pallas as pl
from jax.experimental.pallas import tpu as pltpu
from jax.sharding import PartitionSpec as P

GRID = 7
LANES = 128
ROWS = 8
TAP_ROWS = 64

full_precision = lax.Precision.HIGHEST
half_root = 0.7071067811865476
density_factor = 0.3989422804014327


def gelu_value(values):
    return 0.5 * values * (1.0 + lax.erf(values * half_root))


def gelu_slope(values):
    cumulative = 0.5 * (1.0 + lax.erf(values * half_root))
    return cumulative + values * jnp.exp(-0.5 * values * values) * density_factor


def unit_rows(values):
    inverse = lax.rsqrt(jnp.sum(values * values, axis=1, keepdims=True) + 1e-06)
    return (values * inverse, inverse)


def lane_tile(index):
    return pl.ds(pl.multiple_of(index * LANES, LANES), LANES)


def shifted_rows(x_ref, lanes, by, cell):
    count = x_ref.shape[0]
    moved = []
    for row in range(GRID):
        per_image = []
        for n in range(count):
            tile = x_ref[n, row, :, lanes]
            if by != 0:
                tile = pltpu.roll(tile, (-by) % ROWS, 0)
            if abs(by) > 1:
                inside = (cell + by >= 0) & (cell + by < GRID)
                tile = jnp.where(inside, tile, 0.0)
            per_image.append(tile)
        moved.append(per_image)
    return moved


def conv_norm_kernel(x_ref, k_ref, bias_ref, unit_ref, inv_ref):
    count = x_ref.shape[0]
    channels = x_ref.shape[3]
    tiles = channels // LANES
    reach = (GRID - 1) // 2
    cell = lax.broadcasted_iota(jnp.int32, (ROWS, LANES), 0)
    cells = [(n, p) for p in range(GRID) for n in range(count)]

    def conv_tile(index, sums):
        lanes = lane_tile(index)
        bias = jnp.broadcast_to(bias_ref[:, lanes], (ROWS, LANES))
        out = {at: bias for at in cells}
        for col_off in range(GRID):
            moved = shifted_rows(x_ref, lanes, col_off - reach, cell)
            for row_off in range(GRID):
                tap = row_off * GRID + col_off
                weight = jnp.broadcast_to(k_ref[tap : tap + 1, lanes], (ROWS, LANES))
                for p in range(GRID):
                    row = p + row_off - reach
                    if 0 <= row < GRID:
                        for n in range(count):
                            out[(n, p)] = out[(n, p)] + moved[row][n] * weight
        for n, p in cells:
            unit_ref[n, p, :, lanes] = out[(n, p)]
        return tuple(total + out[at] for total, at in zip(sums, cells))

    zeros = tuple(jnp.zeros((ROWS, LANES), jnp.float32) for _ in cells)
    sums = lax.fori_loop(0, tiles, conv_tile, zeros)
    means = [jnp.sum(total, axis=1, keepdims=True) / channels for total in sums]
    means = [jnp.broadcast_to(mean, (ROWS, LANES)) for mean in means]

    def square_tile(index, sums):
        lanes = lane_tile(index)
        result = []
        for total, mean, (n, p) in zip(sums, means, cells):
            centered = unit_ref[n, p, :, lanes] - mean
            result.append(total + centered * centered)
        return tuple(result)

    squares = lax.fori_loop(0, tiles, square_tile, zeros)
    inverses = []
    for total, (n, p) in zip(squares, cells):
        variance = jnp.sum(total, axis=1, keepdims=True) / channels
        inverse = jnp.broadcast_to(lax.rsqrt(variance + 1e-06), (ROWS, LANES))
        inverse = jnp.where(cell < GRID, inverse, 0.0)
        inv_ref[n, p, :, :] = inverse
        inverses.append(inverse)

    def norm_tile(index, carry):
        lanes = lane_tile(index)
        for inverse, mean, (n, p) in zip(inverses, means, cells):
            unit = (unit_ref[n, p, :, lanes] - mean) * inverse
            unit_ref[n, p, :, lanes] = unit
        return carry

    lax.fori_loop(0, tiles, norm_tile, 0)


def conv_norm(padded, taps, bias):
    count, _, _, channels = padded.shape
    whole = pl.BlockSpec(memory_space=pltpu.VMEM)
    full = jax.ShapeDtypeStruct(padded.shape, jnp.float32)
    return pl.pallas_call(
        conv_norm_kernel,
        out_shape=(
            full,
            jax.ShapeDtypeStruct((count, GRID, ROWS, LANES), jnp.float32),
        ),
        in_specs=[whole] * 3,
        out_specs=(whole, whole),
        compiler_params=pltpu.CompilerParams(vmem_limit_bytes=24 * 1024 * 1024),
    )(padded, taps, bias)


def conv_grad_kernel(x_ref, unit_ref, inv_ref, gain_ref, grad_ref, out_ref, work_ref):
    count = x_ref.shape[0]
    channels = x_ref.shape[3]
    tiles = channels // LANES
    reach = (GRID - 1) // 2
    taps = GRID * GRID
    cell = lax.broadcasted_iota(jnp.int32, (ROWS, LANES), 0)
    cells = [(n, p) for p in range(GRID) for n in range(count)]
    zero = jnp.zeros((ROWS, LANES), jnp.float32)

    def first_tile(index, carry):
        plain, crossed = carry
        lanes = lane_tile(index)
        gain = jnp.broadcast_to(gain_ref[:, lanes], (ROWS, LANES))
        gain_sum = zero
        out_ref[index, 48:TAP_ROWS, :] = jnp.zeros((TAP_ROWS - 48, LANES), jnp.float32)
        plain_out = []
        crossed_out = []
        for at, (n, p) in enumerate(cells):
            unit = unit_ref[n, p, :, lanes]
            grad = grad_ref[n, p, :, lanes]
            gain_sum = gain_sum + grad * unit
            scaled = grad * gain
            plain_out.append(plain[at] + scaled)
            crossed_out.append(crossed[at] + scaled * unit)
        out_ref[index, taps + 1 : taps + 2, :] = jnp.sum(gain_sum, axis=0, keepdims=True)
        return (tuple(plain_out), tuple(crossed_out))

    zeros = tuple(zero for _ in cells)
    plain, crossed = lax.fori_loop(0, tiles, first_tile, (zeros, zeros))
    for at, (n, p) in enumerate(cells):
        first = jnp.sum(plain[at], axis=1, keepdims=True) / channels
        second = jnp.sum(crossed[at], axis=1, keepdims=True) / channels
        work_ref[0, n, p, :, :] = jnp.broadcast_to(first, (ROWS, LANES))
        work_ref[1, n, p, :, :] = jnp.broadcast_to(second, (ROWS, LANES))

    def tap_tile(index, carry):
        lanes = lane_tile(index)
        gain = jnp.broadcast_to(gain_ref[:, lanes], (ROWS, LANES))
        grad_conv = {}
        bias_sum = zero
        for n, p in cells:
            value = inv_ref[n, p, :, :] * (
                grad_ref[n, p, :, lanes] * gain
                - work_ref[0, n, p, :, :]
                - unit_ref[n, p, :, lanes] * work_ref[1, n, p, :, :]
            )
            grad_conv[(n, p)] = value
            bias_sum = bias_sum + value
        out_ref[index, taps : taps + 1, :] = jnp.sum(bias_sum, axis=0, keepdims=True)
        for col_off in range(GRID):
            moved = shifted_rows(x_ref, lanes, col_off - reach, cell)
            for row_off in range(GRID):
                tap = row_off * GRID + col_off
                total = zero
                for p in range(GRID):
                    row = p + row_off - reach
                    if 0 <= row < GRID:
                        for n in range(count):
                            total = total + moved[row][n] * grad_conv[(n, p)]
                out_ref[index, tap : tap + 1, :] = jnp.sum(total, axis=0, keepdims=True)
        return carry

    lax.fori_loop(0, tiles, tap_tile, 0)


def conv_grads(padded, unit, inverse, gain, grad):
    count, _, _, channels = padded.shape
    whole = pl.BlockSpec(memory_space=pltpu.VMEM)
    return pl.pallas_call(
        conv_grad_kernel,
        out_shape=jax.ShapeDtypeStruct((channels // LANES, TAP_ROWS, LANES), jnp.float32),
        in_specs=[whole] * 5,
        out_specs=whole,
        scratch_shapes=[pltpu.VMEM((2, count, GRID, ROWS, LANES), jnp.float32)],
        compiler_params=pltpu.CompilerParams(vmem_limit_bytes=24 * 1024 * 1024),
    )(padded, unit, inverse, gain, grad)


def peer_copies(axis, count, source_of, target, send_sems, recv_sems):
    me = lax.axis_index(axis)
    copies = []
    for by in range(1, count):
        peer = lax.rem(me + by, count)
        copy = pltpu.make_async_remote_copy(
            src_ref=source_of(peer),
            dst_ref=target.at[me],
            send_sem=send_sems.at[by],
            recv_sem=recv_sems.at[by],
            device_id={axis: peer},
            device_id_type=pl.DeviceIdType.MESH,
        )
        copy.start()
        copies.append(copy)
    return copies


def wait_all(copies):
    for copy in copies:
        copy.wait()


def meet_peers(sizes):
    barrier = pltpu.get_barrier_semaphore()
    total = 0
    for axis, count in sizes:
        me = lax.axis_index(axis)
        for by in range(1, count):
            pl.semaphore_signal(
                barrier,
                inc=1,
                device_id={axis: lax.rem(me + by, count)},
                device_id_type=pl.DeviceIdType.MESH,
            )
        total += count - 1
    pl.semaphore_wait(barrier, total)


def head_kernel(
    dp, loop, part_ref, mean_ref, rest_ref, pooled_ref, rest_out_ref, parts, own, sems
):
    meet_peers((("dp", dp), ("loop", loop)))
    loop_me = lax.axis_index("loop")
    dp_me = lax.axis_index("dp")
    dp_copies = peer_copies(
        "dp", dp, lambda peer: part_ref, parts, sems.at[0], sems.at[1]
    )
    rest_copies = peer_copies(
        "loop", loop, lambda peer: rest_ref, rest_out_ref, sems.at[2], sems.at[3]
    )
    parts[dp_me] = part_ref[...]
    rest_out_ref[loop_me] = rest_ref[...]
    wait_all(dp_copies)
    total = parts[0]
    for at in range(1, dp):
        total = total + parts[at]
    own[...] = mean_ref[...] + total
    pooled_copies = peer_copies(
        "loop", loop, lambda peer: own, pooled_ref, sems.at[4], sems.at[5]
    )
    pooled_ref[loop_me] = own[...]
    wait_all(rest_copies)
    wait_all(pooled_copies)


def head_exchange(part, mean, rest):
    dp = lax.axis_size("dp")
    loop = lax.axis_size("loop")
    whole = pl.BlockSpec(memory_space=pltpu.VMEM)
    return pl.pallas_call(
        functools.partial(head_kernel, dp, loop),
        out_shape=(
            jax.ShapeDtypeStruct((loop,) + part.shape, jnp.float32),
            jax.ShapeDtypeStruct((loop,) + rest.shape, jnp.float32),
        ),
        in_specs=[whole] * 3,
        out_specs=(whole, whole),
        scratch_shapes=[
            pltpu.VMEM((dp,) + part.shape, jnp.float32),
            pltpu.VMEM(part.shape, jnp.float32),
            pltpu.SemaphoreType.DMA((6, max(dp, loop))),
        ],
        compiler_params=pltpu.CompilerParams(
            collective_id=0, has_side_effects=True, vmem_limit_bytes=16 * 1024 * 1024
        ),
    )(part, mean, rest)


def total_kernel(dp, loop, part_ref, out_ref, dp_slots, loop_slots, block, chunk, sems):
    meet_peers((("dp", dp), ("loop", loop)))
    loop_me = lax.axis_index("loop")
    dp_me = lax.axis_index("dp")
    copies = peer_copies(
        "dp", dp, lambda peer: part_ref.at[peer], dp_slots, sems.at[0], sems.at[1]
    )
    dp_slots[dp_me] = part_ref[dp_me]
    wait_all(copies)
    total = dp_slots[0]
    for at in range(1, dp):
        total = total + dp_slots[at]
    block[...] = total
    copies = peer_copies(
        "loop", loop, lambda peer: block.at[peer], loop_slots, sems.at[2], sems.at[3]
    )
    loop_slots[loop_me] = block[loop_me]
    wait_all(copies)
    total = loop_slots[0]
    for at in range(1, loop):
        total = total + loop_slots[at]
    chunk[...] = total
    mine = out_ref.at[dp_me]
    copies = peer_copies("loop", loop, lambda peer: chunk, mine, sems.at[4], sems.at[5])
    out_ref[dp_me, loop_me] = chunk[...]
    wait_all(copies)
    copies = peer_copies("dp", dp, lambda peer: mine, out_ref, sems.at[6], sems.at[7])
    wait_all(copies)


def total_sum(part):
    dp = lax.axis_size("dp")
    loop = lax.axis_size("loop")
    rows = part.shape[0] * part.shape[1] // (dp * loop)
    whole = pl.BlockSpec(memory_space=pltpu.VMEM)
    summed = pl.pallas_call(
        functools.partial(total_kernel, dp, loop),
        out_shape=jax.ShapeDtypeStruct((dp, loop, rows, LANES), jnp.float32),
        in_specs=[whole],
        out_specs=whole,
        scratch_shapes=[
            pltpu.VMEM((dp, loop, rows, LANES), jnp.float32),
            pltpu.VMEM((loop, rows, LANES), jnp.float32),
            pltpu.VMEM((loop, rows, LANES), jnp.float32),
            pltpu.VMEM((rows, LANES), jnp.float32),
            pltpu.SemaphoreType.DMA((8, max(dp, loop))),
        ],
        compiler_params=pltpu.CompilerParams(
            collective_id=1, has_side_effects=True, vmem_limit_bytes=32 * 1024 * 1024
        ),
    )(part.reshape(dp, loop, rows, LANES))
    return summed.reshape(part.shape)


def dense_rows(values):
    return values.reshape(-1, LANES)


def general_device(
    features,
    image_ids,
    text_embeds,
    text_ids,
    depth_kernel,
    depth_bias,
    norm_gain,
    w_up,
    w_down,
    projection,
    logit_scale,
    logit_bias,
):
    image_rows = features.shape[0]
    channels = features.shape[3]
    hidden_share = w_up.shape[1]
    cell_count = GRID * GRID
    loop_count = lax.axis_size("loop")
    position = lax.axis_index("loop")
    image_count = image_rows * loop_count
    text_rows = text_embeds.shape[0]
    first_image = position * image_rows
    gather = functools.partial(lax.all_gather, axis_name="loop", axis=0, tiled=True)

    text_unit, text_inverse = unit_rows(text_embeds.astype(jnp.float32))
    cell_mean = jnp.mean(features.astype(jnp.float32), axis=(1, 2))

    padded = jnp.pad(
        features.astype(jnp.float32), ((0, 0), (0, 0), (0, ROWS - GRID), (0, 0))
    )
    gain_row = norm_gain[None, :]
    unit, inverse = conv_norm(
        padded,
        depth_kernel.astype(jnp.float32).reshape(cell_count, channels),
        depth_bias[None, :],
    )
    padded_rows = image_rows * GRID * ROWS
    unit_rows_own = unit.reshape(padded_rows, channels)
    unit_share = lax.all_to_all(unit_rows_own, "loop", split_axis=1, concat_axis=0, tiled=True)
    normed_rows = (unit_rows_own * gain_row).astype(jnp.bfloat16)
    pre_act = jnp.dot(normed_rows, w_up, preferred_element_type=jnp.float32)
    hidden_sum = jnp.sum(
        gelu_value(pre_act).reshape(image_rows, GRID * ROWS, hidden_share), axis=1
    )
    slope = gelu_slope(pre_act)
    hidden_own = (hidden_sum / cell_count).astype(jnp.bfloat16)
    mlp_part = lax.dot_general(
        hidden_own, w_down, (((1,), (1,)), ((), ())), preferred_element_type=jnp.float32
    )
    id_row = jnp.pad(image_ids.astype(jnp.float32), (0, LANES - image_rows))[None, :]
    rest = jnp.concatenate([dense_rows(hidden_sum), dense_rows(text_unit), id_row], axis=0)
    hidden_rows = image_rows * hidden_share // LANES
    text_end = hidden_rows + text_unit.size // LANES
    rest = jnp.pad(rest, ((0, -rest.shape[0] % ROWS), (0, 0)))
    pooled_all, rest_all = head_exchange(dense_rows(mlp_part), dense_rows(cell_mean), rest)
    slope_sent, unit_share, pooled_all = lax.optimization_barrier((slope, unit_share, pooled_all))
    slope_all = gather(slope_sent)
    pooled = pooled_all.reshape(image_count, channels).astype(jnp.bfloat16)
    hidden_all = rest_all[:, :hidden_rows].reshape(image_count, hidden_share)
    hidden_all = (hidden_all / cell_count).astype(jnp.bfloat16)
    text_all = rest_all[:, hidden_rows:text_end].reshape(-1, text_embeds.shape[1])
    ids_all = rest_all[:, text_end, :image_rows].reshape(image_count).astype(jnp.int32)
    embedding = jnp.dot(pooled, projection, preferred_element_type=jnp.float32)
    image_unit, image_inverse = unit_rows(embedding)
    logits = (
        logit_scale[0] * jnp.dot(image_unit, text_all.T, precision=full_precision)
        + logit_bias[0]
    )
    labels = jnp.where(ids_all[:, None] == text_ids[None, :], 1.0, -1.0).astype(jnp.float32)
    loss_all = -jnp.sum(jax.nn.log_sigmoid(labels * logits), axis=1)
    row_loss = lax.dynamic_slice_in_dim(loss_all, first_image, image_rows)
    coeffs = -logit_scale[0] * labels * jax.nn.sigmoid(-labels * logits)
    grad_image = jnp.dot(coeffs, text_all, precision=full_precision)
    own_coeffs = lax.dynamic_slice_in_dim(coeffs, position * text_rows, text_rows, 1)
    grad_text = jnp.dot(own_coeffs.T, image_unit, precision=full_precision)
    grad_texts = text_inverse * (
        grad_text - text_unit * jnp.sum(text_unit * grad_text, axis=1, keepdims=True)
    )
    grad_embed = (
        image_inverse
        * (grad_image - image_unit * jnp.sum(image_unit * grad_image, axis=1, keepdims=True))
    ).astype(jnp.bfloat16)
    grad_pooled = lax.dot_general(
        grad_embed, projection, (((1,), (1,)), ((), ())), preferred_element_type=jnp.float32
    ).astype(jnp.bfloat16)
    spread = jnp.dot(grad_pooled, w_down, preferred_element_type=jnp.float32) / cell_count
    own_spread = lax.dynamic_slice_in_dim(spread, first_image, image_rows)
    grad_pre = (
        (slope.reshape(image_rows, GRID * ROWS, hidden_share) * own_spread[:, None, :])
        .reshape(padded_rows, hidden_share)
        .astype(jnp.bfloat16)
    )
    grad_normed = lax.dot_general(
        grad_pre, w_up, (((1,), (1,)), ((), ())), preferred_element_type=jnp.float32
    ).reshape(padded.shape)
    part = conv_grads(padded, unit, inverse, gain_row, grad_normed)
    total = total_sum(part).transpose(1, 0, 2).reshape(TAP_ROWS, channels)
    grad_kernel = total[:cell_count].reshape(GRID, GRID, channels)
    grad_bias = total[cell_count]
    grad_gain = total[cell_count + 1]

    up_share = channels // loop_count
    grad_pooled_share = lax.dynamic_slice_in_dim(grad_pooled, position * up_share, up_share, 1)
    grad_down = lax.dot_general(
        grad_pooled_share, hidden_all, (((0,), (0,)), ((), ())), preferred_element_type=jnp.float32
    )
    proj_share = up_share // lax.axis_size("dp")
    proj_at = (lax.axis_index("dp") * loop_count + position) * proj_share
    pooled_share = lax.dynamic_slice_in_dim(pooled, proj_at, proj_share, 1)
    grad_proj = lax.dot_general(
        pooled_share, grad_embed, (((0,), (0,)), ((), ())), preferred_element_type=jnp.float32
    )
    grad_pre_all = (
        (slope_all.reshape(image_count, GRID * ROWS, hidden_share) * spread[:, None, :])
        .reshape(loop_count * padded_rows, hidden_share)
        .astype(jnp.bfloat16)
    )
    gain_share = lax.dynamic_slice_in_dim(norm_gain, position * up_share, up_share)
    normed_share = (unit_share * gain_share).astype(jnp.bfloat16)
    grad_up = lax.dot_general(
        normed_share,
        grad_pre_all,
        (((0,), (0,)), ((), ())),
        preferred_element_type=jnp.float32,
    )
    return (row_loss, grad_texts, grad_kernel, grad_bias, grad_gain, grad_up, grad_down, grad_proj)


SPLIT = 128
SIDE = 4
CORES = 2
PACKET = 2304
PART_ROWS = 56
MESH = pl.DeviceIdType.MESH
nn = (((1,), (0,)), ((), ()))
nt = (((1,), (1,)), ((), ()))
tn = (((0,), (0,)), ((), ()))


def product(left, right, dims, precision=None):
    return lax.dot_general(
        left, right, dims, preferred_element_type=jnp.float32, precision=precision
    )


def flipped(index, by):
    if by == 1:
        return index + 1 - 2 * lax.rem(index, 2)
    if by == 2:
        return lax.rem(index + 2, SIDE)
    return SIDE - 1 - index


def columns(start, size):
    return pl.ds(pl.multiple_of(start, LANES), size)


def rounded(values):
    return values.astype(jnp.bfloat16).astype(jnp.float32)


def image_of(first, shape, values):
    cells = GRID * GRID
    row = first + lax.broadcasted_iota(jnp.int32, shape, 0)
    out = jnp.broadcast_to(values[-1], shape)
    for n in reversed(range(len(values) - 1)):
        out = jnp.where(row < (n + 1) * cells, values[n], out)
    return jnp.where(row < len(values) * cells, out, 0.0)


def fused_kernel(
    xb,
    kb,
    wu_hbm,
    wd_hbm,
    pj_hbm,
    bias_ref,
    gain_ref,
    text_ref,
    iid_ref,
    tid_ref,
    scale_ref,
    shift_ref,
    o_loss,
    o_text,
    o_kernel,
    o_bias,
    o_gain,
    o_up,
    o_down,
    o_proj,
    wu,
    wd,
    pj,
    x,
    kf,
    unit,
    inv,
    nf,
    nb,
    pre,
    sl,
    gn,
    full,
    thin,
    far,
    nrow,
    gpre,
    fullb,
    packed,
    packets,
    texts_out,
    texts_in,
    texts,
    part_out,
    part_in,
    means,
    small,
    heads,
    gathered,
    work,
    taps_out,
    taps_in,
    taps_sum,
    taps_z,
    taps_all,
    up_out,
    up_in,
    local_sem,
    send_sem,
    recv_sem,
):
    count, _, _, channels = xb.shape
    hidden = wu.shape[1]
    width = pj.shape[1]
    split = full.shape[1]
    total_rows = nf.shape[0]
    sent_rows = count * GRID * GRID
    sent_rows += -sent_rows % ROWS
    rest_rows = sent_rows - split
    tiles = channels // LANES
    reach = (GRID - 1) // 2
    taps = GRID * GRID
    chip = channels // SIDE
    half = hidden // 2
    dp = lax.axis_index("dp")
    loop = lax.axis_index("loop")
    z = loop // CORES
    core = lax.rem(loop, CORES)
    rank = dp * CORES + core
    planes = SIDE * CORES
    next_sem = [0]

    def take(number):
        first = next_sem[0]
        next_sem[0] += number
        return first

    def remote(src, dst, device, sem):
        return pltpu.make_async_remote_copy(
            src_ref=src,
            dst_ref=dst,
            send_sem=send_sem.at[sem],
            recv_sem=recv_sem.at[sem],
            device_id=device,
            device_id_type=MESH,
        )

    def at_z(index):
        return {"dp": dp, "loop": index * CORES + core}

    def at_dp(index):
        return {"dp": index, "loop": loop}

    def at_rank(index):
        return {"dp": index // CORES, "loop": z * CORES + lax.rem(index, CORES)}

    partner = {"dp": dp, "loop": z * CORES + 1 - core}

    barrier = pltpu.get_barrier_semaphore()
    met = 0
    for by in range(1, planes):
        pl.semaphore_signal(
            barrier, inc=1, device_id={"dp": dp, "loop": lax.rem(loop + by, planes)}, device_id_type=MESH
        )
        met += 1
    for by in range(1, SIDE):
        for other in range(CORES):
            pl.semaphore_signal(
                barrier,
                inc=1,
                device_id={"dp": flipped(dp, by), "loop": z * CORES + other},
                device_id_type=MESH,
            )
            met += 1
    loads = []
    for at, (far_ref, near_ref) in enumerate(((wu_hbm, wu), (wd_hbm, wd), (pj_hbm, pj))):
        copy = pltpu.make_async_copy(far_ref, near_ref, local_sem.at[at])
        copy.start()
        loads.append(copy)

    text = text_ref[...].astype(jnp.float32)
    text_unit, text_inverse = unit_rows(text)
    third = width // 3
    texts_out[...] = jnp.zeros(texts_out.shape, jnp.float32)
    for k in range(3):
        texts_out[2 * k : 2 * k + 2, :] = text_unit[:, k * third : (k + 1) * third]

    cell = lax.broadcasted_iota(jnp.int32, (ROWS, LANES), 0)
    zero = jnp.zeros((ROWS, LANES), jnp.float32)
    cells = [(n, p) for n in range(count) for p in range(GRID)]

    def conv_tile(index, sums):
        lanes = lane_tile(index)
        for n, p in cells:
            x[n, p, 0:GRID, lanes] = xb[n, p, :, lanes].astype(jnp.float32)
            x[n, p, GRID:ROWS, lanes] = jnp.zeros((ROWS - GRID, LANES), jnp.float32)
        for a in range(GRID):
            kf[a * GRID : (a + 1) * GRID, lanes] = kb[a, :, lanes].astype(jnp.float32)
        bias = jnp.broadcast_to(bias_ref[:, lanes], (ROWS, LANES))
        out = {at: bias for at in cells}
        for col_off in range(GRID):
            moved = shifted_rows(x, lanes, col_off - reach, cell)
            for row_off in range(GRID):
                tap = row_off * GRID + col_off
                weight = jnp.broadcast_to(kf[tap : tap + 1, lanes], (ROWS, LANES))
                for p in range(GRID):
                    row = p + row_off - reach
                    if 0 <= row < GRID:
                        for n in range(count):
                            out[(n, p)] = out[(n, p)] + moved[row][n] * weight
        for n, p in cells:
            unit[n, p, :, lanes] = out[(n, p)]
        return tuple(total + out[at] for total, at in zip(sums, cells))

    zeros = tuple(zero for _ in cells)
    sums = lax.fori_loop(0, tiles, conv_tile, zeros)
    centers = [jnp.sum(total, axis=1, keepdims=True) / channels for total in sums]
    centers = [jnp.broadcast_to(mean, (ROWS, LANES)) for mean in centers]

    def square_tile(index, sums):
        lanes = lane_tile(index)
        result = []
        for total, mean, (n, p) in zip(sums, centers, cells):
            centered = unit[n, p, :, lanes] - mean
            result.append(total + centered * centered)
        return tuple(result)

    squares = lax.fori_loop(0, tiles, square_tile, zeros)

    pl.semaphore_wait(barrier, met)
    text_sem = take(planes)
    text_copies = []
    for by in range(1, planes):
        peer = {"dp": dp, "loop": lax.rem(loop + by, planes)}
        copy = remote(texts_out, texts_in.at[loop], peer, text_sem + by)
        copy.start()
        text_copies.append(copy)

    inverses = []
    for total, (n, p) in zip(squares, cells):
        variance = jnp.sum(total, axis=1, keepdims=True) / channels
        inverse = jnp.broadcast_to(lax.rsqrt(variance + 1e-06), (ROWS, LANES))
        inverse = jnp.where(cell < GRID, inverse, 0.0)
        inv[n, p, :, :] = inverse
        inverses.append(inverse)

    edge = total_rows - 2 * ROWS
    nf[edge:total_rows, :] = jnp.zeros((2 * ROWS, channels), jnp.float32)

    def norm_tile(index, carry):
        lanes = lane_tile(index)
        gain = jnp.broadcast_to(gain_ref[:, lanes], (ROWS, LANES))
        for inverse, mean, (n, p) in zip(inverses, centers, cells):
            value = (unit[n, p, :, lanes] - mean) * inverse
            unit[n, p, :, lanes] = value
            first = n * taps + p * GRID
            nf[first : first + ROWS, lanes] = value * gain
        return carry

    lax.fori_loop(0, tiles, norm_tile, 0)

    quarter = channels // SIDE
    slim = chip // SIDE
    own_quarter = columns(dp * quarter, quarter)
    own_slim = columns(dp * slim, slim)
    full_sem = take(SIDE)
    thin_sem = take(SIDE)
    full_copies = {}
    thin_copies = {}
    for by in range(1, SIDE):
        peer = flipped(z, by)
        copy = remote(
            nf.at[pl.ds(0, split), own_quarter],
            full.at[z, :, own_quarter],
            at_z(peer),
            full_sem + by,
        )
        copy.start()
        full_copies[by] = copy
        copy = remote(
            nf.at[pl.ds(split, rest_rows), columns(peer * chip + dp * slim, slim)],
            thin.at[z, pl.ds(0, rest_rows), own_slim],
            at_z(peer),
            thin_sem + by,
        )
        copy.start()
        thin_copies[by] = copy

    def narrow(i, carry):
        rows = pl.ds(pl.multiple_of(i * 2 * ROWS, 2 * ROWS), 2 * ROWS)
        nb[rows, :] = nf[rows, :].astype(jnp.bfloat16)
        return carry

    lax.fori_loop(0, total_rows // (2 * ROWS), narrow, 0)

    loads[0].wait()
    strip = 2 * LANES

    def expand(rows_ref, rows):
        def step(j, carry):
            lanes = pl.ds(pl.multiple_of(j * strip, strip), strip)
            pre[0:rows, lanes] = product(rows_ref[0:rows, :], wu[:, lanes], nn)
            return carry

        lax.fori_loop(0, hidden // strip, step, 0)

    expand(nb, total_rows)

    def activate(i, carry):
        rows = pl.ds(pl.multiple_of((i // 2) * 2 * ROWS, 2 * ROWS), 2 * ROWS)
        lanes = pl.ds(pl.multiple_of(lax.rem(i, 2) * half, LANES), half)
        values = pre[rows, lanes]
        cumulative = 0.5 * (1.0 + lax.erf(values * half_root))
        sl[rows, lanes] = cumulative + values * jnp.exp(-0.5 * values * values) * density_factor
        pre[rows, lanes] = values * cumulative
        return carry

    lax.fori_loop(0, total_rows // ROWS, activate, 0)

    far_sem = take(SIDE)
    far_copies = {}
    for by in range(1, SIDE):
        copy = remote(
            sl.at[pl.ds(split, rest_rows), :],
            far.at[z, pl.ds(0, rest_rows), :],
            at_z(flipped(z, by)),
            far_sem + by,
        )
        copy.start()
        far_copies[by] = copy

    row_wide = lax.broadcasted_iota(jnp.int32, (ROWS, hidden), 0)
    heads[...] = jnp.zeros(heads.shape, jnp.float32)
    for n in range(count):
        begin, end = n * taps, (n + 1) * taps
        total = jnp.zeros((ROWS, hidden), jnp.float32)
        for tile in range(begin // ROWS, -(-end // ROWS)):
            values = pre[tile * ROWS : (tile + 1) * ROWS, :]
            if tile * ROWS < begin:
                values = jnp.where(row_wide >= begin - tile * ROWS, values, 0.0)
            if (tile + 1) * ROWS > end:
                values = jnp.where(row_wide < end - tile * ROWS, values, 0.0)
            total = total + values
        mean = jnp.sum(total, axis=0, keepdims=True) / taps
        heads[n : n + 1, 0:hidden] = rounded(mean)

    loads[1].wait()
    mlp = product(heads[:, 0:hidden].astype(jnp.bfloat16), wd[...], nt)
    part_out[...] = jnp.zeros(part_out.shape, jnp.float32)
    part_out[0:count, :] = mlp[0:count, 0:hidden]
    part_out[count : 2 * count, :] = mlp[0:count, hidden : 2 * hidden]
    part_sem = take(SIDE)
    part_copies = []
    for by in range(1, SIDE):
        copy = remote(part_out, part_in.at[dp], at_dp(flipped(dp, by)), part_sem + by)
        copy.start()
        part_copies.append(copy)
    part_in[dp] = part_out[...]
    means[...] = jnp.zeros(means.shape, jnp.float32)
    for n in range(count):
        total = x[n, 0]
        for p in range(1, GRID):
            total = total + x[n, p]
        mean = jnp.sum(total, axis=0, keepdims=True) / taps
        means[n : n + 1, :] = mean[:, 0:hidden]
        means[count + n : count + n + 1, :] = mean[:, hidden : 2 * hidden]
    for copy in text_copies:
        copy.wait()
    texts_in[loop] = texts_out[...]
    for l in range(planes):
        for k in range(3):
            texts[2 * l : 2 * l + 2, k * third : (k + 1) * third] = texts_in[l, 2 * k : 2 * k + 2, :]
    loads[2].wait()
    small[...] = jnp.zeros(small.shape, jnp.float32)
    for copy in part_copies:
        copy.wait()
    total = part_in[0]
    for at in range(1, SIDE):
        total = total + part_in[at]
    pooled = rounded(means[...] + total)
    small[0:count, 0:hidden] = pooled[0:count, :]
    small[0:count, hidden : 2 * hidden] = pooled[count : 2 * count, :]

    embedding = product(small[...].astype(jnp.bfloat16), pj[...], nn)[0:ROWS, :]
    image_unit, image_inverse = unit_rows(embedding)
    all_texts = texts[...]
    text_count = all_texts.shape[0]
    scale = scale_ref[...]
    logits = scale * product(image_unit, all_texts, nt, full_precision) + shift_ref[...]
    ids = jnp.broadcast_to(iid_ref[...].astype(jnp.float32), (ROWS, count))
    spot_row = lax.broadcasted_iota(jnp.int32, (ROWS, count), 0)
    spot_col = lax.broadcasted_iota(jnp.int32, (ROWS, count), 1)
    own_ids = jnp.sum(jnp.where(spot_row == spot_col, ids, 0.0), axis=1, keepdims=True)
    same = jnp.broadcast_to(own_ids, (ROWS, text_count)) == jnp.broadcast_to(
        tid_ref[...].astype(jnp.float32), (ROWS, text_count)
    )
    labels = jnp.where(same, 1.0, -1.0)
    signed = labels * logits
    losses = jnp.log1p(jnp.exp(-jnp.abs(signed))) - jnp.minimum(signed, 0.0)
    loss = jnp.broadcast_to(jnp.sum(losses, axis=1, keepdims=True), (ROWS, LANES))
    lane_at = lax.broadcasted_iota(jnp.int32, (ROWS, LANES), 1)
    o_loss[...] = jnp.sum(jnp.where(cell == lane_at, loss, 0.0), axis=0, keepdims=True)
    coeffs = -scale * labels * lax.logistic(-signed)
    grad_image = product(coeffs, all_texts, nn, full_precision)
    own_row = lax.broadcasted_iota(jnp.int32, (ROWS, width), 0)
    grad_embed = image_inverse * (
        grad_image - image_unit * jnp.sum(image_unit * grad_image, axis=1, keepdims=True)
    )
    grad_embed = jnp.where(own_row < count, rounded(grad_embed), 0.0)
    grad_text = product(coeffs, image_unit, tn, full_precision)
    heads[0:ROWS, hidden : hidden + width] = grad_embed
    grad_pooled = product(heads[:, hidden : hidden + width].astype(jnp.bfloat16), pj[...], nt)
    grad_pooled = grad_pooled.astype(jnp.bfloat16)
    spread = product(grad_pooled, wd[...], nn) / taps
    grad_pooled = grad_pooled.astype(jnp.float32)

    for at in range(SIDE):
        packed[at, 0:count, 0:chip] = grad_pooled[0:count, at * chip : (at + 1) * chip]
        packed[at, 0:count, chip : chip + LANES] = small[
            0:count, columns(dp * quarter + at * LANES, LANES)
        ]
        packed[at, 0:count, chip + LANES : chip + LANES + width] = grad_embed[0:count, :]
        packed[at, count : 2 * count, 0:hidden] = heads[0:count, 0:hidden]
        packed[at, count : 2 * count, hidden : 2 * hidden] = spread[0:count, :]
        packed[at, 6:8, 0:width] = grad_text[4 * at : 4 * at + 2, :]
        packed[at, 6:8, width : 2 * width] = grad_text[4 * at + 2 : 4 * at + 4, :]
    packet_sem = take(SIDE)
    packet_copies = {}
    for by in range(1, SIDE):
        peer = flipped(z, by)
        copy = remote(packed.at[peer], packets.at[core, z], at_z(peer), packet_sem + by)
        copy.start()
        packet_copies[by] = copy
    packets[core, z] = packed[z]

    full_pass_sem = take(SIDE * SIDE)
    thin_pass_sem = take(SIDE * SIDE)
    passed = {}

    def pass_on(by):
        peer = flipped(z, by)
        full_copies[by].wait()
        thin_copies[by].wait()
        passed[by] = []
        for to in range(1, SIDE):
            device = at_dp(flipped(dp, to))
            for ref, first, lanes in (
                (full.at[peer, :, own_quarter], full_pass_sem, None),
                (thin.at[peer, pl.ds(0, rest_rows), own_slim], thin_pass_sem, None),
            ):
                copy = remote(ref, ref, device, first + by * SIDE + to)
                copy.start()
                passed[by].append(copy)

    pass_on(1)

    spreads = [spread[n : n + 1, :] for n in range(count)]

    def own_slopes(i, carry):
        first = pl.multiple_of(i * 2 * ROWS, 2 * ROWS)
        rows = pl.ds(first, 2 * ROWS)
        for lanes in (slice(0, half), slice(half, hidden)):
            scaled = image_of(first, (2 * ROWS, half), [s[:, lanes] for s in spreads])
            gpre[rows, lanes] = (sl[rows, lanes] * scaled).astype(jnp.bfloat16)
        return carry

    lax.fori_loop(0, total_rows // (2 * ROWS), own_slopes, 0)

    def contract(j, carry):
        lanes = pl.ds(pl.multiple_of(j * strip, strip), strip)
        gn[:, lanes] = product(gpre[0:total_rows, :], wu[lanes, :], nt)
        return carry

    lax.fori_loop(0, channels // strip, contract, 0)
    own_chip = columns(z * chip, chip)
    nrow[0:total_rows, :] = nb[:, own_chip]
    pass_on(2)

    def first_tile(index, carry):
        plain, crossed = carry
        lanes = lane_tile(index)
        gain = jnp.broadcast_to(gain_ref[:, lanes], (ROWS, LANES))
        gain_sum = zero
        taps_out[index, 48:PART_ROWS, :] = jnp.zeros((PART_ROWS - 48, LANES), jnp.float32)
        plain_out = []
        crossed_out = []
        for at, (n, p) in enumerate(cells):
            first = n * taps + p * GRID
            value = unit[n, p, :, lanes]
            grad = gn[first : first + ROWS, lanes]
            gain_sum = gain_sum + grad * value
            scaled = grad * gain
            plain_out.append(plain[at] + scaled)
            crossed_out.append(crossed[at] + scaled * value)
        taps_out[index, taps + 1 : taps + 2, :] = jnp.sum(gain_sum, axis=0, keepdims=True)
        return (tuple(plain_out), tuple(crossed_out))

    plain, crossed = lax.fori_loop(0, tiles, first_tile, (zeros, zeros))
    for at, (n, p) in enumerate(cells):
        first = jnp.sum(plain[at], axis=1, keepdims=True) / channels
        second = jnp.sum(crossed[at], axis=1, keepdims=True) / channels
        work[0, n, p, :, :] = jnp.broadcast_to(first, (ROWS, LANES))
        work[1, n, p, :, :] = jnp.broadcast_to(second, (ROWS, LANES))

    own_tiles = tiles // planes
    sent_tiles = tiles - own_tiles
    taps_sem = take(sent_tiles)

    def taps_copy(i):
        owner = lax.rem(rank + 1 + i // own_tiles, planes)
        return remote(
            taps_out.at[owner * own_tiles + lax.rem(i, own_tiles)],
            taps_in.at[rank, lax.rem(i, own_tiles)],
            at_rank(owner),
            taps_sem + i,
        )

    def tap_tile(i, carry):
        index = lax.rem(rank * own_tiles + own_tiles + i, tiles)
        lanes = lane_tile(index)
        gain = jnp.broadcast_to(gain_ref[:, lanes], (ROWS, LANES))
        grad_conv = {}
        bias_sum = zero
        for n, p in cells:
            first = n * taps + p * GRID
            value = inv[n, p, :, :] * (
                gn[first : first + ROWS, lanes] * gain
                - work[0, n, p, :, :]
                - unit[n, p, :, lanes] * work[1, n, p, :, :]
            )
            grad_conv[(n, p)] = value
            bias_sum = bias_sum + value
        taps_out[index, taps : taps + 1, :] = jnp.sum(bias_sum, axis=0, keepdims=True)
        for col_off in range(GRID):
            moved = shifted_rows(x, lanes, col_off - reach, cell)
            for row_off in range(GRID):
                tap = row_off * GRID + col_off
                total = zero
                for p in range(GRID):
                    row = p + row_off - reach
                    if 0 <= row < GRID:
                        for n in range(count):
                            total = total + moved[row][n] * grad_conv[(n, p)]
                taps_out[index, tap : tap + 1, :] = jnp.sum(total, axis=0, keepdims=True)

        @pl.when(i < sent_tiles)
        def _():
            taps_copy(i).start()

        return carry

    lax.fori_loop(0, tiles, tap_tile, 0)
    pass_on(3)

    def taps_wait(i, carry):
        taps_copy(i).wait()
        return carry

    lax.fori_loop(0, sent_tiles, taps_wait, 0)
    for k in range(own_tiles):
        total = taps_out[rank * own_tiles + k]
        for by in range(1, planes):
            total = total + taps_in[lax.rem(rank + by, planes), k]
        taps_sum[k] = total
    along_sem = take(SIDE)
    along_copies = []
    for by in range(1, SIDE):
        copy = remote(taps_sum, taps_z.at[z], at_z(flipped(z, by)), along_sem + by)
        copy.start()
        along_copies.append(copy)
    taps_z[z] = taps_sum[...]

    for by in range(1, SIDE):
        packet_copies[by].wait()
    cross_sem = take(1)
    cross = remote(packets.at[core], packets.at[core], partner, cross_sem)
    cross.start()

    def other_rows(by):
        peer = flipped(z, by)
        base = by * total_rows
        for copy in passed[by]:
            copy.wait()
        far_copies[by].wait()

        def cast(i, carry):
            first = pl.multiple_of(i * 2 * ROWS, 2 * ROWS)
            rows = pl.ds(first, 2 * ROWS)
            fullb[rows, :] = full[peer, rows, :].astype(jnp.bfloat16)
            nrow[pl.ds(base + first, 2 * ROWS), :] = full[peer, rows, own_chip].astype(jnp.bfloat16)
            return carry

        lax.fori_loop(0, split // (2 * ROWS), cast, 0)
        expand(fullb, split)
        spreads = [
            packets[core, peer, count + n : count + n + 1, hidden : 2 * hidden] for n in range(count)
        ]

        def slopes(i, carry):
            first = pl.multiple_of(i * 2 * ROWS, 2 * ROWS)
            for lanes in (slice(0, half), slice(half, hidden)):
                scaled = image_of(first, (2 * ROWS, half), [s[:, lanes] for s in spreads])
                values = gelu_slope(pre[pl.ds(first, 2 * ROWS), lanes]) * scaled
                gpre[pl.ds(base + first, 2 * ROWS), lanes] = values.astype(jnp.bfloat16)
            return carry

        lax.fori_loop(0, split // (2 * ROWS), slopes, 0)
        for i in range((total_rows - split) // (2 * ROWS)):
            first = i * 2 * ROWS
            at = split + first
            rows = slice(first, first + 2 * ROWS)
            keep = lax.broadcasted_iota(jnp.int32, (2 * ROWS, chip), 0) + at < count * taps
            values = jnp.where(keep, thin[peer, rows, :], 0.0)
            nrow[base + at : base + at + 2 * ROWS, :] = values.astype(jnp.bfloat16)
            for lanes in (slice(0, half), slice(half, hidden)):
                keep = lax.broadcasted_iota(jnp.int32, (2 * ROWS, half), 0) + at < count * taps
                scaled = image_of(at, (2 * ROWS, half), [s[:, lanes] for s in spreads])
                values = jnp.where(keep, far[peer, rows, lanes] * scaled, 0.0)
                gpre[base + at : base + at + 2 * ROWS, lanes] = values.astype(jnp.bfloat16)

    other_rows(1)

    for copy in along_copies:
        copy.wait()
    for k in range(own_tiles):
        total = taps_z[0, k]
        for at in range(1, SIDE):
            total = total + taps_z[at, k]
        taps_all[rank * own_tiles + k] = total
    spread_sem = take(planes)
    mine = taps_all.at[pl.ds(rank * own_tiles, own_tiles)]
    spread_copies = []
    for by in range(1, planes):
        copy = remote(mine, mine, at_rank(lax.rem(rank + by, planes)), spread_sem + by)
        copy.start()
        spread_copies.append(copy)

    other_rows(2)

    cross.wait()

    def collect(lanes, shift, first_lane):
        for other in range(CORES):
            for at in range(SIDE):
                values = packets[other, at, :, lanes]
                if shift:
                    values = pltpu.roll(values, ROWS - shift, 0)
                keep = lax.broadcasted_iota(jnp.int32, values.shape, 0) < count
                first = (other * SIDE + at) * ROWS
                gathered[first : first + ROWS, first_lane : first_lane + values.shape[1]] = jnp.where(
                    keep, values, 0.0
                )

    share = chip // CORES
    collect(columns(core * share, share), 0, 0)
    collect(slice(chip, chip + LANES + width), 0, share)
    collect(slice(0, hidden), count, share + LANES + width)
    end = share + LANES + width
    o_down[...] = product(
        gathered[:, 0:share].astype(jnp.bfloat16), gathered[:, end : end + hidden].astype(jnp.bfloat16), tn
    )
    proj_two = product(
        gathered[:, share : share + LANES].astype(jnp.bfloat16),
        gathered[:, share + LANES : end].astype(jnp.bfloat16),
        tn,
    )
    proj_rows = LANES // CORES
    gn[0:LANES, 0:width] = proj_two
    o_proj[...] = gn[pl.ds(pl.multiple_of(core * proj_rows, proj_rows), proj_rows), 0:width]
    total = jnp.zeros((ROWS, width), jnp.float32)
    for at in range(SIDE):
        for other in range(CORES):
            total = total + packets[other, at, :, columns(core * width, width)]
    grad_text = total[6:8, :]
    o_text[...] = text_inverse * (
        grad_text - text_unit * jnp.sum(text_unit * grad_text, axis=1, keepdims=True)
    )

    other_rows(3)

    def up_strip(rows_at, j):
        lanes = pl.ds(pl.multiple_of(j * strip, strip), strip)
        return lanes, product(nrow[:, rows_at], gpre[:, lanes], tn)

    theirs = columns((1 - core) * share, share)
    ours = columns(core * share, share)
    steps = hidden // strip
    up_sem = take(steps)

    def up_copy(j):
        return remote(up_out.at[j], up_in.at[j], partner, up_sem + j)

    def up_send(j, carry):
        lanes, values = up_strip(theirs, j)
        up_out[j] = values
        up_copy(j).start()
        return carry

    lax.fori_loop(0, steps, up_send, 0)

    def up_own(j, carry):
        lanes, values = up_strip(ours, j)
        o_up[:, lanes] = values
        return carry

    lax.fori_loop(0, steps, up_own, 0)

    for copy in spread_copies:
        copy.wait()
    for index in range(tiles):
        lanes = slice(index * LANES, (index + 1) * LANES)
        for a in range(GRID):
            o_kernel[a, :, lanes] = taps_all[index, a * GRID : (a + 1) * GRID, :]
        o_bias[:, lanes] = taps_all[index, taps : taps + 1, :]
        o_gain[:, lanes] = taps_all[index, taps + 1 : taps + 2, :]

    def up_add(j, carry):
        lanes = pl.ds(pl.multiple_of(j * strip, strip), strip)
        up_copy(j).wait()
        o_up[:, lanes] = o_up[:, lanes] + up_in[j]
        return carry

    lax.fori_loop(0, steps, up_add, 0)


def fused_device(
    features,
    image_ids,
    text_embeds,
    text_ids,
    depth_kernel,
    depth_bias,
    norm_gain,
    w_up,
    w_down,
    projection,
    logit_scale,
    logit_bias,
):
    count, _, _, channels = features.shape
    hidden = w_up.shape[1]
    width = projection.shape[1]
    texts = text_ids.shape[0]
    text_rows = text_embeds.shape[0]
    cells = count * GRID * GRID
    rows = cells + -cells % (2 * ROWS)
    chip = channels // SIDE
    share = chip // CORES
    strip = 2 * LANES
    planes = SIDE * CORES
    own_tiles = channels // LANES // planes
    whole = pl.BlockSpec(memory_space=pltpu.VMEM)
    outside = pl.BlockSpec(memory_space=pl.ANY)

    def room(*shape):
        return pltpu.VMEM(shape, jnp.float32)

    def narrow(*shape):
        return pltpu.VMEM(shape, jnp.bfloat16)

    def result(*shape):
        return jax.ShapeDtypeStruct(shape, jnp.float32)

    loss, grad_texts, grad_kernel, grad_bias, grad_gain, grad_up, grad_down, grad_proj = pl.pallas_call(
        fused_kernel,
        out_shape=(
            result(1, LANES),
            result(text_rows, width),
            result(GRID, GRID, channels),
            result(1, channels),
            result(1, channels),
            result(share, hidden),
            result(share, hidden),
            result(LANES // CORES, width),
        ),
        in_specs=[whole] * 2 + [outside] * 3 + [whole] * 7,
        out_specs=(whole,) * 8,
        scratch_shapes=[
            narrow(channels, hidden),
            narrow(channels, hidden),
            narrow(channels, width),
            room(count, GRID, ROWS, channels),
            room(PART_ROWS, channels),
            room(count, GRID, ROWS, channels),
            room(count, GRID, ROWS, LANES),
            room(rows, channels),
            narrow(rows, channels),
            room(rows, hidden),
            room(rows, hidden),
            room(rows, channels),
            room(SIDE, SPLIT, channels),
            room(SIDE, rows - SPLIT, chip),
            room(SIDE, rows - SPLIT, hidden),
            narrow(SIDE * rows, chip),
            narrow(SIDE * rows, hidden),
            narrow(SPLIT, channels),
            room(SIDE, ROWS, PACKET),
            room(CORES, SIDE, ROWS, PACKET),
            room(ROWS, width // 3),
            room(planes, ROWS, width // 3),
            room(texts, width),
            room(ROWS, hidden),
            room(SIDE, ROWS, hidden),
            room(ROWS, hidden),
            room(2 * ROWS, channels),
            room(2 * ROWS, hidden + width),
            room(planes * ROWS, share + LANES + width + hidden),
            room(2, count, GRID, ROWS, LANES),
            room(channels // LANES, PART_ROWS, LANES),
            room(planes, own_tiles, PART_ROWS, LANES),
            room(own_tiles, PART_ROWS, LANES),
            room(SIDE, own_tiles, PART_ROWS, LANES),
            room(channels // LANES, PART_ROWS, LANES),
            room(hidden // strip, share, strip),
            room(hidden // strip, share, strip),
            pltpu.SemaphoreType.DMA((3,)),
            pltpu.SemaphoreType.DMA((128,)),
            pltpu.SemaphoreType.DMA((128,)),
        ],
        compiler_params=pltpu.CompilerParams(
            collective_id=2, has_side_effects=True, vmem_limit_bytes=56 * 1024 * 1024
        ),
    )(
        features,
        depth_kernel,
        w_up,
        w_down,
        projection,
        depth_bias[None, :],
        norm_gain[None, :],
        text_embeds,
        image_ids[None, :],
        text_ids[None, :],
        logit_scale[None, :],
        logit_bias[None, :],
    )
    return (
        loss[0, :count],
        grad_texts,
        grad_kernel,
        grad_bias[0],
        grad_gain[0],
        grad_up,
        grad_down,
        grad_proj,
    )


def fits_fused(mesh):
    return mesh.shape["dp"] == SIDE and mesh.shape["loop"] == SIDE * CORES


def solution(mesh):
    placed = (
        P("loop", None, None, None),
        P("loop"),
        P("loop", None),
        P(),
        P(),
        P(),
        P(),
        P(None, "dp"),
        P(None, "dp"),
        P(),
        P(),
        P(),
    )
    fused = fits_fused(mesh)
    return jax.shard_map(
        fused_device if fused else general_device,
        mesh=mesh,
        in_specs=placed,
        out_specs=(
            P("loop"),
            P("loop", None),
            P(),
            P(),
            P(),
            P("loop", "dp"),
            P("loop", "dp"),
            P(("dp", "loop"), None),
        ),
        check_vma=False,
    )
```

```python
import functools
import jax
import jax.numpy as jnp
from jax import lax
from jax.experimental import pallas as pl
from jax.experimental.pallas import tpu as pltpu
from jax.sharding import PartitionSpec as P

GRID = 7
LANES = 128
ROWS = 8
TAP_ROWS = 64

full_precision = lax.Precision.HIGHEST
half_root = 0.7071067811865476
density_factor = 0.3989422804014327


def gelu_value(values):
    return 0.5 * values * (1.0 + lax.erf(values * half_root))


def gelu_slope(values):
    cumulative = 0.5 * (1.0 + lax.erf(values * half_root))
    return cumulative + values * jnp.exp(-0.5 * values * values) * density_factor


def unit_rows(values):
    inverse = lax.rsqrt(jnp.sum(values * values, axis=1, keepdims=True) + 1e-06)
    return (values * inverse, inverse)


def lane_tile(index):
    return pl.ds(pl.multiple_of(index * LANES, LANES), LANES)


def shifted_rows(x_ref, lanes, by, cell):
    count = x_ref.shape[0]
    moved = []
    for row in range(GRID):
        per_image = []
        for n in range(count):
            tile = x_ref[n, row, :, lanes]
            if by != 0:
                tile = pltpu.roll(tile, (-by) % ROWS, 0)
            if abs(by) > 1:
                inside = (cell + by >= 0) & (cell + by < GRID)
                tile = jnp.where(inside, tile, 0.0)
            per_image.append(tile)
        moved.append(per_image)
    return moved


def conv_norm_kernel(x_ref, k_ref, bias_ref, unit_ref, inv_ref):
    count = x_ref.shape[0]
    channels = x_ref.shape[3]
    tiles = channels // LANES
    reach = (GRID - 1) // 2
    cell = lax.broadcasted_iota(jnp.int32, (ROWS, LANES), 0)
    cells = [(n, p) for p in range(GRID) for n in range(count)]

    def conv_tile(index, sums):
        lanes = lane_tile(index)
        bias = jnp.broadcast_to(bias_ref[:, lanes], (ROWS, LANES))
        out = {at: bias for at in cells}
        for col_off in range(GRID):
            moved = shifted_rows(x_ref, lanes, col_off - reach, cell)
            for row_off in range(GRID):
                tap = row_off * GRID + col_off
                weight = jnp.broadcast_to(k_ref[tap : tap + 1, lanes], (ROWS, LANES))
                for p in range(GRID):
                    row = p + row_off - reach
                    if 0 <= row < GRID:
                        for n in range(count):
                            out[(n, p)] = out[(n, p)] + moved[row][n] * weight
        for n, p in cells:
            unit_ref[n, p, :, lanes] = out[(n, p)]
        return tuple(total + out[at] for total, at in zip(sums, cells))

    zeros = tuple(jnp.zeros((ROWS, LANES), jnp.float32) for _ in cells)
    sums = lax.fori_loop(0, tiles, conv_tile, zeros)
    means = [jnp.sum(total, axis=1, keepdims=True) / channels for total in sums]
    means = [jnp.broadcast_to(mean, (ROWS, LANES)) for mean in means]

    def square_tile(index, sums):
        lanes = lane_tile(index)
        result = []
        for total, mean, (n, p) in zip(sums, means, cells):
            centered = unit_ref[n, p, :, lanes] - mean
            result.append(total + centered * centered)
        return tuple(result)

    squares = lax.fori_loop(0, tiles, square_tile, zeros)
    inverses = []
    for total, (n, p) in zip(squares, cells):
        variance = jnp.sum(total, axis=1, keepdims=True) / channels
        inverse = jnp.broadcast_to(lax.rsqrt(variance + 1e-06), (ROWS, LANES))
        inverse = jnp.where(cell < GRID, inverse, 0.0)
        inv_ref[n, p, :, :] = inverse
        inverses.append(inverse)

    def norm_tile(index, carry):
        lanes = lane_tile(index)
        for inverse, mean, (n, p) in zip(inverses, means, cells):
            unit = (unit_ref[n, p, :, lanes] - mean) * inverse
            unit_ref[n, p, :, lanes] = unit
        return carry

    lax.fori_loop(0, tiles, norm_tile, 0)


def conv_norm(padded, taps, bias):
    count, _, _, channels = padded.shape
    whole = pl.BlockSpec(memory_space=pltpu.VMEM)
    full = jax.ShapeDtypeStruct(padded.shape, jnp.float32)
    return pl.pallas_call(
        conv_norm_kernel,
        out_shape=(
            full,
            jax.ShapeDtypeStruct((count, GRID, ROWS, LANES), jnp.float32),
        ),
        in_specs=[whole] * 3,
        out_specs=(whole, whole),
        compiler_params=pltpu.CompilerParams(vmem_limit_bytes=24 * 1024 * 1024),
    )(padded, taps, bias)


def conv_grad_kernel(x_ref, unit_ref, inv_ref, gain_ref, grad_ref, out_ref, work_ref):
    count = x_ref.shape[0]
    channels = x_ref.shape[3]
    tiles = channels // LANES
    reach = (GRID - 1) // 2
    taps = GRID * GRID
    cell = lax.broadcasted_iota(jnp.int32, (ROWS, LANES), 0)
    cells = [(n, p) for p in range(GRID) for n in range(count)]
    zero = jnp.zeros((ROWS, LANES), jnp.float32)

    def first_tile(index, carry):
        plain, crossed = carry
        lanes = lane_tile(index)
        gain = jnp.broadcast_to(gain_ref[:, lanes], (ROWS, LANES))
        gain_sum = zero
        out_ref[index, 48:TAP_ROWS, :] = jnp.zeros((TAP_ROWS - 48, LANES), jnp.float32)
        plain_out = []
        crossed_out = []
        for at, (n, p) in enumerate(cells):
            unit = unit_ref[n, p, :, lanes]
            grad = grad_ref[n, p, :, lanes]
            gain_sum = gain_sum + grad * unit
            scaled = grad * gain
            plain_out.append(plain[at] + scaled)
            crossed_out.append(crossed[at] + scaled * unit)
        out_ref[index, taps + 1 : taps + 2, :] = jnp.sum(gain_sum, axis=0, keepdims=True)
        return (tuple(plain_out), tuple(crossed_out))

    zeros = tuple(zero for _ in cells)
    plain, crossed = lax.fori_loop(0, tiles, first_tile, (zeros, zeros))
    for at, (n, p) in enumerate(cells):
        first = jnp.sum(plain[at], axis=1, keepdims=True) / channels
        second = jnp.sum(crossed[at], axis=1, keepdims=True) / channels
        work_ref[0, n, p, :, :] = jnp.broadcast_to(first, (ROWS, LANES))
        work_ref[1, n, p, :, :] = jnp.broadcast_to(second, (ROWS, LANES))

    def tap_tile(index, carry):
        lanes = lane_tile(index)
        gain = jnp.broadcast_to(gain_ref[:, lanes], (ROWS, LANES))
        grad_conv = {}
        bias_sum = zero
        for n, p in cells:
            value = inv_ref[n, p, :, :] * (
                grad_ref[n, p, :, lanes] * gain
                - work_ref[0, n, p, :, :]
                - unit_ref[n, p, :, lanes] * work_ref[1, n, p, :, :]
            )
            grad_conv[(n, p)] = value
            bias_sum = bias_sum + value
        out_ref[index, taps : taps + 1, :] = jnp.sum(bias_sum, axis=0, keepdims=True)
        for col_off in range(GRID):
            moved = shifted_rows(x_ref, lanes, col_off - reach, cell)
            for row_off in range(GRID):
                tap = row_off * GRID + col_off
                total = zero
                for p in range(GRID):
                    row = p + row_off - reach
                    if 0 <= row < GRID:
                        for n in range(count):
                            total = total + moved[row][n] * grad_conv[(n, p)]
                out_ref[index, tap : tap + 1, :] = jnp.sum(total, axis=0, keepdims=True)
        return carry

    lax.fori_loop(0, tiles, tap_tile, 0)


def conv_grads(padded, unit, inverse, gain, grad):
    count, _, _, channels = padded.shape
    whole = pl.BlockSpec(memory_space=pltpu.VMEM)
    return pl.pallas_call(
        conv_grad_kernel,
        out_shape=jax.ShapeDtypeStruct((channels // LANES, TAP_ROWS, LANES), jnp.float32),
        in_specs=[whole] * 5,
        out_specs=whole,
        scratch_shapes=[pltpu.VMEM((2, count, GRID, ROWS, LANES), jnp.float32)],
        compiler_params=pltpu.CompilerParams(vmem_limit_bytes=24 * 1024 * 1024),
    )(padded, unit, inverse, gain, grad)


def peer_copies(axis, count, source_of, target, send_sems, recv_sems):
    me = lax.axis_index(axis)
    copies = []
    for by in range(1, count):
        peer = lax.rem(me + by, count)
        copy = pltpu.make_async_remote_copy(
            src_ref=source_of(peer),
            dst_ref=target.at[me],
            send_sem=send_sems.at[by],
            recv_sem=recv_sems.at[by],
            device_id={axis: peer},
            device_id_type=pl.DeviceIdType.MESH,
        )
        copy.start()
        copies.append(copy)
    return copies


def wait_all(copies):
    for copy in copies:
        copy.wait()


def meet_peers(sizes):
    barrier = pltpu.get_barrier_semaphore()
    total = 0
    for axis, count in sizes:
        me = lax.axis_index(axis)
        for by in range(1, count):
            pl.semaphore_signal(
                barrier,
                inc=1,
                device_id={axis: lax.rem(me + by, count)},
                device_id_type=pl.DeviceIdType.MESH,
            )
        total += count - 1
    pl.semaphore_wait(barrier, total)


def head_kernel(
    dp, loop, part_ref, mean_ref, rest_ref, pooled_ref, rest_out_ref, parts, own, sems
):
    meet_peers((("dp", dp), ("loop", loop)))
    loop_me = lax.axis_index("loop")
    dp_me = lax.axis_index("dp")
    dp_copies = peer_copies(
        "dp", dp, lambda peer: part_ref, parts, sems.at[0], sems.at[1]
    )
    rest_copies = peer_copies(
        "loop", loop, lambda peer: rest_ref, rest_out_ref, sems.at[2], sems.at[3]
    )
    parts[dp_me] = part_ref[...]
    rest_out_ref[loop_me] = rest_ref[...]
    wait_all(dp_copies)
    total = parts[0]
    for at in range(1, dp):
        total = total + parts[at]
    own[...] = mean_ref[...] + total
    pooled_copies = peer_copies(
        "loop", loop, lambda peer: own, pooled_ref, sems.at[4], sems.at[5]
    )
    pooled_ref[loop_me] = own[...]
    wait_all(rest_copies)
    wait_all(pooled_copies)


def head_exchange(part, mean, rest):
    dp = lax.axis_size("dp")
    loop = lax.axis_size("loop")
    whole = pl.BlockSpec(memory_space=pltpu.VMEM)
    return pl.pallas_call(
        functools.partial(head_kernel, dp, loop),
        out_shape=(
            jax.ShapeDtypeStruct((loop,) + part.shape, jnp.float32),
            jax.ShapeDtypeStruct((loop,) + rest.shape, jnp.float32),
        ),
        in_specs=[whole] * 3,
        out_specs=(whole, whole),
        scratch_shapes=[
            pltpu.VMEM((dp,) + part.shape, jnp.float32),
            pltpu.VMEM(part.shape, jnp.float32),
            pltpu.SemaphoreType.DMA((6, max(dp, loop))),
        ],
        compiler_params=pltpu.CompilerParams(
            collective_id=0, has_side_effects=True, vmem_limit_bytes=16 * 1024 * 1024
        ),
    )(part, mean, rest)


def total_kernel(dp, loop, part_ref, out_ref, dp_slots, loop_slots, block, chunk, sems):
    meet_peers((("dp", dp), ("loop", loop)))
    loop_me = lax.axis_index("loop")
    dp_me = lax.axis_index("dp")
    copies = peer_copies(
        "dp", dp, lambda peer: part_ref.at[peer], dp_slots, sems.at[0], sems.at[1]
    )
    dp_slots[dp_me] = part_ref[dp_me]
    wait_all(copies)
    total = dp_slots[0]
    for at in range(1, dp):
        total = total + dp_slots[at]
    block[...] = total
    copies = peer_copies(
        "loop", loop, lambda peer: block.at[peer], loop_slots, sems.at[2], sems.at[3]
    )
    loop_slots[loop_me] = block[loop_me]
    wait_all(copies)
    total = loop_slots[0]
    for at in range(1, loop):
        total = total + loop_slots[at]
    chunk[...] = total
    mine = out_ref.at[dp_me]
    copies = peer_copies("loop", loop, lambda peer: chunk, mine, sems.at[4], sems.at[5])
    out_ref[dp_me, loop_me] = chunk[...]
    wait_all(copies)
    copies = peer_copies("dp", dp, lambda peer: mine, out_ref, sems.at[6], sems.at[7])
    wait_all(copies)


def total_sum(part):
    dp = lax.axis_size("dp")
    loop = lax.axis_size("loop")
    rows = part.shape[0] * part.shape[1] // (dp * loop)
    whole = pl.BlockSpec(memory_space=pltpu.VMEM)
    summed = pl.pallas_call(
        functools.partial(total_kernel, dp, loop),
        out_shape=jax.ShapeDtypeStruct((dp, loop, rows, LANES), jnp.float32),
        in_specs=[whole],
        out_specs=whole,
        scratch_shapes=[
            pltpu.VMEM((dp, loop, rows, LANES), jnp.float32),
            pltpu.VMEM((loop, rows, LANES), jnp.float32),
            pltpu.VMEM((loop, rows, LANES), jnp.float32),
            pltpu.VMEM((rows, LANES), jnp.float32),
            pltpu.SemaphoreType.DMA((8, max(dp, loop))),
        ],
        compiler_params=pltpu.CompilerParams(
            collective_id=1, has_side_effects=True, vmem_limit_bytes=32 * 1024 * 1024
        ),
    )(part.reshape(dp, loop, rows, LANES))
    return summed.reshape(part.shape)


def dense_rows(values):
    return values.reshape(-1, LANES)


def general_device(
    features,
    image_ids,
    text_embeds,
    text_ids,
    depth_kernel,
    depth_bias,
    norm_gain,
    w_up,
    w_down,
    projection,
    logit_scale,
    logit_bias,
):
    image_rows = features.shape[0]
    channels = features.shape[3]
    hidden_share = w_up.shape[1]
    cell_count = GRID * GRID
    loop_count = lax.axis_size("loop")
    position = lax.axis_index("loop")
    image_count = image_rows * loop_count
    text_rows = text_embeds.shape[0]
    first_image = position * image_rows
    gather = functools.partial(lax.all_gather, axis_name="loop", axis=0, tiled=True)

    text_unit, text_inverse = unit_rows(text_embeds.astype(jnp.float32))
    cell_mean = jnp.mean(features.astype(jnp.float32), axis=(1, 2))

    padded = jnp.pad(
        features.astype(jnp.float32), ((0, 0), (0, 0), (0, ROWS - GRID), (0, 0))
    )
    gain_row = norm_gain[None, :]
    unit, inverse = conv_norm(
        padded,
        depth_kernel.astype(jnp.float32).reshape(cell_count, channels),
        depth_bias[None, :],
    )
    padded_rows = image_rows * GRID * ROWS
    unit_rows_own = unit.reshape(padded_rows, channels)
    unit_share = lax.all_to_all(unit_rows_own, "loop", split_axis=1, concat_axis=0, tiled=True)
    normed_rows = (unit_rows_own * gain_row).astype(jnp.bfloat16)
    pre_act = jnp.dot(normed_rows, w_up, preferred_element_type=jnp.float32)
    hidden_sum = jnp.sum(
        gelu_value(pre_act).reshape(image_rows, GRID * ROWS, hidden_share), axis=1
    )
    slope = gelu_slope(pre_act)
    hidden_own = (hidden_sum / cell_count).astype(jnp.bfloat16)
    mlp_part = lax.dot_general(
        hidden_own, w_down, (((1,), (1,)), ((), ())), preferred_element_type=jnp.float32
    )
    id_row = jnp.pad(image_ids.astype(jnp.float32), (0, LANES - image_rows))[None, :]
    rest = jnp.concatenate([dense_rows(hidden_sum), dense_rows(text_unit), id_row], axis=0)
    hidden_rows = image_rows * hidden_share // LANES
    text_end = hidden_rows + text_unit.size // LANES
    rest = jnp.pad(rest, ((0, -rest.shape[0] % ROWS), (0, 0)))
    pooled_all, rest_all = head_exchange(dense_rows(mlp_part), dense_rows(cell_mean), rest)
    slope_sent, unit_share, pooled_all = lax.optimization_barrier((slope, unit_share, pooled_all))
    slope_all = gather(slope_sent)
    pooled = pooled_all.reshape(image_count, channels).astype(jnp.bfloat16)
    hidden_all = rest_all[:, :hidden_rows].reshape(image_count, hidden_share)
    hidden_all = (hidden_all / cell_count).astype(jnp.bfloat16)
    text_all = rest_all[:, hidden_rows:text_end].reshape(-1, text_embeds.shape[1])
    ids_all = rest_all[:, text_end, :image_rows].reshape(image_count).astype(jnp.int32)
    embedding = jnp.dot(pooled, projection, preferred_element_type=jnp.float32)
    image_unit, image_inverse = unit_rows(embedding)
    logits = (
        logit_scale[0] * jnp.dot(image_unit, text_all.T, precision=full_precision)
        + logit_bias[0]
    )
    labels = jnp.where(ids_all[:, None] == text_ids[None, :], 1.0, -1.0).astype(jnp.float32)
    loss_all = -jnp.sum(jax.nn.log_sigmoid(labels * logits), axis=1)
    row_loss = lax.dynamic_slice_in_dim(loss_all, first_image, image_rows)
    coeffs = -logit_scale[0] * labels * jax.nn.sigmoid(-labels * logits)
    grad_image = jnp.dot(coeffs, text_all, precision=full_precision)
    own_coeffs = lax.dynamic_slice_in_dim(coeffs, position * text_rows, text_rows, 1)
    grad_text = jnp.dot(own_coeffs.T, image_unit, precision=full_precision)
    grad_texts = text_inverse * (
        grad_text - text_unit * jnp.sum(text_unit * grad_text, axis=1, keepdims=True)
    )
    grad_embed = (
        image_inverse
        * (grad_image - image_unit * jnp.sum(image_unit * grad_image, axis=1, keepdims=True))
    ).astype(jnp.bfloat16)
    grad_pooled = lax.dot_general(
        grad_embed, projection, (((1,), (1,)), ((), ())), preferred_element_type=jnp.float32
    ).astype(jnp.bfloat16)
    spread = jnp.dot(grad_pooled, w_down, preferred_element_type=jnp.float32) / cell_count
    own_spread = lax.dynamic_slice_in_dim(spread, first_image, image_rows)
    grad_pre = (
        (slope.reshape(image_rows, GRID * ROWS, hidden_share) * own_spread[:, None, :])
        .reshape(padded_rows, hidden_share)
        .astype(jnp.bfloat16)
    )
    grad_normed = lax.dot_general(
        grad_pre, w_up, (((1,), (1,)), ((), ())), preferred_element_type=jnp.float32
    ).reshape(padded.shape)
    part = conv_grads(padded, unit, inverse, gain_row, grad_normed)
    total = total_sum(part).transpose(1, 0, 2).reshape(TAP_ROWS, channels)
    grad_kernel = total[:cell_count].reshape(GRID, GRID, channels)
    grad_bias = total[cell_count]
    grad_gain = total[cell_count + 1]

    up_share = channels // loop_count
    grad_pooled_share = lax.dynamic_slice_in_dim(grad_pooled, position * up_share, up_share, 1)
    grad_down = lax.dot_general(
        grad_pooled_share, hidden_all, (((0,), (0,)), ((), ())), preferred_element_type=jnp.float32
    )
    proj_share = up_share // lax.axis_size("dp")
    proj_at = (lax.axis_index("dp") * loop_count + position) * proj_share
    pooled_share = lax.dynamic_slice_in_dim(pooled, proj_at, proj_share, 1)
    grad_proj = lax.dot_general(
        pooled_share, grad_embed, (((0,), (0,)), ((), ())), preferred_element_type=jnp.float32
    )
    grad_pre_all = (
        (slope_all.reshape(image_count, GRID * ROWS, hidden_share) * spread[:, None, :])
        .reshape(loop_count * padded_rows, hidden_share)
        .astype(jnp.bfloat16)
    )
    gain_share = lax.dynamic_slice_in_dim(norm_gain, position * up_share, up_share)
    normed_share = (unit_share * gain_share).astype(jnp.bfloat16)
    grad_up = lax.dot_general(
        normed_share,
        grad_pre_all,
        (((0,), (0,)), ((), ())),
        preferred_element_type=jnp.float32,
    )
    return (row_loss, grad_texts, grad_kernel, grad_bias, grad_gain, grad_up, grad_down, grad_proj)


SPLIT = 96
SIDE = 4
CORES = 2
PACKET = 2304
PART_ROWS = 56
MESH = pl.DeviceIdType.MESH
nn = (((1,), (0,)), ((), ()))
nt = (((1,), (1,)), ((), ()))
tn = (((0,), (0,)), ((), ()))


def product(left, right, dims, precision=None):
    return lax.dot_general(
        left, right, dims, preferred_element_type=jnp.float32, precision=precision
    )


def flipped(index, by):
    if by == 1:
        return index + 1 - 2 * lax.rem(index, 2)
    if by == 2:
        return lax.rem(index + 2, SIDE)
    return SIDE - 1 - index


def columns(start, size):
    return pl.ds(pl.multiple_of(start, LANES), size)


def rounded(values):
    return values.astype(jnp.bfloat16).astype(jnp.float32)


def image_of(first, shape, values):
    cells = GRID * GRID
    row = first + lax.broadcasted_iota(jnp.int32, shape, 0)
    out = jnp.broadcast_to(values[-1], shape)
    for n in reversed(range(len(values) - 1)):
        out = jnp.where(row < (n + 1) * cells, values[n], out)
    return jnp.where(row < len(values) * cells, out, 0.0)


def fused_kernel(
    xb,
    kb,
    wu_hbm,
    wd_hbm,
    pj_hbm,
    bias_ref,
    gain_ref,
    text_ref,
    iid_ref,
    tid_ref,
    scale_ref,
    shift_ref,
    o_loss,
    *refs,
):
    placed = refs[:7]
    (
        o_text,
        o_kernel,
        o_bias,
        o_gain,
        o_up,
        o_down,
        o_proj,
        wu,
        wd,
        pj,
        x,
        kf,
        unit,
        inv,
        nf,
        nb,
        stats,
        stats_out,
        stats_in,
        pre,
        sl,
        gn,
        full,
        thin,
        far,
        nrow,
        gpre,
        fullb,
        packed,
        packets,
        texts_out,
        texts_in,
        texts,
        part_out,
        part_in,
        means,
        small,
        heads,
        gathered,
        work,
        taps_out,
        taps_in,
        taps_sum,
        taps_z,
        taps_all,
        up_out,
        up_in,
        local_sem,
        send_sem,
        recv_sem,
    ) = refs[7:]
    count, _, _, channels = xb.shape
    hidden = wu.shape[1]
    width = pj.shape[1]
    split = full.shape[1]
    total_rows = nf.shape[0]
    sent_rows = count * GRID * GRID
    sent_rows += -sent_rows % ROWS
    rest_rows = sent_rows - split
    tiles = channels // LANES
    reach = (GRID - 1) // 2
    taps = GRID * GRID
    chip = channels // SIDE
    half = hidden // 2
    dp = lax.axis_index("dp")
    loop = lax.axis_index("loop")
    z = loop // CORES
    core = lax.rem(loop, CORES)
    rank = dp * CORES + core
    planes = SIDE * CORES
    next_sem = [0]

    def take(number):
        first = next_sem[0]
        next_sem[0] += number
        return first

    def remote(src, dst, device, sem, sent=None):
        return pltpu.make_async_remote_copy(
            src_ref=src,
            dst_ref=dst,
            send_sem=send_sem.at[sem if sent is None else sent],
            recv_sem=recv_sem.at[sem],
            device_id=device,
            device_id_type=MESH,
        )

    def at_z(index):
        return {"dp": dp, "loop": index * CORES + core}

    def at_dp(index):
        return {"dp": index, "loop": loop}

    def at_rank(index):
        return {"dp": index // CORES, "loop": z * CORES + lax.rem(index, CORES)}

    partner = {"dp": dp, "loop": z * CORES + 1 - core}

    stores = []

    def store(at, held):
        copy = pltpu.make_async_copy(held, placed[at], local_sem.at[3 + at])
        copy.start()
        stores.append(copy)

    barrier = pltpu.get_barrier_semaphore()
    met = 0
    for by in range(1, planes):
        pl.semaphore_signal(
            barrier, inc=1, device_id={"dp": dp, "loop": lax.rem(loop + by, planes)}, device_id_type=MESH
        )
        met += 1
    for by in range(1, SIDE):
        for other in range(CORES):
            pl.semaphore_signal(
                barrier,
                inc=1,
                device_id={"dp": flipped(dp, by), "loop": z * CORES + other},
                device_id_type=MESH,
            )
            met += 1
    loads = []
    for at, (far_ref, near_ref) in enumerate(((wu_hbm, wu), (wd_hbm, wd), (pj_hbm, pj))):
        copy = pltpu.make_async_copy(far_ref, near_ref, local_sem.at[at])
        copy.start()
        loads.append(copy)

    text = text_ref[...].astype(jnp.float32)
    text_unit, text_inverse = unit_rows(text)
    third = width // 3
    texts_out[...] = jnp.zeros(texts_out.shape, jnp.float32)
    for k in range(3):
        texts_out[2 * k : 2 * k + 2, :] = text_unit[:, k * third : (k + 1) * third]

    cell = lax.broadcasted_iota(jnp.int32, (ROWS, LANES), 0)
    zero = jnp.zeros((ROWS, LANES), jnp.float32)
    cells = [(n, p) for n in range(count) for p in range(GRID)]

    edge = total_rows - 2 * ROWS
    nf[edge:total_rows, :] = jnp.zeros((2 * ROWS, channels), jnp.float32)

    def conv_tile(i, sums):
        lanes = lane_tile(lax.rem(dp * (tiles // SIDE) + i, tiles))
        for n, p in cells:
            x[n, p, 0:GRID, lanes] = xb[n, p, :, lanes].astype(jnp.float32)
            x[n, p, GRID:ROWS, lanes] = jnp.zeros((ROWS - GRID, LANES), jnp.float32)
        for a in range(GRID):
            kf[a * GRID : (a + 1) * GRID, lanes] = kb[a, :, lanes].astype(jnp.float32)
        bias = jnp.broadcast_to(bias_ref[:, lanes], (ROWS, LANES))
        out = {at: bias for at in cells}
        for col_off in range(GRID):
            moved = shifted_rows(x, lanes, col_off - reach, cell)
            for row_off in range(GRID):
                tap = row_off * GRID + col_off
                weight = jnp.broadcast_to(kf[tap : tap + 1, lanes], (ROWS, LANES))
                for p in range(GRID):
                    row = p + row_off - reach
                    if 0 <= row < GRID:
                        for n in range(count):
                            out[(n, p)] = out[(n, p)] + moved[row][n] * weight
        for n, p in cells:
            unit[n, p, :, lanes] = out[(n, p)]
            first = n * taps + p * GRID
            nf[first : first + ROWS, lanes] = out[(n, p)]
        return tuple(total + out[at] for total, at in zip(sums, cells))

    zeros = tuple(zero for _ in cells)
    early = tiles // SIDE
    sums = lax.fori_loop(0, early, conv_tile, zeros)

    pl.semaphore_wait(barrier, met)
    text_sem = take(planes)
    text_copies = []
    for by in range(1, planes):
        peer = {"dp": dp, "loop": lax.rem(loop + by, planes)}
        copy = remote(texts_out, texts_in.at[loop], peer, text_sem + by)
        copy.start()
        text_copies.append(copy)

    quarter = channels // SIDE
    slim = chip // SIDE
    own_quarter = columns(dp * quarter, quarter)
    own_slim = columns(dp * slim, slim)
    full_sem = take(SIDE)
    thin_sem = take(SIDE)
    far_sem = take(SIDE)
    relay_sem = take(2)
    inner = z * (SIDE - 1 - z) > 0
    full_copies = {}
    thin_copies = {}
    far_copies = {}
    for by in range(1, SIDE):
        peer = flipped(z, by)
        full_copies[by] = remote(
            nf.at[pl.ds(0, split), own_quarter],
            full.at[z, :, own_quarter],
            at_z(peer),
            full_sem + by,
        )
        thin_copies[by] = remote(
            nf.at[pl.ds(split, rest_rows), columns(peer * chip + dp * slim, slim)],
            thin.at[z, pl.ds(0, rest_rows), own_slim],
            at_z(peer),
            thin_sem + by,
        )
        far_copies[by] = remote(
            sl.at[pl.ds(split, rest_rows), :],
            far.at[z, pl.ds(0, rest_rows), :],
            at_z(peer),
            far_sem + by,
        )
    two_away = flipped(z, 2)
    full_relay = remote(
        full.at[two_away, :, own_quarter],
        full.at[two_away, :, own_quarter],
        at_z(flipped(z, 1)),
        full_sem + 3,
        relay_sem,
    )
    far_relay = remote(
        far.at[two_away, pl.ds(0, rest_rows), :],
        far.at[two_away, pl.ds(0, rest_rows), :],
        at_z(flipped(z, 1)),
        far_sem + 3,
        relay_sem + 1,
    )

    def when_inner(*actions):
        @pl.when(inner)
        def _():
            for action in actions:
                action()

    full_copies[1].start()
    full_copies[2].start()
    when_inner(full_copies[3].start)

    sums = lax.fori_loop(early, tiles, conv_tile, sums)
    for by in range(1, SIDE):
        thin_copies[by].start()
    centers = [jnp.sum(total, axis=1, keepdims=True) / channels for total in sums]
    centers = [jnp.broadcast_to(mean, (ROWS, LANES)) for mean in centers]

    def square_tile(index, sums):
        lanes = lane_tile(index)
        result = []
        for total, mean, (n, p) in zip(sums, centers, cells):
            centered = unit[n, p, :, lanes] - mean
            result.append(total + centered * centered)
        return tuple(result)

    squares = lax.fori_loop(0, tiles, square_tile, zeros)

    inverses = []
    for total, (n, p) in zip(squares, cells):
        variance = jnp.sum(total, axis=1, keepdims=True) / channels
        inverse = jnp.broadcast_to(lax.rsqrt(variance + 1e-06), (ROWS, LANES))
        inverse = jnp.where(cell < GRID, inverse, 0.0)
        inv[n, p, :, :] = inverse
        inverses.append(inverse)
    lane_at = lax.broadcasted_iota(jnp.int32, (ROWS, LANES), 1)
    side_by_side = lane_at < LANES // 2
    stats[edge:total_rows, :] = jnp.zeros((2 * ROWS, LANES), jnp.float32)
    for inverse, mean, (n, p) in zip(inverses, centers, cells):
        first = n * taps + p * GRID
        stats[first : first + ROWS, :] = jnp.where(side_by_side, mean, inverse)
    total = zero
    for k in range(total_rows // ROWS):
        values = stats[k * ROWS : (k + 1) * ROWS, :]
        total = total + jnp.where(lax.rem(lane_at, LANES // 2) == k, values, 0.0)
    stats_out[...] = total
    stats_sem = take(SIDE)
    stats_copies = {}
    for by in range(1, SIDE):
        copy = remote(stats_out, stats_in.at[z], at_z(flipped(z, by)), stats_sem + by)
        copy.start()
        stats_copies[by] = copy

    gn[edge:total_rows, :] = jnp.zeros((2 * ROWS, channels), jnp.float32)

    def norm_tile(index, carry):
        lanes = lane_tile(index)
        gain = jnp.broadcast_to(gain_ref[:, lanes], (ROWS, LANES))
        for inverse, mean, (n, p) in zip(inverses, centers, cells):
            value = (unit[n, p, :, lanes] - mean) * inverse
            unit[n, p, :, lanes] = value
            first = n * taps + p * GRID
            gn[first : first + ROWS, lanes] = value * gain
        return carry

    lax.fori_loop(0, tiles, norm_tile, 0)

    def narrow(i, carry):
        rows = pl.ds(pl.multiple_of(i * 2 * ROWS, 2 * ROWS), 2 * ROWS)
        nb[rows, :] = gn[rows, :].astype(jnp.bfloat16)
        return carry

    lax.fori_loop(0, total_rows // (2 * ROWS), narrow, 0)

    loads[0].wait()
    strip = 2 * LANES

    def expand(rows_ref, rows):
        def step(j, carry):
            lanes = pl.ds(pl.multiple_of(j * strip, strip), strip)
            pre[0:rows, lanes] = product(rows_ref[0:rows, :], wu[:, lanes], nn)
            return carry

        lax.fori_loop(0, hidden // strip, step, 0)

    expand(nb, total_rows)

    def activate(i, carry):
        rows = pl.ds(pl.multiple_of((i // 2) * 2 * ROWS, 2 * ROWS), 2 * ROWS)
        lanes = pl.ds(pl.multiple_of(lax.rem(i, 2) * half, LANES), half)
        values = pre[rows, lanes]
        cumulative = 0.5 * (1.0 + lax.erf(values * half_root))
        sl[rows, lanes] = cumulative + values * jnp.exp(-0.5 * values * values) * density_factor
        pre[rows, lanes] = values * cumulative
        return carry

    lax.fori_loop(0, total_rows // ROWS, activate, 0)

    far_copies[1].start()

    row_wide = lax.broadcasted_iota(jnp.int32, (ROWS, hidden), 0)
    heads[...] = jnp.zeros(heads.shape, jnp.float32)
    for n in range(count):
        begin, end = n * taps, (n + 1) * taps
        total = jnp.zeros((ROWS, hidden), jnp.float32)
        for tile in range(begin // ROWS, -(-end // ROWS)):
            values = pre[tile * ROWS : (tile + 1) * ROWS, :]
            if tile * ROWS < begin:
                values = jnp.where(row_wide >= begin - tile * ROWS, values, 0.0)
            if (tile + 1) * ROWS > end:
                values = jnp.where(row_wide < end - tile * ROWS, values, 0.0)
            total = total + values
        mean = jnp.sum(total, axis=0, keepdims=True) / taps
        heads[n : n + 1, 0:hidden] = rounded(mean)

    loads[1].wait()
    mlp = product(heads[:, 0:hidden].astype(jnp.bfloat16), wd[...], nt)
    part_out[...] = jnp.zeros(part_out.shape, jnp.float32)
    part_out[0:count, :] = mlp[0:count, 0:hidden]
    part_out[count : 2 * count, :] = mlp[0:count, hidden : 2 * hidden]
    part_sem = take(SIDE)
    part_copies = []
    for by in range(1, SIDE):
        copy = remote(part_out, part_in.at[dp], at_dp(flipped(dp, by)), part_sem + by)
        copy.start()
        part_copies.append(copy)
    first_sem = take(3 * SIDE)
    second_sem = take(3 * SIDE)
    slim_sem = take(SIDE * SIDE)
    half_quarter = quarter // 2
    first_hop = {}
    second_hop = {}
    slim_hop = {}

    def hop_one(by):
        peer = flipped(z, by)
        if by == 3:
            full_copies[3].wait_recv()
            when_inner(full_copies[3].wait_send, full_relay.wait_send)
        else:
            full_copies[by].wait()
        if by == 2:
            when_inner(full_relay.start)
        thin_copies[by].wait()
        block = full.at[peer, :, own_quarter]
        first_hop[by] = []
        for to in (1, 2):
            copy = remote(block, block, at_dp(flipped(dp, to)), first_sem + 3 * by + to)
            copy.start()
            first_hop[by].append(copy)
        piece = thin.at[peer, pl.ds(0, rest_rows), own_slim]
        slim_hop[by] = []
        for to in range(1, SIDE):
            copy = remote(piece, piece, at_dp(flipped(dp, to)), slim_sem + SIDE * by + to)
            copy.start()
            slim_hop[by].append(copy)

    def hop_two(by):
        peer = flipped(z, by)
        second_hop[by] = []
        for to in (1, 2):
            first_hop[by][to - 1].wait_recv()
            source = flipped(dp, to)
            block = full.at[peer, :, columns(source * quarter + (to - 1) * half_quarter, half_quarter)]
            copy = remote(block, block, at_dp(flipped(dp, 3 - to)), second_sem + 3 * by + to)
            copy.start()
            second_hop[by].append(copy)

    def arrived(by):
        for copy in second_hop[by]:
            copy.wait()
        for copy in first_hop[by]:
            copy.wait_send()
        for copy in slim_hop[by]:
            copy.wait()
        if by == 3:
            far_copies[3].wait_recv()
            when_inner(far_copies[3].wait_send, far_relay.wait_send)
        else:
            far_copies[by].wait()
            if by == 2:
                when_inner(far_relay.start)

    hop_one(1)
    part_in[dp] = part_out[...]
    means[...] = jnp.zeros(means.shape, jnp.float32)
    for n in range(count):
        total = x[n, 0]
        for p in range(1, GRID):
            total = total + x[n, p]
        mean = jnp.sum(total, axis=0, keepdims=True) / taps
        means[n : n + 1, :] = mean[:, 0:hidden]
        means[count + n : count + n + 1, :] = mean[:, hidden : 2 * hidden]
    for copy in text_copies:
        copy.wait()
    texts_in[loop] = texts_out[...]
    for l in range(planes):
        for k in range(3):
            texts[2 * l : 2 * l + 2, k * third : (k + 1) * third] = texts_in[l, 2 * k : 2 * k + 2, :]
    loads[2].wait()
    small[...] = jnp.zeros(small.shape, jnp.float32)
    for copy in part_copies:
        copy.wait()
    total = part_in[0]
    for at in range(1, SIDE):
        total = total + part_in[at]
    pooled = rounded(means[...] + total)
    small[0:count, 0:hidden] = pooled[0:count, :]
    small[0:count, hidden : 2 * hidden] = pooled[count : 2 * count, :]

    embedding = product(small[...].astype(jnp.bfloat16), pj[...], nn)[0:ROWS, :]
    image_unit, image_inverse = unit_rows(embedding)
    all_texts = texts[...]
    text_count = all_texts.shape[0]
    scale = scale_ref[...]
    logits = scale * product(image_unit, all_texts, nt, full_precision) + shift_ref[...]
    ids = jnp.broadcast_to(iid_ref[...].astype(jnp.float32), (ROWS, count))
    spot_row = lax.broadcasted_iota(jnp.int32, (ROWS, count), 0)
    spot_col = lax.broadcasted_iota(jnp.int32, (ROWS, count), 1)
    own_ids = jnp.sum(jnp.where(spot_row == spot_col, ids, 0.0), axis=1, keepdims=True)
    same = jnp.broadcast_to(own_ids, (ROWS, text_count)) == jnp.broadcast_to(
        tid_ref[...].astype(jnp.float32), (ROWS, text_count)
    )
    labels = jnp.where(same, 1.0, -1.0)
    signed = labels * logits
    losses = jnp.log1p(jnp.exp(-jnp.abs(signed))) - jnp.minimum(signed, 0.0)
    loss = jnp.broadcast_to(jnp.sum(losses, axis=1, keepdims=True), (ROWS, LANES))
    o_loss[...] = jnp.sum(jnp.where(cell == lane_at, loss, 0.0), axis=0, keepdims=True)
    coeffs = -scale * labels * lax.logistic(-signed)
    grad_image = product(coeffs, all_texts, nn, full_precision)
    own_row = lax.broadcasted_iota(jnp.int32, (ROWS, width), 0)
    grad_embed = image_inverse * (
        grad_image - image_unit * jnp.sum(image_unit * grad_image, axis=1, keepdims=True)
    )
    grad_embed = jnp.where(own_row < count, rounded(grad_embed), 0.0)
    grad_text = product(coeffs, image_unit, tn, full_precision)
    heads[0:ROWS, hidden : hidden + width] = grad_embed
    grad_pooled = product(heads[:, hidden : hidden + width].astype(jnp.bfloat16), pj[...], nt)
    grad_pooled = grad_pooled.astype(jnp.bfloat16)
    spread = product(grad_pooled, wd[...], nn) / taps
    grad_pooled = grad_pooled.astype(jnp.float32)

    for at in range(SIDE):
        packed[at, 0:count, 0:chip] = grad_pooled[0:count, at * chip : (at + 1) * chip]
        packed[at, 0:count, chip : chip + LANES] = small[
            0:count, columns(dp * quarter + at * LANES, LANES)
        ]
        packed[at, 0:count, chip + LANES : chip + LANES + width] = grad_embed[0:count, :]
        packed[at, count : 2 * count, 0:hidden] = heads[0:count, 0:hidden]
        packed[at, count : 2 * count, hidden : 2 * hidden] = spread[0:count, :]
        packed[at, 6:8, 0:width] = grad_text[4 * at : 4 * at + 2, :]
        packed[at, 6:8, width : 2 * width] = grad_text[4 * at + 2 : 4 * at + 4, :]
    packet_sem = take(SIDE)
    packet_copies = {}
    for by in range(1, SIDE):
        peer = flipped(z, by)
        copy = remote(packed.at[peer], packets.at[core, z], at_z(peer), packet_sem + by)
        copy.start()
        packet_copies[by] = copy
    packets[core, z] = packed[z]

    far_copies[2].start()
    when_inner(far_copies[3].start)

    spreads = [spread[n : n + 1, :] for n in range(count)]

    def own_slopes(i, carry):
        first = pl.multiple_of(i * 2 * ROWS, 2 * ROWS)
        rows = pl.ds(first, 2 * ROWS)
        for lanes in (slice(0, half), slice(half, hidden)):
            scaled = image_of(first, (2 * ROWS, half), [s[:, lanes] for s in spreads])
            gpre[rows, lanes] = (sl[rows, lanes] * scaled).astype(jnp.bfloat16)
        return carry

    lax.fori_loop(0, total_rows // (2 * ROWS), own_slopes, 0)
    hop_one(2)
    hop_two(1)

    def contract(j, carry):
        lanes = pl.ds(pl.multiple_of(j * strip, strip), strip)
        gn[:, lanes] = product(gpre[0:total_rows, :], wu[lanes, :], nt)
        return carry

    lax.fori_loop(0, channels // strip, contract, 0)
    own_chip = columns(z * chip, chip)
    nrow[0:total_rows, :] = nb[:, own_chip]

    def first_tile(index, carry):
        plain, crossed = carry
        lanes = lane_tile(index)
        gain = jnp.broadcast_to(gain_ref[:, lanes], (ROWS, LANES))
        gain_sum = zero
        taps_out[index, 48:PART_ROWS, :] = jnp.zeros((PART_ROWS - 48, LANES), jnp.float32)
        plain_out = []
        crossed_out = []
        for at, (n, p) in enumerate(cells):
            first = n * taps + p * GRID
            value = unit[n, p, :, lanes]
            grad = gn[first : first + ROWS, lanes]
            gain_sum = gain_sum + grad * value
            scaled = grad * gain
            plain_out.append(plain[at] + scaled)
            crossed_out.append(crossed[at] + scaled * value)
        taps_out[index, taps + 1 : taps + 2, :] = jnp.sum(gain_sum, axis=0, keepdims=True)
        return (tuple(plain_out), tuple(crossed_out))

    plain, crossed = lax.fori_loop(0, tiles, first_tile, (zeros, zeros))
    for at, (n, p) in enumerate(cells):
        first = jnp.sum(plain[at], axis=1, keepdims=True) / channels
        second = jnp.sum(crossed[at], axis=1, keepdims=True) / channels
        work[0, n, p, :, :] = jnp.broadcast_to(first, (ROWS, LANES))
        work[1, n, p, :, :] = jnp.broadcast_to(second, (ROWS, LANES))

    own_tiles = tiles // planes
    sent_tiles = tiles - own_tiles
    taps_sem = take(sent_tiles)

    def taps_copy(i):
        owner = lax.rem(rank + 1 + i // own_tiles, planes)
        return remote(
            taps_out.at[owner * own_tiles + lax.rem(i, own_tiles)],
            taps_in.at[rank, lax.rem(i, own_tiles)],
            at_rank(owner),
            taps_sem + i,
        )

    def tap_tile(i, carry):
        index = lax.rem(rank * own_tiles + own_tiles + i, tiles)
        lanes = lane_tile(index)
        gain = jnp.broadcast_to(gain_ref[:, lanes], (ROWS, LANES))
        grad_conv = {}
        bias_sum = zero
        for n, p in cells:
            first = n * taps + p * GRID
            value = inv[n, p, :, :] * (
                gn[first : first + ROWS, lanes] * gain
                - work[0, n, p, :, :]
                - unit[n, p, :, lanes] * work[1, n, p, :, :]
            )
            grad_conv[(n, p)] = value
            bias_sum = bias_sum + value
        taps_out[index, taps : taps + 1, :] = jnp.sum(bias_sum, axis=0, keepdims=True)
        for col_off in range(GRID):
            moved = shifted_rows(x, lanes, col_off - reach, cell)
            for row_off in range(GRID):
                tap = row_off * GRID + col_off
                total = zero
                for p in range(GRID):
                    row = p + row_off - reach
                    if 0 <= row < GRID:
                        for n in range(count):
                            total = total + moved[row][n] * grad_conv[(n, p)]
                taps_out[index, tap : tap + 1, :] = jnp.sum(total, axis=0, keepdims=True)

        @pl.when(i < sent_tiles)
        def _():
            taps_copy(i).start()

        return carry

    lax.fori_loop(0, tiles // 2, tap_tile, 0)
    hop_one(3)
    hop_two(2)
    lax.fori_loop(tiles // 2, tiles, tap_tile, 0)

    for by in range(1, SIDE):
        packet_copies[by].wait()
    cross_sem = take(1)
    cross = remote(packets.at[core], packets.at[core], partner, cross_sem)
    cross.start()

    def other_rows(by):
        peer = flipped(z, by)
        base = by * total_rows
        arrived(by)
        stats_copies[by].wait()
        scales = stats_in[peer]

        def spot(k):
            return jnp.sum(jnp.where(lane_at == k, scales, 0.0), axis=1, keepdims=True)

        def normed(values, k, gain):
            parts = []
            for at in range(2):
                part = values[at * ROWS : (at + 1) * ROWS, :] - spot(k + at)
                parts.append(part * spot(k + at + LANES // 2) * gain)
            return jnp.concatenate(parts, axis=0)

        def cast(i, carry):
            first = pl.multiple_of(i * 2 * ROWS, 2 * ROWS)
            rows = pl.ds(first, 2 * ROWS)
            fullb[rows, :] = normed(full[peer, rows, :], 2 * i, gain_ref[...]).astype(jnp.bfloat16)
            nrow[pl.ds(base + first, 2 * ROWS), :] = fullb[rows, own_chip]
            return carry

        lax.fori_loop(0, split // (2 * ROWS), cast, 0)
        expand(fullb, split)
        spreads = [
            packets[core, peer, count + n : count + n + 1, hidden : 2 * hidden] for n in range(count)
        ]

        def slopes(i, carry):
            first = pl.multiple_of(i * 2 * ROWS, 2 * ROWS)
            for lanes in (slice(0, half), slice(half, hidden)):
                scaled = image_of(first, (2 * ROWS, half), [s[:, lanes] for s in spreads])
                values = gelu_slope(pre[pl.ds(first, 2 * ROWS), lanes]) * scaled
                gpre[pl.ds(base + first, 2 * ROWS), lanes] = values.astype(jnp.bfloat16)
            return carry

        lax.fori_loop(0, split // (2 * ROWS), slopes, 0)
        for i in range((total_rows - split) // (2 * ROWS)):
            first = i * 2 * ROWS
            at = split + first
            rows = slice(first, first + 2 * ROWS)
            keep = lax.broadcasted_iota(jnp.int32, (2 * ROWS, chip), 0) + at < count * taps
            values = normed(thin[peer, rows, :], at // ROWS, gain_ref[:, own_chip])
            values = jnp.where(keep, values, 0.0)
            nrow[base + at : base + at + 2 * ROWS, :] = values.astype(jnp.bfloat16)
            for lanes in (slice(0, half), slice(half, hidden)):
                keep = lax.broadcasted_iota(jnp.int32, (2 * ROWS, half), 0) + at < count * taps
                scaled = image_of(at, (2 * ROWS, half), [s[:, lanes] for s in spreads])
                values = jnp.where(keep, far[peer, rows, lanes] * scaled, 0.0)
                gpre[base + at : base + at + 2 * ROWS, lanes] = values.astype(jnp.bfloat16)

    other_rows(1)

    def taps_wait(i, carry):
        taps_copy(i).wait()
        return carry

    lax.fori_loop(0, sent_tiles, taps_wait, 0)
    for k in range(own_tiles):
        total = taps_out[rank * own_tiles + k]
        for by in range(1, planes):
            total = total + taps_in[lax.rem(rank + by, planes), k]
        taps_sum[k] = total
    along_sem = take(SIDE)
    along_copies = []
    for by in range(1, SIDE):
        copy = remote(taps_sum, taps_z.at[z], at_z(flipped(z, by)), along_sem + by)
        copy.start()
        along_copies.append(copy)
    taps_z[z] = taps_sum[...]

    cross.wait()

    def collect(lanes, shift, first_lane):
        for other in range(CORES):
            for at in range(SIDE):
                values = packets[other, at, :, lanes]
                if shift:
                    values = pltpu.roll(values, ROWS - shift, 0)
                keep = lax.broadcasted_iota(jnp.int32, values.shape, 0) < count
                first = (other * SIDE + at) * ROWS
                gathered[first : first + ROWS, first_lane : first_lane + values.shape[1]] = jnp.where(
                    keep, values, 0.0
                )

    share = chip // CORES
    collect(columns(core * share, share), 0, 0)
    collect(slice(chip, chip + LANES + width), 0, share)
    collect(slice(0, hidden), count, share + LANES + width)
    end = share + LANES + width
    o_down[...] = product(
        gathered[:, 0:share].astype(jnp.bfloat16), gathered[:, end : end + hidden].astype(jnp.bfloat16), tn
    )
    proj_two = product(
        gathered[:, share : share + LANES].astype(jnp.bfloat16),
        gathered[:, share + LANES : end].astype(jnp.bfloat16),
        tn,
    )
    proj_rows = LANES // CORES
    gn[0:LANES, 0:width] = proj_two
    o_proj[...] = gn[pl.ds(pl.multiple_of(core * proj_rows, proj_rows), proj_rows), 0:width]
    store(5, o_down)
    store(6, o_proj)
    total = jnp.zeros((ROWS, width), jnp.float32)
    for at in range(SIDE):
        for other in range(CORES):
            total = total + packets[other, at, :, columns(core * width, width)]
    grad_text = total[6:8, :]
    o_text[...] = text_inverse * (
        grad_text - text_unit * jnp.sum(text_unit * grad_text, axis=1, keepdims=True)
    )

    store(0, o_text)

    hop_two(3)
    other_rows(2)

    for copy in along_copies:
        copy.wait()
    for k in range(own_tiles):
        total = taps_z[0, k]
        for at in range(1, SIDE):
            total = total + taps_z[at, k]
        taps_all[rank * own_tiles + k] = total
    spread_sem = take(planes)
    mine = taps_all.at[pl.ds(rank * own_tiles, own_tiles)]
    spread_copies = []
    for by in range(1, planes):
        copy = remote(mine, mine, at_rank(lax.rem(rank + by, planes)), spread_sem + by)
        copy.start()
        spread_copies.append(copy)

    other_rows(3)

    def up_strip(rows_at, j):
        lanes = pl.ds(pl.multiple_of(j * strip, strip), strip)
        return lanes, product(nrow[:, rows_at], gpre[:, lanes], tn)

    theirs = columns((1 - core) * share, share)
    ours = columns(core * share, share)
    steps = hidden // strip
    up_sem = take(steps)

    def up_copy(j):
        return remote(up_out.at[j], up_in.at[j], partner, up_sem + j)

    def up_send(j, carry):
        lanes, values = up_strip(theirs, j)
        up_out[j] = values
        up_copy(j).start()
        return carry

    lax.fori_loop(0, steps, up_send, 0)

    def up_own(j, carry):
        lanes, values = up_strip(ours, j)
        o_up[:, lanes] = values
        return carry

    lax.fori_loop(0, steps, up_own, 0)

    for copy in spread_copies:
        copy.wait()
    for index in range(tiles):
        lanes = slice(index * LANES, (index + 1) * LANES)
        for a in range(GRID):
            o_kernel[a, :, lanes] = taps_all[index, a * GRID : (a + 1) * GRID, :]
        o_bias[:, lanes] = taps_all[index, taps : taps + 1, :]
        o_gain[:, lanes] = taps_all[index, taps + 1 : taps + 2, :]

    store(1, o_kernel)
    store(2, o_bias)
    store(3, o_gain)

    def up_add(j, carry):
        lanes = pl.ds(pl.multiple_of(j * strip, strip), strip)
        up_copy(j).wait()
        o_up[:, lanes] = o_up[:, lanes] + up_in[j]
        return carry

    lax.fori_loop(0, steps, up_add, 0)
    store(4, o_up)
    wait_all(stores)


def deliver_kernel(loss, *refs):
    number = (len(refs) - 2) // 2
    held, out_loss, placed, sems = refs[:number], refs[number], refs[number + 1 : -1], refs[-1]
    copies = []
    for at in range(number):
        copy = pltpu.make_async_copy(held[at], placed[at], sems.at[at])
        copy.start()
        copies.append(copy)
    for n in range(out_loss.shape[0]):
        out_loss[n] = loss[0, n]
    wait_all(copies)


def deliver(count, loss, *held):
    outside = pl.BlockSpec(memory_space=pl.ANY)
    return pl.pallas_call(
        deliver_kernel,
        out_shape=(jax.ShapeDtypeStruct((count,), jnp.float32),)
        + tuple(jax.ShapeDtypeStruct(h.shape, h.dtype) for h in held),
        in_specs=[pl.BlockSpec(memory_space=pltpu.VMEM)] * (1 + len(held)),
        out_specs=(pl.BlockSpec(memory_space=pltpu.SMEM),) + (outside,) * len(held),
        scratch_shapes=[pltpu.SemaphoreType.DMA((len(held),))],
        compiler_params=pltpu.CompilerParams(vmem_limit_bytes=56 * 1024 * 1024),
    )(loss, *held)


def fused_device(
    features,
    image_ids,
    text_embeds,
    text_ids,
    depth_kernel,
    depth_bias,
    norm_gain,
    w_up,
    w_down,
    projection,
    logit_scale,
    logit_bias,
):
    count, _, _, channels = features.shape
    hidden = w_up.shape[1]
    width = projection.shape[1]
    texts = text_ids.shape[0]
    text_rows = text_embeds.shape[0]
    cells = count * GRID * GRID
    rows = cells + -cells % (2 * ROWS)
    chip = channels // SIDE
    share = chip // CORES
    strip = 2 * LANES
    planes = SIDE * CORES
    own_tiles = channels // LANES // planes
    whole = pl.BlockSpec(memory_space=pltpu.VMEM)
    outside = pl.BlockSpec(memory_space=pl.ANY)

    def room(*shape):
        return pltpu.VMEM(shape, jnp.float32)

    def narrow(*shape):
        return pltpu.VMEM(shape, jnp.bfloat16)

    def result(*shape):
        return jax.ShapeDtypeStruct(shape, jnp.float32)

    results = pl.pallas_call(
        fused_kernel,
        out_shape=(
            result(1, LANES),
            result(text_rows, width),
            result(GRID, GRID, channels),
            result(1, channels),
            result(1, channels),
            result(share, hidden),
            result(share, hidden),
            result(LANES // CORES, width),
        ),
        in_specs=[whole] * 2 + [outside] * 3 + [whole] * 7,
        out_specs=(whole,) + (outside,) * 7,
        scratch_shapes=[
            room(text_rows, width),
            room(GRID, GRID, channels),
            room(1, channels),
            room(1, channels),
            room(share, hidden),
            room(share, hidden),
            room(LANES // CORES, width),
            narrow(channels, hidden),
            narrow(channels, hidden),
            narrow(channels, width),
            room(count, GRID, ROWS, channels),
            room(PART_ROWS, channels),
            room(count, GRID, ROWS, channels),
            room(count, GRID, ROWS, LANES),
            room(rows, channels),
            narrow(rows, channels),
            room(rows, LANES),
            room(ROWS, LANES),
            room(SIDE, ROWS, LANES),
            room(rows, hidden),
            room(rows, hidden),
            room(rows, channels),
            room(SIDE, SPLIT, channels),
            room(SIDE, rows - SPLIT, chip),
            room(SIDE, rows - SPLIT, hidden),
            narrow(SIDE * rows, chip),
            narrow(SIDE * rows, hidden),
            narrow(SPLIT, channels),
            room(SIDE, ROWS, PACKET),
            room(CORES, SIDE, ROWS, PACKET),
            room(ROWS, width // 3),
            room(planes, ROWS, width // 3),
            room(texts, width),
            room(ROWS, hidden),
            room(SIDE, ROWS, hidden),
            room(ROWS, hidden),
            room(2 * ROWS, channels),
            room(2 * ROWS, hidden + width),
            room(planes * ROWS, share + LANES + width + hidden),
            room(2, count, GRID, ROWS, LANES),
            room(channels // LANES, PART_ROWS, LANES),
            room(planes, own_tiles, PART_ROWS, LANES),
            room(own_tiles, PART_ROWS, LANES),
            room(SIDE, own_tiles, PART_ROWS, LANES),
            room(channels // LANES, PART_ROWS, LANES),
            room(hidden // strip, share, strip),
            room(hidden // strip, share, strip),
            pltpu.SemaphoreType.DMA((10,)),
            pltpu.SemaphoreType.DMA((128,)),
            pltpu.SemaphoreType.DMA((128,)),
        ],
        compiler_params=pltpu.CompilerParams(
            collective_id=2, has_side_effects=True, vmem_limit_bytes=56 * 1024 * 1024
        ),
    )(
        features,
        depth_kernel,
        w_up,
        w_down,
        projection,
        depth_bias[None, :],
        norm_gain[None, :],
        text_embeds,
        image_ids[None, :],
        text_ids[None, :],
        logit_scale[None, :],
        logit_bias[None, :],
    )
    loss, grad_texts, grad_kernel, grad_bias, grad_gain, grad_up, grad_down, grad_proj = deliver(
        count, *results
    )
    return (
        loss,
        grad_texts,
        grad_kernel,
        grad_bias[0],
        grad_gain[0],
        grad_up,
        grad_down,
        grad_proj,
    )


def fits_fused(mesh):
    return mesh.shape["dp"] == SIDE and mesh.shape["loop"] == SIDE * CORES


def solution(mesh):
    placed = (
        P("loop", None, None, None),
        P("loop"),
        P("loop", None),
        P(),
        P(),
        P(),
        P(),
        P(None, "dp"),
        P(None, "dp"),
        P(),
        P(),
        P(),
    )
    fused = fits_fused(mesh)
    return jax.shard_map(
        fused_device if fused else general_device,
        mesh=mesh,
        in_specs=placed,
        out_specs=(
            P("loop"),
            P("loop", None),
            P(),
            P(),
            P(),
            P("loop", "dp"),
            P("loop", "dp"),
            P(("dp", "loop"), None),
        ),
        check_vma=False,
    )
```

```python
import functools
import jax
import jax.numpy as jnp
from jax import lax
from jax.experimental import pallas as pl
from jax.experimental.pallas import tpu as pltpu
from jax.sharding import PartitionSpec as P

GRID = 7
LANES = 128
ROWS = 8
TAP_ROWS = 64

full_precision = lax.Precision.HIGHEST
half_root = 0.7071067811865476
density_factor = 0.3989422804014327


def gelu_value(values):
    return 0.5 * values * (1.0 + lax.erf(values * half_root))


def gelu_slope(values):
    cumulative = 0.5 * (1.0 + lax.erf(values * half_root))
    return cumulative + values * jnp.exp(-0.5 * values * values) * density_factor


def unit_rows(values):
    inverse = lax.rsqrt(jnp.sum(values * values, axis=1, keepdims=True) + 1e-06)
    return (values * inverse, inverse)


def lane_tile(index):
    return pl.ds(pl.multiple_of(index * LANES, LANES), LANES)


def shifted_rows(x_ref, lanes, by, cell):
    count = x_ref.shape[0]
    moved = []
    for row in range(GRID):
        per_image = []
        for n in range(count):
            tile = x_ref[n, row, :, lanes]
            if by != 0:
                tile = pltpu.roll(tile, (-by) % ROWS, 0)
            if abs(by) > 1:
                inside = (cell + by >= 0) & (cell + by < GRID)
                tile = jnp.where(inside, tile, 0.0)
            per_image.append(tile)
        moved.append(per_image)
    return moved


def conv_norm_kernel(x_ref, k_ref, bias_ref, unit_ref, inv_ref):
    count = x_ref.shape[0]
    channels = x_ref.shape[3]
    tiles = channels // LANES
    reach = (GRID - 1) // 2
    cell = lax.broadcasted_iota(jnp.int32, (ROWS, LANES), 0)
    cells = [(n, p) for p in range(GRID) for n in range(count)]

    def conv_tile(index, sums):
        lanes = lane_tile(index)
        bias = jnp.broadcast_to(bias_ref[:, lanes], (ROWS, LANES))
        out = {at: bias for at in cells}
        for col_off in range(GRID):
            moved = shifted_rows(x_ref, lanes, col_off - reach, cell)
            for row_off in range(GRID):
                tap = row_off * GRID + col_off
                weight = jnp.broadcast_to(k_ref[tap : tap + 1, lanes], (ROWS, LANES))
                for p in range(GRID):
                    row = p + row_off - reach
                    if 0 <= row < GRID:
                        for n in range(count):
                            out[(n, p)] = out[(n, p)] + moved[row][n] * weight
        for n, p in cells:
            unit_ref[n, p, :, lanes] = out[(n, p)]
        return tuple(total + out[at] for total, at in zip(sums, cells))

    zeros = tuple(jnp.zeros((ROWS, LANES), jnp.float32) for _ in cells)
    sums = lax.fori_loop(0, tiles, conv_tile, zeros)
    means = [jnp.sum(total, axis=1, keepdims=True) / channels for total in sums]
    means = [jnp.broadcast_to(mean, (ROWS, LANES)) for mean in means]

    def square_tile(index, sums):
        lanes = lane_tile(index)
        result = []
        for total, mean, (n, p) in zip(sums, means, cells):
            centered = unit_ref[n, p, :, lanes] - mean
            result.append(total + centered * centered)
        return tuple(result)

    squares = lax.fori_loop(0, tiles, square_tile, zeros)
    inverses = []
    for total, (n, p) in zip(squares, cells):
        variance = jnp.sum(total, axis=1, keepdims=True) / channels
        inverse = jnp.broadcast_to(lax.rsqrt(variance + 1e-06), (ROWS, LANES))
        inverse = jnp.where(cell < GRID, inverse, 0.0)
        inv_ref[n, p, :, :] = inverse
        inverses.append(inverse)

    def norm_tile(index, carry):
        lanes = lane_tile(index)
        for inverse, mean, (n, p) in zip(inverses, means, cells):
            unit = (unit_ref[n, p, :, lanes] - mean) * inverse
            unit_ref[n, p, :, lanes] = unit
        return carry

    lax.fori_loop(0, tiles, norm_tile, 0)


def conv_norm(padded, taps, bias):
    count, _, _, channels = padded.shape
    whole = pl.BlockSpec(memory_space=pltpu.VMEM)
    full = jax.ShapeDtypeStruct(padded.shape, jnp.float32)
    return pl.pallas_call(
        conv_norm_kernel,
        out_shape=(
            full,
            jax.ShapeDtypeStruct((count, GRID, ROWS, LANES), jnp.float32),
        ),
        in_specs=[whole] * 3,
        out_specs=(whole, whole),
        compiler_params=pltpu.CompilerParams(vmem_limit_bytes=24 * 1024 * 1024),
    )(padded, taps, bias)


def conv_grad_kernel(x_ref, unit_ref, inv_ref, gain_ref, grad_ref, out_ref, work_ref):
    count = x_ref.shape[0]
    channels = x_ref.shape[3]
    tiles = channels // LANES
    reach = (GRID - 1) // 2
    taps = GRID * GRID
    cell = lax.broadcasted_iota(jnp.int32, (ROWS, LANES), 0)
    cells = [(n, p) for p in range(GRID) for n in range(count)]
    zero = jnp.zeros((ROWS, LANES), jnp.float32)

    def first_tile(index, carry):
        plain, crossed = carry
        lanes = lane_tile(index)
        gain = jnp.broadcast_to(gain_ref[:, lanes], (ROWS, LANES))
        gain_sum = zero
        out_ref[index, 48:TAP_ROWS, :] = jnp.zeros((TAP_ROWS - 48, LANES), jnp.float32)
        plain_out = []
        crossed_out = []
        for at, (n, p) in enumerate(cells):
            unit = unit_ref[n, p, :, lanes]
            grad = grad_ref[n, p, :, lanes]
            gain_sum = gain_sum + grad * unit
            scaled = grad * gain
            plain_out.append(plain[at] + scaled)
            crossed_out.append(crossed[at] + scaled * unit)
        out_ref[index, taps + 1 : taps + 2, :] = jnp.sum(gain_sum, axis=0, keepdims=True)
        return (tuple(plain_out), tuple(crossed_out))

    zeros = tuple(zero for _ in cells)
    plain, crossed = lax.fori_loop(0, tiles, first_tile, (zeros, zeros))
    for at, (n, p) in enumerate(cells):
        first = jnp.sum(plain[at], axis=1, keepdims=True) / channels
        second = jnp.sum(crossed[at], axis=1, keepdims=True) / channels
        work_ref[0, n, p, :, :] = jnp.broadcast_to(first, (ROWS, LANES))
        work_ref[1, n, p, :, :] = jnp.broadcast_to(second, (ROWS, LANES))

    def tap_tile(index, carry):
        lanes = lane_tile(index)
        gain = jnp.broadcast_to(gain_ref[:, lanes], (ROWS, LANES))
        grad_conv = {}
        bias_sum = zero
        for n, p in cells:
            value = inv_ref[n, p, :, :] * (
                grad_ref[n, p, :, lanes] * gain
                - work_ref[0, n, p, :, :]
                - unit_ref[n, p, :, lanes] * work_ref[1, n, p, :, :]
            )
            grad_conv[(n, p)] = value
            bias_sum = bias_sum + value
        out_ref[index, taps : taps + 1, :] = jnp.sum(bias_sum, axis=0, keepdims=True)
        for col_off in range(GRID):
            moved = shifted_rows(x_ref, lanes, col_off - reach, cell)
            for row_off in range(GRID):
                tap = row_off * GRID + col_off
                total = zero
                for p in range(GRID):
                    row = p + row_off - reach
                    if 0 <= row < GRID:
                        for n in range(count):
                            total = total + moved[row][n] * grad_conv[(n, p)]
                out_ref[index, tap : tap + 1, :] = jnp.sum(total, axis=0, keepdims=True)
        return carry

    lax.fori_loop(0, tiles, tap_tile, 0)


def conv_grads(padded, unit, inverse, gain, grad):
    count, _, _, channels = padded.shape
    whole = pl.BlockSpec(memory_space=pltpu.VMEM)
    return pl.pallas_call(
        conv_grad_kernel,
        out_shape=jax.ShapeDtypeStruct((channels // LANES, TAP_ROWS, LANES), jnp.float32),
        in_specs=[whole] * 5,
        out_specs=whole,
        scratch_shapes=[pltpu.VMEM((2, count, GRID, ROWS, LANES), jnp.float32)],
        compiler_params=pltpu.CompilerParams(vmem_limit_bytes=24 * 1024 * 1024),
    )(padded, unit, inverse, gain, grad)


def peer_copies(axis, count, source_of, target, send_sems, recv_sems):
    me = lax.axis_index(axis)
    copies = []
    for by in range(1, count):
        peer = lax.rem(me + by, count)
        copy = pltpu.make_async_remote_copy(
            src_ref=source_of(peer),
            dst_ref=target.at[me],
            send_sem=send_sems.at[by],
            recv_sem=recv_sems.at[by],
            device_id={axis: peer},
            device_id_type=pl.DeviceIdType.MESH,
        )
        copy.start()
        copies.append(copy)
    return copies


def wait_all(copies):
    for copy in copies:
        copy.wait()


def meet_peers(sizes):
    barrier = pltpu.get_barrier_semaphore()
    total = 0
    for axis, count in sizes:
        me = lax.axis_index(axis)
        for by in range(1, count):
            pl.semaphore_signal(
                barrier,
                inc=1,
                device_id={axis: lax.rem(me + by, count)},
                device_id_type=pl.DeviceIdType.MESH,
            )
        total += count - 1
    pl.semaphore_wait(barrier, total)


def head_kernel(
    dp, loop, part_ref, mean_ref, rest_ref, pooled_ref, rest_out_ref, parts, own, sems
):
    meet_peers((("dp", dp), ("loop", loop)))
    loop_me = lax.axis_index("loop")
    dp_me = lax.axis_index("dp")
    dp_copies = peer_copies(
        "dp", dp, lambda peer: part_ref, parts, sems.at[0], sems.at[1]
    )
    rest_copies = peer_copies(
        "loop", loop, lambda peer: rest_ref, rest_out_ref, sems.at[2], sems.at[3]
    )
    parts[dp_me] = part_ref[...]
    rest_out_ref[loop_me] = rest_ref[...]
    wait_all(dp_copies)
    total = parts[0]
    for at in range(1, dp):
        total = total + parts[at]
    own[...] = mean_ref[...] + total
    pooled_copies = peer_copies(
        "loop", loop, lambda peer: own, pooled_ref, sems.at[4], sems.at[5]
    )
    pooled_ref[loop_me] = own[...]
    wait_all(rest_copies)
    wait_all(pooled_copies)


def head_exchange(part, mean, rest):
    dp = lax.axis_size("dp")
    loop = lax.axis_size("loop")
    whole = pl.BlockSpec(memory_space=pltpu.VMEM)
    return pl.pallas_call(
        functools.partial(head_kernel, dp, loop),
        out_shape=(
            jax.ShapeDtypeStruct((loop,) + part.shape, jnp.float32),
            jax.ShapeDtypeStruct((loop,) + rest.shape, jnp.float32),
        ),
        in_specs=[whole] * 3,
        out_specs=(whole, whole),
        scratch_shapes=[
            pltpu.VMEM((dp,) + part.shape, jnp.float32),
            pltpu.VMEM(part.shape, jnp.float32),
            pltpu.SemaphoreType.DMA((6, max(dp, loop))),
        ],
        compiler_params=pltpu.CompilerParams(
            collective_id=0, has_side_effects=True, vmem_limit_bytes=16 * 1024 * 1024
        ),
    )(part, mean, rest)


def total_kernel(dp, loop, part_ref, out_ref, dp_slots, loop_slots, block, chunk, sems):
    meet_peers((("dp", dp), ("loop", loop)))
    loop_me = lax.axis_index("loop")
    dp_me = lax.axis_index("dp")
    copies = peer_copies(
        "dp", dp, lambda peer: part_ref.at[peer], dp_slots, sems.at[0], sems.at[1]
    )
    dp_slots[dp_me] = part_ref[dp_me]
    wait_all(copies)
    total = dp_slots[0]
    for at in range(1, dp):
        total = total + dp_slots[at]
    block[...] = total
    copies = peer_copies(
        "loop", loop, lambda peer: block.at[peer], loop_slots, sems.at[2], sems.at[3]
    )
    loop_slots[loop_me] = block[loop_me]
    wait_all(copies)
    total = loop_slots[0]
    for at in range(1, loop):
        total = total + loop_slots[at]
    chunk[...] = total
    mine = out_ref.at[dp_me]
    copies = peer_copies("loop", loop, lambda peer: chunk, mine, sems.at[4], sems.at[5])
    out_ref[dp_me, loop_me] = chunk[...]
    wait_all(copies)
    copies = peer_copies("dp", dp, lambda peer: mine, out_ref, sems.at[6], sems.at[7])
    wait_all(copies)


def total_sum(part):
    dp = lax.axis_size("dp")
    loop = lax.axis_size("loop")
    rows = part.shape[0] * part.shape[1] // (dp * loop)
    whole = pl.BlockSpec(memory_space=pltpu.VMEM)
    summed = pl.pallas_call(
        functools.partial(total_kernel, dp, loop),
        out_shape=jax.ShapeDtypeStruct((dp, loop, rows, LANES), jnp.float32),
        in_specs=[whole],
        out_specs=whole,
        scratch_shapes=[
            pltpu.VMEM((dp, loop, rows, LANES), jnp.float32),
            pltpu.VMEM((loop, rows, LANES), jnp.float32),
            pltpu.VMEM((loop, rows, LANES), jnp.float32),
            pltpu.VMEM((rows, LANES), jnp.float32),
            pltpu.SemaphoreType.DMA((8, max(dp, loop))),
        ],
        compiler_params=pltpu.CompilerParams(
            collective_id=1, has_side_effects=True, vmem_limit_bytes=32 * 1024 * 1024
        ),
    )(part.reshape(dp, loop, rows, LANES))
    return summed.reshape(part.shape)


def dense_rows(values):
    return values.reshape(-1, LANES)


def general_device(
    features,
    image_ids,
    text_embeds,
    text_ids,
    depth_kernel,
    depth_bias,
    norm_gain,
    w_up,
    w_down,
    projection,
    logit_scale,
    logit_bias,
):
    image_rows = features.shape[0]
    channels = features.shape[3]
    hidden_share = w_up.shape[1]
    cell_count = GRID * GRID
    loop_count = lax.axis_size("loop")
    position = lax.axis_index("loop")
    image_count = image_rows * loop_count
    text_rows = text_embeds.shape[0]
    first_image = position * image_rows
    gather = functools.partial(lax.all_gather, axis_name="loop", axis=0, tiled=True)

    text_unit, text_inverse = unit_rows(text_embeds.astype(jnp.float32))
    cell_mean = jnp.mean(features.astype(jnp.float32), axis=(1, 2))

    padded = jnp.pad(
        features.astype(jnp.float32), ((0, 0), (0, 0), (0, ROWS - GRID), (0, 0))
    )
    gain_row = norm_gain[None, :]
    unit, inverse = conv_norm(
        padded,
        depth_kernel.astype(jnp.float32).reshape(cell_count, channels),
        depth_bias[None, :],
    )
    padded_rows = image_rows * GRID * ROWS
    unit_rows_own = unit.reshape(padded_rows, channels)
    unit_share = lax.all_to_all(unit_rows_own, "loop", split_axis=1, concat_axis=0, tiled=True)
    normed_rows = (unit_rows_own * gain_row).astype(jnp.bfloat16)
    pre_act = jnp.dot(normed_rows, w_up, preferred_element_type=jnp.float32)
    hidden_sum = jnp.sum(
        gelu_value(pre_act).reshape(image_rows, GRID * ROWS, hidden_share), axis=1
    )
    slope = gelu_slope(pre_act)
    hidden_own = (hidden_sum / cell_count).astype(jnp.bfloat16)
    mlp_part = lax.dot_general(
        hidden_own, w_down, (((1,), (1,)), ((), ())), preferred_element_type=jnp.float32
    )
    id_row = jnp.pad(image_ids.astype(jnp.float32), (0, LANES - image_rows))[None, :]
    rest = jnp.concatenate([dense_rows(hidden_sum), dense_rows(text_unit), id_row], axis=0)
    hidden_rows = image_rows * hidden_share // LANES
    text_end = hidden_rows + text_unit.size // LANES
    rest = jnp.pad(rest, ((0, -rest.shape[0] % ROWS), (0, 0)))
    pooled_all, rest_all = head_exchange(dense_rows(mlp_part), dense_rows(cell_mean), rest)
    slope_sent, unit_share, pooled_all = lax.optimization_barrier((slope, unit_share, pooled_all))
    slope_all = gather(slope_sent)
    pooled = pooled_all.reshape(image_count, channels).astype(jnp.bfloat16)
    hidden_all = rest_all[:, :hidden_rows].reshape(image_count, hidden_share)
    hidden_all = (hidden_all / cell_count).astype(jnp.bfloat16)
    text_all = rest_all[:, hidden_rows:text_end].reshape(-1, text_embeds.shape[1])
    ids_all = rest_all[:, text_end, :image_rows].reshape(image_count).astype(jnp.int32)
    embedding = jnp.dot(pooled, projection, preferred_element_type=jnp.float32)
    image_unit, image_inverse = unit_rows(embedding)
    logits = (
        logit_scale[0] * jnp.dot(image_unit, text_all.T, precision=full_precision)
        + logit_bias[0]
    )
    labels = jnp.where(ids_all[:, None] == text_ids[None, :], 1.0, -1.0).astype(jnp.float32)
    loss_all = -jnp.sum(jax.nn.log_sigmoid(labels * logits), axis=1)
    row_loss = lax.dynamic_slice_in_dim(loss_all, first_image, image_rows)
    coeffs = -logit_scale[0] * labels * jax.nn.sigmoid(-labels * logits)
    grad_image = jnp.dot(coeffs, text_all, precision=full_precision)
    own_coeffs = lax.dynamic_slice_in_dim(coeffs, position * text_rows, text_rows, 1)
    grad_text = jnp.dot(own_coeffs.T, image_unit, precision=full_precision)
    grad_texts = text_inverse * (
        grad_text - text_unit * jnp.sum(text_unit * grad_text, axis=1, keepdims=True)
    )
    grad_embed = (
        image_inverse
        * (grad_image - image_unit * jnp.sum(image_unit * grad_image, axis=1, keepdims=True))
    ).astype(jnp.bfloat16)
    grad_pooled = lax.dot_general(
        grad_embed, projection, (((1,), (1,)), ((), ())), preferred_element_type=jnp.float32
    ).astype(jnp.bfloat16)
    spread = jnp.dot(grad_pooled, w_down, preferred_element_type=jnp.float32) / cell_count
    own_spread = lax.dynamic_slice_in_dim(spread, first_image, image_rows)
    grad_pre = (
        (slope.reshape(image_rows, GRID * ROWS, hidden_share) * own_spread[:, None, :])
        .reshape(padded_rows, hidden_share)
        .astype(jnp.bfloat16)
    )
    grad_normed = lax.dot_general(
        grad_pre, w_up, (((1,), (1,)), ((), ())), preferred_element_type=jnp.float32
    ).reshape(padded.shape)
    part = conv_grads(padded, unit, inverse, gain_row, grad_normed)
    total = total_sum(part).transpose(1, 0, 2).reshape(TAP_ROWS, channels)
    grad_kernel = total[:cell_count].reshape(GRID, GRID, channels)
    grad_bias = total[cell_count]
    grad_gain = total[cell_count + 1]

    up_share = channels // loop_count
    grad_pooled_share = lax.dynamic_slice_in_dim(grad_pooled, position * up_share, up_share, 1)
    grad_down = lax.dot_general(
        grad_pooled_share, hidden_all, (((0,), (0,)), ((), ())), preferred_element_type=jnp.float32
    )
    proj_share = up_share // lax.axis_size("dp")
    proj_at = (lax.axis_index("dp") * loop_count + position) * proj_share
    pooled_share = lax.dynamic_slice_in_dim(pooled, proj_at, proj_share, 1)
    grad_proj = lax.dot_general(
        pooled_share, grad_embed, (((0,), (0,)), ((), ())), preferred_element_type=jnp.float32
    )
    grad_pre_all = (
        (slope_all.reshape(image_count, GRID * ROWS, hidden_share) * spread[:, None, :])
        .reshape(loop_count * padded_rows, hidden_share)
        .astype(jnp.bfloat16)
    )
    gain_share = lax.dynamic_slice_in_dim(norm_gain, position * up_share, up_share)
    normed_share = (unit_share * gain_share).astype(jnp.bfloat16)
    grad_up = lax.dot_general(
        normed_share,
        grad_pre_all,
        (((0,), (0,)), ((), ())),
        preferred_element_type=jnp.float32,
    )
    return (row_loss, grad_texts, grad_kernel, grad_bias, grad_gain, grad_up, grad_down, grad_proj)


SPLIT = 96
SIDE = 4
CORES = 2
PACKET = 2304
PART_ROWS = 56
MESH = pl.DeviceIdType.MESH
nn = (((1,), (0,)), ((), ()))
nt = (((1,), (1,)), ((), ()))
tn = (((0,), (0,)), ((), ()))


def product(left, right, dims, precision=None):
    return lax.dot_general(
        left, right, dims, preferred_element_type=jnp.float32, precision=precision
    )


def flipped(index, by):
    if by == 1:
        return index + 1 - 2 * lax.rem(index, 2)
    if by == 2:
        return lax.rem(index + 2, SIDE)
    return SIDE - 1 - index


def columns(start, size):
    return pl.ds(pl.multiple_of(start, LANES), size)


def rounded(values):
    return values.astype(jnp.bfloat16).astype(jnp.float32)


def image_of(first, shape, values):
    cells = GRID * GRID
    row = first + lax.broadcasted_iota(jnp.int32, shape, 0)
    out = jnp.broadcast_to(values[-1], shape)
    for n in reversed(range(len(values) - 1)):
        out = jnp.where(row < (n + 1) * cells, values[n], out)
    return jnp.where(row < len(values) * cells, out, 0.0)


def fused_kernel(
    xb,
    kb,
    wu_hbm,
    wd_hbm,
    pj_hbm,
    bias_ref,
    gain_ref,
    text_ref,
    iid_ref,
    tid_ref,
    scale_ref,
    shift_ref,
    o_loss,
    *refs,
):
    (
        o_text,
        o_kernel,
        o_bias,
        o_gain,
        o_up,
        o_down,
        o_proj,
        wu,
        wd,
        pj,
        x,
        kf,
        unit,
        inv,
        nf,
        nb,
        stats,
        stats_out,
        stats_in,
        pre,
        sl,
        gn,
        full,
        thin,
        far,
        nrow,
        gpre,
        fullb,
        packed,
        packets,
        texts_out,
        texts_in,
        texts,
        part_out,
        part_in,
        means,
        small,
        heads,
        gathered,
        work,
        taps_out,
        taps_in,
        taps_sum,
        taps_z,
        taps_all,
        up_out,
        up_in,
        local_sem,
        send_sem,
        recv_sem,
    ) = refs
    count, _, _, channels = xb.shape
    hidden = wu.shape[1]
    width = pj.shape[1]
    split = full.shape[1]
    total_rows = nf.shape[0]
    sent_rows = count * GRID * GRID
    sent_rows += -sent_rows % ROWS
    rest_rows = sent_rows - split
    tiles = channels // LANES
    reach = (GRID - 1) // 2
    taps = GRID * GRID
    chip = channels // SIDE
    half = hidden // 2
    dp = lax.axis_index("dp")
    loop = lax.axis_index("loop")
    z = loop // CORES
    core = lax.rem(loop, CORES)
    rank = dp * CORES + core
    planes = SIDE * CORES
    next_sem = [0]

    def take(number):
        first = next_sem[0]
        next_sem[0] += number
        return first

    def remote(src, dst, device, sem, sent=None):
        return pltpu.make_async_remote_copy(
            src_ref=src,
            dst_ref=dst,
            send_sem=send_sem.at[sem if sent is None else sent],
            recv_sem=recv_sem.at[sem],
            device_id=device,
            device_id_type=MESH,
        )

    def at_z(index):
        return {"dp": dp, "loop": index * CORES + core}

    def at_dp(index):
        return {"dp": index, "loop": loop}

    def at_rank(index):
        return {"dp": index // CORES, "loop": z * CORES + lax.rem(index, CORES)}

    partner = {"dp": dp, "loop": z * CORES + 1 - core}

    barrier = pltpu.get_barrier_semaphore()
    met = 0
    for by in range(1, planes):
        pl.semaphore_signal(
            barrier, inc=1, device_id={"dp": dp, "loop": lax.rem(loop + by, planes)}, device_id_type=MESH
        )
        met += 1
    for by in range(1, SIDE):
        for other in range(CORES):
            pl.semaphore_signal(
                barrier,
                inc=1,
                device_id={"dp": flipped(dp, by), "loop": z * CORES + other},
                device_id_type=MESH,
            )
            met += 1
    loads = []
    for at, (far_ref, near_ref) in enumerate(((wu_hbm, wu), (wd_hbm, wd), (pj_hbm, pj))):
        copy = pltpu.make_async_copy(far_ref, near_ref, local_sem.at[at])
        copy.start()
        loads.append(copy)

    text = text_ref[...].astype(jnp.float32)
    text_unit, text_inverse = unit_rows(text)
    third = width // 3
    texts_out[...] = jnp.zeros(texts_out.shape, jnp.float32)
    for k in range(3):
        texts_out[2 * k : 2 * k + 2, :] = text_unit[:, k * third : (k + 1) * third]

    cell = lax.broadcasted_iota(jnp.int32, (ROWS, LANES), 0)
    zero = jnp.zeros((ROWS, LANES), jnp.float32)
    cells = [(n, p) for n in range(count) for p in range(GRID)]

    edge = total_rows - 2 * ROWS
    nf[edge:total_rows, :] = jnp.zeros((2 * ROWS, channels), jnp.float32)

    def conv_tile(i, sums):
        lanes = lane_tile(lax.rem(dp * (tiles // SIDE) + i, tiles))
        for n, p in cells:
            x[n, p, 0:GRID, lanes] = xb[n, p, :, lanes].astype(jnp.float32)
            x[n, p, GRID:ROWS, lanes] = jnp.zeros((ROWS - GRID, LANES), jnp.float32)
        for a in range(GRID):
            kf[a * GRID : (a + 1) * GRID, lanes] = kb[a, :, lanes].astype(jnp.float32)
        bias = jnp.broadcast_to(bias_ref[:, lanes], (ROWS, LANES))
        out = {at: bias for at in cells}
        for col_off in range(GRID):
            moved = shifted_rows(x, lanes, col_off - reach, cell)
            for row_off in range(GRID):
                tap = row_off * GRID + col_off
                weight = jnp.broadcast_to(kf[tap : tap + 1, lanes], (ROWS, LANES))
                for p in range(GRID):
                    row = p + row_off - reach
                    if 0 <= row < GRID:
                        for n in range(count):
                            out[(n, p)] = out[(n, p)] + moved[row][n] * weight
        for n, p in cells:
            unit[n, p, :, lanes] = out[(n, p)]
            first = n * taps + p * GRID
            nf[first : first + ROWS, lanes] = out[(n, p)]
        return tuple(total + out[at] for total, at in zip(sums, cells))

    zeros = tuple(zero for _ in cells)
    early = tiles // SIDE
    sums = lax.fori_loop(0, early, conv_tile, zeros)

    pl.semaphore_wait(barrier, met)
    text_sem = take(planes)
    text_copies = []
    for by in range(1, planes):
        peer = {"dp": dp, "loop": lax.rem(loop + by, planes)}
        copy = remote(texts_out, texts_in.at[loop], peer, text_sem + by)
        copy.start()
        text_copies.append(copy)

    quarter = channels // SIDE
    slim = chip // SIDE
    own_quarter = columns(dp * quarter, quarter)
    own_slim = columns(dp * slim, slim)
    full_sem = take(SIDE)
    thin_sem = take(SIDE)
    far_sem = take(SIDE)
    relay_sem = take(2)
    inner = z * (SIDE - 1 - z) > 0
    full_copies = {}
    thin_copies = {}
    far_copies = {}
    for by in range(1, SIDE):
        peer = flipped(z, by)
        full_copies[by] = remote(
            nf.at[pl.ds(0, split), own_quarter],
            full.at[z, :, own_quarter],
            at_z(peer),
            full_sem + by,
        )
        thin_copies[by] = remote(
            nf.at[pl.ds(split, rest_rows), columns(peer * chip + dp * slim, slim)],
            thin.at[z, pl.ds(0, rest_rows), own_slim],
            at_z(peer),
            thin_sem + by,
        )
        far_copies[by] = remote(
            sl.at[pl.ds(split, rest_rows), :],
            far.at[z, pl.ds(0, rest_rows), :],
            at_z(peer),
            far_sem + by,
        )
    two_away = flipped(z, 2)
    full_relay = remote(
        full.at[two_away, :, own_quarter],
        full.at[two_away, :, own_quarter],
        at_z(flipped(z, 1)),
        full_sem + 3,
        relay_sem,
    )
    far_relay = remote(
        far.at[two_away, pl.ds(0, rest_rows), :],
        far.at[two_away, pl.ds(0, rest_rows), :],
        at_z(flipped(z, 1)),
        far_sem + 3,
        relay_sem + 1,
    )

    def when_inner(*actions):
        @pl.when(inner)
        def _():
            for action in actions:
                action()

    full_copies[1].start()
    full_copies[2].start()
    when_inner(full_copies[3].start)

    sums = lax.fori_loop(early, tiles, conv_tile, sums)
    for by in range(1, SIDE):
        thin_copies[by].start()
    centers = [jnp.sum(total, axis=1, keepdims=True) / channels for total in sums]
    centers = [jnp.broadcast_to(mean, (ROWS, LANES)) for mean in centers]

    def square_tile(index, sums):
        lanes = lane_tile(index)
        result = []
        for total, mean, (n, p) in zip(sums, centers, cells):
            centered = unit[n, p, :, lanes] - mean
            result.append(total + centered * centered)
        return tuple(result)

    squares = lax.fori_loop(0, tiles, square_tile, zeros)

    inverses = []
    for total, (n, p) in zip(squares, cells):
        variance = jnp.sum(total, axis=1, keepdims=True) / channels
        inverse = jnp.broadcast_to(lax.rsqrt(variance + 1e-06), (ROWS, LANES))
        inverse = jnp.where(cell < GRID, inverse, 0.0)
        inv[n, p, :, :] = inverse
        inverses.append(inverse)
    lane_at = lax.broadcasted_iota(jnp.int32, (ROWS, LANES), 1)
    side_by_side = lane_at < LANES // 2
    stats[edge:total_rows, :] = jnp.zeros((2 * ROWS, LANES), jnp.float32)
    for inverse, mean, (n, p) in zip(inverses, centers, cells):
        first = n * taps + p * GRID
        stats[first : first + ROWS, :] = jnp.where(side_by_side, mean, inverse)
    total = zero
    for k in range(total_rows // ROWS):
        values = stats[k * ROWS : (k + 1) * ROWS, :]
        total = total + jnp.where(lax.rem(lane_at, LANES // 2) == k, values, 0.0)
    stats_out[...] = total
    stats_sem = take(SIDE)
    stats_copies = {}
    for by in range(1, SIDE):
        copy = remote(stats_out, stats_in.at[z], at_z(flipped(z, by)), stats_sem + by)
        copy.start()
        stats_copies[by] = copy

    gn[edge:total_rows, :] = jnp.zeros((2 * ROWS, channels), jnp.float32)

    def norm_tile(index, carry):
        lanes = lane_tile(index)
        gain = jnp.broadcast_to(gain_ref[:, lanes], (ROWS, LANES))
        for inverse, mean, (n, p) in zip(inverses, centers, cells):
            value = (unit[n, p, :, lanes] - mean) * inverse
            unit[n, p, :, lanes] = value
            first = n * taps + p * GRID
            gn[first : first + ROWS, lanes] = value * gain
        return carry

    lax.fori_loop(0, tiles, norm_tile, 0)

    def narrow(i, carry):
        rows = pl.ds(pl.multiple_of(i * 2 * ROWS, 2 * ROWS), 2 * ROWS)
        nb[rows, :] = gn[rows, :].astype(jnp.bfloat16)
        return carry

    lax.fori_loop(0, total_rows // (2 * ROWS), narrow, 0)

    loads[0].wait()
    strip = 2 * LANES

    def expand(rows_ref, rows):
        def step(j, carry):
            lanes = pl.ds(pl.multiple_of(j * strip, strip), strip)
            pre[0:rows, lanes] = product(rows_ref[0:rows, :], wu[:, lanes], nn)
            return carry

        lax.fori_loop(0, hidden // strip, step, 0)

    expand(nb, total_rows)

    def activate(i, carry):
        rows = pl.ds(pl.multiple_of((i // 2) * 2 * ROWS, 2 * ROWS), 2 * ROWS)
        lanes = pl.ds(pl.multiple_of(lax.rem(i, 2) * half, LANES), half)
        values = pre[rows, lanes]
        cumulative = 0.5 * (1.0 + lax.erf(values * half_root))
        sl[rows, lanes] = cumulative + values * jnp.exp(-0.5 * values * values) * density_factor
        pre[rows, lanes] = values * cumulative
        return carry

    lax.fori_loop(0, total_rows // ROWS, activate, 0)

    far_copies[1].start()

    row_wide = lax.broadcasted_iota(jnp.int32, (ROWS, hidden), 0)
    heads[...] = jnp.zeros(heads.shape, jnp.float32)
    for n in range(count):
        begin, end = n * taps, (n + 1) * taps
        total = jnp.zeros((ROWS, hidden), jnp.float32)
        for tile in range(begin // ROWS, -(-end // ROWS)):
            values = pre[tile * ROWS : (tile + 1) * ROWS, :]
            if tile * ROWS < begin:
                values = jnp.where(row_wide >= begin - tile * ROWS, values, 0.0)
            if (tile + 1) * ROWS > end:
                values = jnp.where(row_wide < end - tile * ROWS, values, 0.0)
            total = total + values
        mean = jnp.sum(total, axis=0, keepdims=True) / taps
        heads[n : n + 1, 0:hidden] = rounded(mean)

    loads[1].wait()
    mlp = product(heads[:, 0:hidden].astype(jnp.bfloat16), wd[...], nt)
    part_out[...] = jnp.zeros(part_out.shape, jnp.float32)
    part_out[0:count, :] = mlp[0:count, 0:hidden]
    part_out[count : 2 * count, :] = mlp[0:count, hidden : 2 * hidden]
    part_sem = take(SIDE)
    part_copies = []
    for by in range(1, SIDE):
        copy = remote(part_out, part_in.at[dp], at_dp(flipped(dp, by)), part_sem + by)
        copy.start()
        part_copies.append(copy)
    first_sem = take(3 * SIDE)
    second_sem = take(3 * SIDE)
    slim_sem = take(SIDE * SIDE)
    half_quarter = quarter // 2
    first_hop = {}
    second_hop = {}
    slim_hop = {}

    def hop_one(by):
        peer = flipped(z, by)
        if by == 3:
            full_copies[3].wait_recv()
            when_inner(full_copies[3].wait_send, full_relay.wait_send)
        else:
            full_copies[by].wait()
        if by == 2:
            when_inner(full_relay.start)
        thin_copies[by].wait()
        block = full.at[peer, :, own_quarter]
        first_hop[by] = []
        for to in (1, 2):
            copy = remote(block, block, at_dp(flipped(dp, to)), first_sem + 3 * by + to)
            copy.start()
            first_hop[by].append(copy)
        piece = thin.at[peer, pl.ds(0, rest_rows), own_slim]
        slim_hop[by] = []
        for to in range(1, SIDE):
            copy = remote(piece, piece, at_dp(flipped(dp, to)), slim_sem + SIDE * by + to)
            copy.start()
            slim_hop[by].append(copy)

    def hop_two(by):
        peer = flipped(z, by)
        second_hop[by] = []
        for to in (1, 2):
            first_hop[by][to - 1].wait_recv()
            source = flipped(dp, to)
            block = full.at[peer, :, columns(source * quarter + (to - 1) * half_quarter, half_quarter)]
            copy = remote(block, block, at_dp(flipped(dp, 3 - to)), second_sem + 3 * by + to)
            copy.start()
            second_hop[by].append(copy)

    def arrived(by):
        for copy in second_hop[by]:
            copy.wait()
        for copy in first_hop[by]:
            copy.wait_send()
        for copy in slim_hop[by]:
            copy.wait()
        if by == 3:
            far_copies[3].wait_recv()
            when_inner(far_copies[3].wait_send, far_relay.wait_send)
        elif by == 1:
            far_copies[1].wait()

    hop_one(1)
    part_in[dp] = part_out[...]
    means[...] = jnp.zeros(means.shape, jnp.float32)
    for n in range(count):
        total = x[n, 0]
        for p in range(1, GRID):
            total = total + x[n, p]
        mean = jnp.sum(total, axis=0, keepdims=True) / taps
        means[n : n + 1, :] = mean[:, 0:hidden]
        means[count + n : count + n + 1, :] = mean[:, hidden : 2 * hidden]
    for copy in text_copies:
        copy.wait()
    texts_in[loop] = texts_out[...]
    for l in range(planes):
        for k in range(3):
            texts[2 * l : 2 * l + 2, k * third : (k + 1) * third] = texts_in[l, 2 * k : 2 * k + 2, :]
    loads[2].wait()
    small[...] = jnp.zeros(small.shape, jnp.float32)
    for copy in part_copies:
        copy.wait()
    total = part_in[0]
    for at in range(1, SIDE):
        total = total + part_in[at]
    pooled = rounded(means[...] + total)
    small[0:count, 0:hidden] = pooled[0:count, :]
    small[0:count, hidden : 2 * hidden] = pooled[count : 2 * count, :]

    embedding = product(small[...].astype(jnp.bfloat16), pj[...], nn)[0:ROWS, :]
    image_unit, image_inverse = unit_rows(embedding)
    all_texts = texts[...]
    text_count = all_texts.shape[0]
    scale = scale_ref[...]
    logits = scale * product(image_unit, all_texts, nt, full_precision) + shift_ref[...]
    ids = jnp.broadcast_to(iid_ref[...].astype(jnp.float32), (ROWS, count))
    spot_row = lax.broadcasted_iota(jnp.int32, (ROWS, count), 0)
    spot_col = lax.broadcasted_iota(jnp.int32, (ROWS, count), 1)
    own_ids = jnp.sum(jnp.where(spot_row == spot_col, ids, 0.0), axis=1, keepdims=True)
    same = jnp.broadcast_to(own_ids, (ROWS, text_count)) == jnp.broadcast_to(
        tid_ref[...].astype(jnp.float32), (ROWS, text_count)
    )
    labels = jnp.where(same, 1.0, -1.0)
    signed = labels * logits
    losses = jnp.log1p(jnp.exp(-jnp.abs(signed))) - jnp.minimum(signed, 0.0)
    loss = jnp.broadcast_to(jnp.sum(losses, axis=1, keepdims=True), (ROWS, LANES))
    o_loss[...] = jnp.sum(jnp.where(cell == lane_at, loss, 0.0), axis=0, keepdims=True)
    coeffs = -scale * labels * lax.logistic(-signed)
    grad_image = product(coeffs, all_texts, nn, full_precision)
    own_row = lax.broadcasted_iota(jnp.int32, (ROWS, width), 0)
    grad_embed = image_inverse * (
        grad_image - image_unit * jnp.sum(image_unit * grad_image, axis=1, keepdims=True)
    )
    grad_embed = jnp.where(own_row < count, rounded(grad_embed), 0.0)
    grad_text = product(coeffs, image_unit, tn, full_precision)
    heads[0:ROWS, hidden : hidden + width] = grad_embed
    grad_pooled = product(heads[:, hidden : hidden + width].astype(jnp.bfloat16), pj[...], nt)
    grad_pooled = grad_pooled.astype(jnp.bfloat16)
    spread = product(grad_pooled, wd[...], nn) / taps
    grad_pooled = grad_pooled.astype(jnp.float32)

    for at in range(SIDE):
        packed[at, 0:count, 0:chip] = grad_pooled[0:count, at * chip : (at + 1) * chip]
        packed[at, 0:count, chip : chip + LANES] = small[
            0:count, columns(dp * quarter + at * LANES, LANES)
        ]
        packed[at, 0:count, chip + LANES : chip + LANES + width] = grad_embed[0:count, :]
        packed[at, count : 2 * count, 0:hidden] = heads[0:count, 0:hidden]
        packed[at, count : 2 * count, hidden : 2 * hidden] = spread[0:count, :]
        packed[at, 6:8, 0:width] = grad_text[4 * at : 4 * at + 2, :]
        packed[at, 6:8, width : 2 * width] = grad_text[4 * at + 2 : 4 * at + 4, :]
    packet_sem = take(SIDE)
    packet_copies = {}
    for by in range(1, SIDE):
        peer = flipped(z, by)
        copy = remote(packed.at[peer], packets.at[core, z], at_z(peer), packet_sem + by)
        copy.start()
        packet_copies[by] = copy
    packets[core, z] = packed[z]
    far_copies[2].start()
    when_inner(far_copies[3].start)


    spreads = [spread[n : n + 1, :] for n in range(count)]

    def own_slopes(i, carry):
        first = pl.multiple_of(i * 2 * ROWS, 2 * ROWS)
        rows = pl.ds(first, 2 * ROWS)
        for lanes in (slice(0, half), slice(half, hidden)):
            scaled = image_of(first, (2 * ROWS, half), [s[:, lanes] for s in spreads])
            gpre[rows, lanes] = (sl[rows, lanes] * scaled).astype(jnp.bfloat16)
        return carry

    lax.fori_loop(0, total_rows // (2 * ROWS), own_slopes, 0)
    hop_one(2)
    hop_two(1)

    def contract(j, carry):
        lanes = pl.ds(pl.multiple_of(j * strip, strip), strip)
        gn[:, lanes] = product(gpre[0:total_rows, :], wu[lanes, :], nt)
        return carry

    lax.fori_loop(0, channels // strip, contract, 0)
    own_chip = columns(z * chip, chip)
    nrow[0:total_rows, :] = nb[:, own_chip]

    def first_tile(index, carry):
        plain, crossed = carry
        lanes = lane_tile(index)
        gain = jnp.broadcast_to(gain_ref[:, lanes], (ROWS, LANES))
        gain_sum = zero
        taps_out[index, 48:PART_ROWS, :] = jnp.zeros((PART_ROWS - 48, LANES), jnp.float32)
        plain_out = []
        crossed_out = []
        for at, (n, p) in enumerate(cells):
            first = n * taps + p * GRID
            value = unit[n, p, :, lanes]
            grad = gn[first : first + ROWS, lanes]
            gain_sum = gain_sum + grad * value
            scaled = grad * gain
            plain_out.append(plain[at] + scaled)
            crossed_out.append(crossed[at] + scaled * value)
        taps_out[index, taps + 1 : taps + 2, :] = jnp.sum(gain_sum, axis=0, keepdims=True)
        return (tuple(plain_out), tuple(crossed_out))

    plain, crossed = lax.fori_loop(0, tiles, first_tile, (zeros, zeros))
    for at, (n, p) in enumerate(cells):
        first = jnp.sum(plain[at], axis=1, keepdims=True) / channels
        second = jnp.sum(crossed[at], axis=1, keepdims=True) / channels
        work[0, n, p, :, :] = jnp.broadcast_to(first, (ROWS, LANES))
        work[1, n, p, :, :] = jnp.broadcast_to(second, (ROWS, LANES))

    own_tiles = tiles // planes
    sent_tiles = tiles - own_tiles
    taps_sem = take(sent_tiles)

    def taps_copy(i):
        owner = lax.rem(rank + 1 + i // own_tiles, planes)
        return remote(
            taps_out.at[owner * own_tiles + lax.rem(i, own_tiles)],
            taps_in.at[rank, lax.rem(i, own_tiles)],
            at_rank(owner),
            taps_sem + i,
        )

    def tap_tile(i, carry):
        index = lax.rem(rank * own_tiles + own_tiles + i, tiles)
        lanes = lane_tile(index)
        gain = jnp.broadcast_to(gain_ref[:, lanes], (ROWS, LANES))
        grad_conv = {}
        bias_sum = zero
        for n, p in cells:
            first = n * taps + p * GRID
            value = inv[n, p, :, :] * (
                gn[first : first + ROWS, lanes] * gain
                - work[0, n, p, :, :]
                - unit[n, p, :, lanes] * work[1, n, p, :, :]
            )
            grad_conv[(n, p)] = value
            bias_sum = bias_sum + value
        taps_out[index, taps : taps + 1, :] = jnp.sum(bias_sum, axis=0, keepdims=True)
        for col_off in range(GRID):
            moved = shifted_rows(x, lanes, col_off - reach, cell)
            for row_off in range(GRID):
                tap = row_off * GRID + col_off
                total = zero
                for p in range(GRID):
                    row = p + row_off - reach
                    if 0 <= row < GRID:
                        for n in range(count):
                            total = total + moved[row][n] * grad_conv[(n, p)]
                taps_out[index, tap : tap + 1, :] = jnp.sum(total, axis=0, keepdims=True)

        @pl.when(i < sent_tiles)
        def _():
            taps_copy(i).start()

        return carry

    lax.fori_loop(0, tiles // 2, tap_tile, 0)
    hop_two(2)
    lax.fori_loop(tiles // 2, tiles, tap_tile, 0)
    hop_one(3)

    for by in range(1, SIDE):
        packet_copies[by].wait()
    cross_sem = take(1)
    cross = remote(packets.at[core], packets.at[core], partner, cross_sem)
    cross.start()

    def other_rows(by):
        peer = flipped(z, by)
        base = by * total_rows
        arrived(by)
        stats_copies[by].wait()
        scales = stats_in[peer]

        def spot(k):
            return jnp.sum(jnp.where(lane_at == k, scales, 0.0), axis=1, keepdims=True)

        def normed(values, k, gain):
            parts = []
            for at in range(2):
                part = values[at * ROWS : (at + 1) * ROWS, :] - spot(k + at)
                parts.append(part * spot(k + at + LANES // 2) * gain)
            return jnp.concatenate(parts, axis=0)

        def cast(i, carry):
            first = pl.multiple_of(i * 2 * ROWS, 2 * ROWS)
            rows = pl.ds(first, 2 * ROWS)
            fullb[rows, :] = normed(full[peer, rows, :], 2 * i, gain_ref[...]).astype(jnp.bfloat16)
            nrow[pl.ds(base + first, 2 * ROWS), :] = fullb[rows, own_chip]
            return carry

        lax.fori_loop(0, split // (2 * ROWS), cast, 0)
        expand(fullb, split)
        spreads = [
            packets[core, peer, count + n : count + n + 1, hidden : 2 * hidden] for n in range(count)
        ]

        def slopes(i, carry):
            first = pl.multiple_of(i * 2 * ROWS, 2 * ROWS)
            for lanes in (slice(0, half), slice(half, hidden)):
                scaled = image_of(first, (2 * ROWS, half), [s[:, lanes] for s in spreads])
                values = gelu_slope(pre[pl.ds(first, 2 * ROWS), lanes]) * scaled
                gpre[pl.ds(base + first, 2 * ROWS), lanes] = values.astype(jnp.bfloat16)
            return carry

        lax.fori_loop(0, split // (2 * ROWS), slopes, 0)
        for i in range((total_rows - split) // (2 * ROWS)):
            first = i * 2 * ROWS
            at = split + first
            rows = slice(first, first + 2 * ROWS)
            keep = lax.broadcasted_iota(jnp.int32, (2 * ROWS, chip), 0) + at < count * taps
            values = normed(thin[peer, rows, :], at // ROWS, gain_ref[:, own_chip])
            values = jnp.where(keep, values, 0.0)
            nrow[base + at : base + at + 2 * ROWS, :] = values.astype(jnp.bfloat16)
            for lanes in (slice(0, half), slice(half, hidden)):
                keep = lax.broadcasted_iota(jnp.int32, (2 * ROWS, half), 0) + at < count * taps
                scaled = image_of(at, (2 * ROWS, half), [s[:, lanes] for s in spreads])
                values = jnp.where(keep, far[peer, rows, lanes] * scaled, 0.0)
                gpre[base + at : base + at + 2 * ROWS, lanes] = values.astype(jnp.bfloat16)

    other_rows(1)

    def taps_wait(i, carry):
        taps_copy(i).wait()
        return carry

    lax.fori_loop(0, sent_tiles, taps_wait, 0)
    for k in range(own_tiles):
        total = taps_out[rank * own_tiles + k]
        for by in range(1, planes):
            total = total + taps_in[lax.rem(rank + by, planes), k]
        taps_sum[k] = total
    along_sem = take(SIDE)
    along_copies = []
    for by in range(1, SIDE):
        copy = remote(taps_sum, taps_z.at[z], at_z(flipped(z, by)), along_sem + by)
        copy.start()
        along_copies.append(copy)
    taps_z[z] = taps_sum[...]

    cross.wait()

    def collect(lanes, shift, first_lane):
        for other in range(CORES):
            for at in range(SIDE):
                values = packets[other, at, :, lanes]
                if shift:
                    values = pltpu.roll(values, ROWS - shift, 0)
                keep = lax.broadcasted_iota(jnp.int32, values.shape, 0) < count
                first = (other * SIDE + at) * ROWS
                gathered[first : first + ROWS, first_lane : first_lane + values.shape[1]] = jnp.where(
                    keep, values, 0.0
                )

    share = chip // CORES
    collect(columns(core * share, share), 0, 0)
    collect(slice(chip, chip + LANES + width), 0, share)
    collect(slice(0, hidden), count, share + LANES + width)
    end = share + LANES + width
    o_down[...] = product(
        gathered[:, 0:share].astype(jnp.bfloat16), gathered[:, end : end + hidden].astype(jnp.bfloat16), tn
    )
    proj_two = product(
        gathered[:, share : share + LANES].astype(jnp.bfloat16),
        gathered[:, share + LANES : end].astype(jnp.bfloat16),
        tn,
    )
    proj_rows = LANES // CORES
    gn[0:LANES, 0:width] = proj_two
    o_proj[...] = gn[pl.ds(pl.multiple_of(core * proj_rows, proj_rows), proj_rows), 0:width]
    total = jnp.zeros((ROWS, width), jnp.float32)
    for at in range(SIDE):
        for other in range(CORES):
            total = total + packets[other, at, :, columns(core * width, width)]
    grad_text = total[6:8, :]
    o_text[...] = text_inverse * (
        grad_text - text_unit * jnp.sum(text_unit * grad_text, axis=1, keepdims=True)
    )


    far_copies[2].wait()
    when_inner(far_relay.start)
    hop_two(3)
    other_rows(2)

    for copy in along_copies:
        copy.wait()
    for k in range(own_tiles):
        total = taps_z[0, k]
        for at in range(1, SIDE):
            total = total + taps_z[at, k]
        taps_all[rank * own_tiles + k] = total
    spread_sem = take(2 * SIDE)

    def tiles_of(index):
        return taps_all.at[pl.ds(index * own_tiles, own_tiles)]

    mine = tiles_of(rank)
    spread_copies = [remote(mine, mine, partner, spread_sem)]
    for by in range(1, SIDE):
        spread_copies.append(remote(mine, mine, at_dp(flipped(dp, by)), spread_sem + by))
    for copy in spread_copies:
        copy.start()

    other_rows(3)

    def up_strip(rows_at, j):
        lanes = pl.ds(pl.multiple_of(j * strip, strip), strip)
        return lanes, product(nrow[:, rows_at], gpre[:, lanes], tn)

    theirs = columns((1 - core) * share, share)
    ours = columns(core * share, share)
    steps = hidden // strip
    up_sem = take(steps)

    def up_copy(j):
        return remote(up_out.at[j], up_in.at[j], partner, up_sem + j)

    def up_send(j, carry):
        lanes, values = up_strip(theirs, j)
        up_out[j] = values
        up_copy(j).start()
        return carry

    lax.fori_loop(0, steps, up_send, 0)
    share_copies = []
    for by in range(1, SIDE):
        spread_copies[by].wait()
        theirs_at = flipped(dp, by) * CORES + core
        copy = remote(tiles_of(theirs_at), tiles_of(theirs_at), partner, spread_sem + SIDE + by)
        copy.start()
        share_copies.append(copy)

    def up_own(j, carry):
        lanes, values = up_strip(ours, j)
        o_up[:, lanes] = values
        return carry

    lax.fori_loop(0, steps, up_own, 0)

    spread_copies[0].wait()
    for copy in share_copies:
        copy.wait()
    for index in range(tiles):
        lanes = slice(index * LANES, (index + 1) * LANES)
        for a in range(GRID):
            o_kernel[a, :, lanes] = taps_all[index, a * GRID : (a + 1) * GRID, :]
        o_bias[:, lanes] = taps_all[index, taps : taps + 1, :]
        o_gain[:, lanes] = taps_all[index, taps + 1 : taps + 2, :]


    def up_add(j, carry):
        lanes = pl.ds(pl.multiple_of(j * strip, strip), strip)
        up_copy(j).wait()
        o_up[:, lanes] = o_up[:, lanes] + up_in[j]
        return carry

    lax.fori_loop(0, steps, up_add, 0)


def deliver_kernel(loss, *refs):
    number = (len(refs) - 2) // 2
    held, out_loss, placed, sems = refs[:number], refs[number], refs[number + 1 : -1], refs[-1]
    copies = []
    for at in range(number):
        copy = pltpu.make_async_copy(held[at], placed[at], sems.at[at])
        copy.start()
        copies.append(copy)
    for n in range(out_loss.shape[0]):
        out_loss[n] = loss[0, n]
    wait_all(copies)


def deliver(count, loss, *held):
    outside = pl.BlockSpec(memory_space=pl.ANY)
    return pl.pallas_call(
        deliver_kernel,
        out_shape=(jax.ShapeDtypeStruct((count,), jnp.float32),)
        + tuple(jax.ShapeDtypeStruct(h.shape, h.dtype) for h in held),
        in_specs=[pl.BlockSpec(memory_space=pltpu.VMEM)] * (1 + len(held)),
        out_specs=(pl.BlockSpec(memory_space=pltpu.SMEM),) + (outside,) * len(held),
        scratch_shapes=[pltpu.SemaphoreType.DMA((len(held),))],
        compiler_params=pltpu.CompilerParams(vmem_limit_bytes=8 * 1024 * 1024),
    )(loss, *held)


def fused_device(
    features,
    image_ids,
    text_embeds,
    text_ids,
    depth_kernel,
    depth_bias,
    norm_gain,
    w_up,
    w_down,
    projection,
    logit_scale,
    logit_bias,
):
    count, _, _, channels = features.shape
    hidden = w_up.shape[1]
    width = projection.shape[1]
    texts = text_ids.shape[0]
    text_rows = text_embeds.shape[0]
    cells = count * GRID * GRID
    rows = cells + -cells % (2 * ROWS)
    chip = channels // SIDE
    share = chip // CORES
    strip = 2 * LANES
    planes = SIDE * CORES
    own_tiles = channels // LANES // planes
    whole = pl.BlockSpec(memory_space=pltpu.VMEM)
    outside = pl.BlockSpec(memory_space=pl.ANY)

    def room(*shape):
        return pltpu.VMEM(shape, jnp.float32)

    def narrow(*shape):
        return pltpu.VMEM(shape, jnp.bfloat16)

    def result(*shape):
        return pltpu.VMEM(shape, jnp.float32)

    results = pl.pallas_call(
        fused_kernel,
        out_shape=(
            result(1, LANES),
            result(text_rows, width),
            result(GRID, GRID, channels),
            result(1, channels),
            result(1, channels),
            result(share, hidden),
            result(share, hidden),
            result(LANES // CORES, width),
        ),
        in_specs=[whole] * 2 + [outside] * 3 + [whole] * 7,
        out_specs=(whole,) * 8,
        scratch_shapes=[
            narrow(channels, hidden),
            narrow(channels, hidden),
            narrow(channels, width),
            room(count, GRID, ROWS, channels),
            room(PART_ROWS, channels),
            room(count, GRID, ROWS, channels),
            room(count, GRID, ROWS, LANES),
            room(rows, channels),
            narrow(rows, channels),
            room(rows, LANES),
            room(ROWS, LANES),
            room(SIDE, ROWS, LANES),
            room(rows, hidden),
            room(rows, hidden),
            room(rows, channels),
            room(SIDE, SPLIT, channels),
            room(SIDE, rows - SPLIT, chip),
            room(SIDE, rows - SPLIT, hidden),
            narrow(SIDE * rows, chip),
            narrow(SIDE * rows, hidden),
            narrow(SPLIT, channels),
            room(SIDE, ROWS, PACKET),
            room(CORES, SIDE, ROWS, PACKET),
            room(ROWS, width // 3),
            room(planes, ROWS, width // 3),
            room(texts, width),
            room(ROWS, hidden),
            room(SIDE, ROWS, hidden),
            room(ROWS, hidden),
            room(2 * ROWS, channels),
            room(2 * ROWS, hidden + width),
            room(planes * ROWS, share + LANES + width + hidden),
            room(2, count, GRID, ROWS, LANES),
            room(channels // LANES, PART_ROWS, LANES),
            room(planes, own_tiles, PART_ROWS, LANES),
            room(own_tiles, PART_ROWS, LANES),
            room(SIDE, own_tiles, PART_ROWS, LANES),
            room(channels // LANES, PART_ROWS, LANES),
            room(hidden // strip, share, strip),
            room(hidden // strip, share, strip),
            pltpu.SemaphoreType.DMA((3,)),
            pltpu.SemaphoreType.DMA((128,)),
            pltpu.SemaphoreType.DMA((128,)),
        ],
        compiler_params=pltpu.CompilerParams(
            collective_id=2, has_side_effects=True, vmem_limit_bytes=54 * 1024 * 1024
        ),
    )(
        features,
        depth_kernel,
        w_up,
        w_down,
        projection,
        depth_bias[None, :],
        norm_gain[None, :],
        text_embeds,
        image_ids[None, :],
        text_ids[None, :],
        logit_scale[None, :],
        logit_bias[None, :],
    )
    loss, grad_texts, grad_kernel, grad_bias, grad_gain, grad_up, grad_down, grad_proj = deliver(
        count, *results
    )
    return (
        loss,
        grad_texts,
        grad_kernel,
        grad_bias[0],
        grad_gain[0],
        grad_up,
        grad_down,
        grad_proj,
    )


def fits_fused(mesh):
    return mesh.shape["dp"] == SIDE and mesh.shape["loop"] == SIDE * CORES


def solution(mesh):
    placed = (
        P("loop", None, None, None),
        P("loop"),
        P("loop", None),
        P(),
        P(),
        P(),
        P(),
        P(None, "dp"),
        P(None, "dp"),
        P(),
        P(),
        P(),
    )
    fused = fits_fused(mesh)
    return jax.shard_map(
        fused_device if fused else general_device,
        mesh=mesh,
        in_specs=placed,
        out_specs=(
            P("loop"),
            P("loop", None),
            P(),
            P(),
            P(),
            P("loop", "dp"),
            P("loop", "dp"),
            P(("dp", "loop"), None),
        ),
        check_vma=False,
    )
```

```python
import functools
import jax
import jax.numpy as jnp
from jax import lax
from jax.experimental import pallas as pl
from jax.experimental.pallas import tpu as pltpu
from jax.sharding import PartitionSpec as P

GRID = 7
LANES = 128
ROWS = 8
TAP_ROWS = 64

full_precision = lax.Precision.HIGHEST
half_root = 0.7071067811865476
density_factor = 0.3989422804014327


def gelu_value(values):
    return 0.5 * values * (1.0 + lax.erf(values * half_root))


def gelu_slope(values):
    cumulative = 0.5 * (1.0 + lax.erf(values * half_root))
    return cumulative + values * jnp.exp(-0.5 * values * values) * density_factor


def unit_rows(values):
    inverse = lax.rsqrt(jnp.sum(values * values, axis=1, keepdims=True) + 1e-06)
    return (values * inverse, inverse)


def lane_tile(index):
    return pl.ds(pl.multiple_of(index * LANES, LANES), LANES)


def shifted_rows(x_ref, lanes, by, cell):
    count = x_ref.shape[0]
    moved = []
    for row in range(GRID):
        per_image = []
        for n in range(count):
            tile = x_ref[n, row, :, lanes]
            if by != 0:
                tile = pltpu.roll(tile, (-by) % ROWS, 0)
            if abs(by) > 1:
                inside = (cell + by >= 0) & (cell + by < GRID)
                tile = jnp.where(inside, tile, 0.0)
            per_image.append(tile)
        moved.append(per_image)
    return moved


def conv_norm_kernel(x_ref, k_ref, bias_ref, unit_ref, inv_ref):
    count = x_ref.shape[0]
    channels = x_ref.shape[3]
    tiles = channels // LANES
    reach = (GRID - 1) // 2
    cell = lax.broadcasted_iota(jnp.int32, (ROWS, LANES), 0)
    cells = [(n, p) for p in range(GRID) for n in range(count)]

    def conv_tile(index, sums):
        lanes = lane_tile(index)
        bias = jnp.broadcast_to(bias_ref[:, lanes], (ROWS, LANES))
        out = {at: bias for at in cells}
        for col_off in range(GRID):
            moved = shifted_rows(x_ref, lanes, col_off - reach, cell)
            for row_off in range(GRID):
                tap = row_off * GRID + col_off
                weight = jnp.broadcast_to(k_ref[tap : tap + 1, lanes], (ROWS, LANES))
                for p in range(GRID):
                    row = p + row_off - reach
                    if 0 <= row < GRID:
                        for n in range(count):
                            out[(n, p)] = out[(n, p)] + moved[row][n] * weight
        for n, p in cells:
            unit_ref[n, p, :, lanes] = out[(n, p)]
        return tuple(total + out[at] for total, at in zip(sums, cells))

    zeros = tuple(jnp.zeros((ROWS, LANES), jnp.float32) for _ in cells)
    sums = lax.fori_loop(0, tiles, conv_tile, zeros)
    means = [jnp.sum(total, axis=1, keepdims=True) / channels for total in sums]
    means = [jnp.broadcast_to(mean, (ROWS, LANES)) for mean in means]

    def square_tile(index, sums):
        lanes = lane_tile(index)
        result = []
        for total, mean, (n, p) in zip(sums, means, cells):
            centered = unit_ref[n, p, :, lanes] - mean
            result.append(total + centered * centered)
        return tuple(result)

    squares = lax.fori_loop(0, tiles, square_tile, zeros)
    inverses = []
    for total, (n, p) in zip(squares, cells):
        variance = jnp.sum(total, axis=1, keepdims=True) / channels
        inverse = jnp.broadcast_to(lax.rsqrt(variance + 1e-06), (ROWS, LANES))
        inverse = jnp.where(cell < GRID, inverse, 0.0)
        inv_ref[n, p, :, :] = inverse
        inverses.append(inverse)

    def norm_tile(index, carry):
        lanes = lane_tile(index)
        for inverse, mean, (n, p) in zip(inverses, means, cells):
            unit = (unit_ref[n, p, :, lanes] - mean) * inverse
            unit_ref[n, p, :, lanes] = unit
        return carry

    lax.fori_loop(0, tiles, norm_tile, 0)


def conv_norm(padded, taps, bias):
    count, _, _, channels = padded.shape
    whole = pl.BlockSpec(memory_space=pltpu.VMEM)
    full = jax.ShapeDtypeStruct(padded.shape, jnp.float32)
    return pl.pallas_call(
        conv_norm_kernel,
        out_shape=(
            full,
            jax.ShapeDtypeStruct((count, GRID, ROWS, LANES), jnp.float32),
        ),
        in_specs=[whole] * 3,
        out_specs=(whole, whole),
        compiler_params=pltpu.CompilerParams(vmem_limit_bytes=24 * 1024 * 1024),
    )(padded, taps, bias)


def conv_grad_kernel(x_ref, unit_ref, inv_ref, gain_ref, grad_ref, out_ref, work_ref):
    count = x_ref.shape[0]
    channels = x_ref.shape[3]
    tiles = channels // LANES
    reach = (GRID - 1) // 2
    taps = GRID * GRID
    cell = lax.broadcasted_iota(jnp.int32, (ROWS, LANES), 0)
    cells = [(n, p) for p in range(GRID) for n in range(count)]
    zero = jnp.zeros((ROWS, LANES), jnp.float32)

    def first_tile(index, carry):
        plain, crossed = carry
        lanes = lane_tile(index)
        gain = jnp.broadcast_to(gain_ref[:, lanes], (ROWS, LANES))
        gain_sum = zero
        out_ref[index, 48:TAP_ROWS, :] = jnp.zeros((TAP_ROWS - 48, LANES), jnp.float32)
        plain_out = []
        crossed_out = []
        for at, (n, p) in enumerate(cells):
            unit = unit_ref[n, p, :, lanes]
            grad = grad_ref[n, p, :, lanes]
            gain_sum = gain_sum + grad * unit
            scaled = grad * gain
            plain_out.append(plain[at] + scaled)
            crossed_out.append(crossed[at] + scaled * unit)
        out_ref[index, taps + 1 : taps + 2, :] = jnp.sum(gain_sum, axis=0, keepdims=True)
        return (tuple(plain_out), tuple(crossed_out))

    zeros = tuple(zero for _ in cells)
    plain, crossed = lax.fori_loop(0, tiles, first_tile, (zeros, zeros))
    for at, (n, p) in enumerate(cells):
        first = jnp.sum(plain[at], axis=1, keepdims=True) / channels
        second = jnp.sum(crossed[at], axis=1, keepdims=True) / channels
        work_ref[0, n, p, :, :] = jnp.broadcast_to(first, (ROWS, LANES))
        work_ref[1, n, p, :, :] = jnp.broadcast_to(second, (ROWS, LANES))

    def tap_tile(index, carry):
        lanes = lane_tile(index)
        gain = jnp.broadcast_to(gain_ref[:, lanes], (ROWS, LANES))
        grad_conv = {}
        bias_sum = zero
        for n, p in cells:
            value = inv_ref[n, p, :, :] * (
                grad_ref[n, p, :, lanes] * gain
                - work_ref[0, n, p, :, :]
                - unit_ref[n, p, :, lanes] * work_ref[1, n, p, :, :]
            )
            grad_conv[(n, p)] = value
            bias_sum = bias_sum + value
        out_ref[index, taps : taps + 1, :] = jnp.sum(bias_sum, axis=0, keepdims=True)
        for col_off in range(GRID):
            moved = shifted_rows(x_ref, lanes, col_off - reach, cell)
            for row_off in range(GRID):
                tap = row_off * GRID + col_off
                total = zero
                for p in range(GRID):
                    row = p + row_off - reach
                    if 0 <= row < GRID:
                        for n in range(count):
                            total = total + moved[row][n] * grad_conv[(n, p)]
                out_ref[index, tap : tap + 1, :] = jnp.sum(total, axis=0, keepdims=True)
        return carry

    lax.fori_loop(0, tiles, tap_tile, 0)


def conv_grads(padded, unit, inverse, gain, grad):
    count, _, _, channels = padded.shape
    whole = pl.BlockSpec(memory_space=pltpu.VMEM)
    return pl.pallas_call(
        conv_grad_kernel,
        out_shape=jax.ShapeDtypeStruct((channels // LANES, TAP_ROWS, LANES), jnp.float32),
        in_specs=[whole] * 5,
        out_specs=whole,
        scratch_shapes=[pltpu.VMEM((2, count, GRID, ROWS, LANES), jnp.float32)],
        compiler_params=pltpu.CompilerParams(vmem_limit_bytes=24 * 1024 * 1024),
    )(padded, unit, inverse, gain, grad)


def peer_copies(axis, count, source_of, target, send_sems, recv_sems):
    me = lax.axis_index(axis)
    copies = []
    for by in range(1, count):
        peer = lax.rem(me + by, count)
        copy = pltpu.make_async_remote_copy(
            src_ref=source_of(peer),
            dst_ref=target.at[me],
            send_sem=send_sems.at[by],
            recv_sem=recv_sems.at[by],
            device_id={axis: peer},
            device_id_type=pl.DeviceIdType.MESH,
        )
        copy.start()
        copies.append(copy)
    return copies


def wait_all(copies):
    for copy in copies:
        copy.wait()


def meet_peers(sizes):
    barrier = pltpu.get_barrier_semaphore()
    total = 0
    for axis, count in sizes:
        me = lax.axis_index(axis)
        for by in range(1, count):
            pl.semaphore_signal(
                barrier,
                inc=1,
                device_id={axis: lax.rem(me + by, count)},
                device_id_type=pl.DeviceIdType.MESH,
            )
        total += count - 1
    pl.semaphore_wait(barrier, total)


def head_kernel(
    dp, loop, part_ref, mean_ref, rest_ref, pooled_ref, rest_out_ref, parts, own, sems
):
    meet_peers((("dp", dp), ("loop", loop)))
    loop_me = lax.axis_index("loop")
    dp_me = lax.axis_index("dp")
    dp_copies = peer_copies(
        "dp", dp, lambda peer: part_ref, parts, sems.at[0], sems.at[1]
    )
    rest_copies = peer_copies(
        "loop", loop, lambda peer: rest_ref, rest_out_ref, sems.at[2], sems.at[3]
    )
    parts[dp_me] = part_ref[...]
    rest_out_ref[loop_me] = rest_ref[...]
    wait_all(dp_copies)
    total = parts[0]
    for at in range(1, dp):
        total = total + parts[at]
    own[...] = mean_ref[...] + total
    pooled_copies = peer_copies(
        "loop", loop, lambda peer: own, pooled_ref, sems.at[4], sems.at[5]
    )
    pooled_ref[loop_me] = own[...]
    wait_all(rest_copies)
    wait_all(pooled_copies)


def head_exchange(part, mean, rest):
    dp = lax.axis_size("dp")
    loop = lax.axis_size("loop")
    whole = pl.BlockSpec(memory_space=pltpu.VMEM)
    return pl.pallas_call(
        functools.partial(head_kernel, dp, loop),
        out_shape=(
            jax.ShapeDtypeStruct((loop,) + part.shape, jnp.float32),
            jax.ShapeDtypeStruct((loop,) + rest.shape, jnp.float32),
        ),
        in_specs=[whole] * 3,
        out_specs=(whole, whole),
        scratch_shapes=[
            pltpu.VMEM((dp,) + part.shape, jnp.float32),
            pltpu.VMEM(part.shape, jnp.float32),
            pltpu.SemaphoreType.DMA((6, max(dp, loop))),
        ],
        compiler_params=pltpu.CompilerParams(
            collective_id=0, has_side_effects=True, vmem_limit_bytes=16 * 1024 * 1024
        ),
    )(part, mean, rest)


def total_kernel(dp, loop, part_ref, out_ref, dp_slots, loop_slots, block, chunk, sems):
    meet_peers((("dp", dp), ("loop", loop)))
    loop_me = lax.axis_index("loop")
    dp_me = lax.axis_index("dp")
    copies = peer_copies(
        "dp", dp, lambda peer: part_ref.at[peer], dp_slots, sems.at[0], sems.at[1]
    )
    dp_slots[dp_me] = part_ref[dp_me]
    wait_all(copies)
    total = dp_slots[0]
    for at in range(1, dp):
        total = total + dp_slots[at]
    block[...] = total
    copies = peer_copies(
        "loop", loop, lambda peer: block.at[peer], loop_slots, sems.at[2], sems.at[3]
    )
    loop_slots[loop_me] = block[loop_me]
    wait_all(copies)
    total = loop_slots[0]
    for at in range(1, loop):
        total = total + loop_slots[at]
    chunk[...] = total
    mine = out_ref.at[dp_me]
    copies = peer_copies("loop", loop, lambda peer: chunk, mine, sems.at[4], sems.at[5])
    out_ref[dp_me, loop_me] = chunk[...]
    wait_all(copies)
    copies = peer_copies("dp", dp, lambda peer: mine, out_ref, sems.at[6], sems.at[7])
    wait_all(copies)


def total_sum(part):
    dp = lax.axis_size("dp")
    loop = lax.axis_size("loop")
    rows = part.shape[0] * part.shape[1] // (dp * loop)
    whole = pl.BlockSpec(memory_space=pltpu.VMEM)
    summed = pl.pallas_call(
        functools.partial(total_kernel, dp, loop),
        out_shape=jax.ShapeDtypeStruct((dp, loop, rows, LANES), jnp.float32),
        in_specs=[whole],
        out_specs=whole,
        scratch_shapes=[
            pltpu.VMEM((dp, loop, rows, LANES), jnp.float32),
            pltpu.VMEM((loop, rows, LANES), jnp.float32),
            pltpu.VMEM((loop, rows, LANES), jnp.float32),
            pltpu.VMEM((rows, LANES), jnp.float32),
            pltpu.SemaphoreType.DMA((8, max(dp, loop))),
        ],
        compiler_params=pltpu.CompilerParams(
            collective_id=1, has_side_effects=True, vmem_limit_bytes=32 * 1024 * 1024
        ),
    )(part.reshape(dp, loop, rows, LANES))
    return summed.reshape(part.shape)


def dense_rows(values):
    return values.reshape(-1, LANES)


def general_device(
    features,
    image_ids,
    text_embeds,
    text_ids,
    depth_kernel,
    depth_bias,
    norm_gain,
    w_up,
    w_down,
    projection,
    logit_scale,
    logit_bias,
):
    image_rows = features.shape[0]
    channels = features.shape[3]
    hidden_share = w_up.shape[1]
    cell_count = GRID * GRID
    loop_count = lax.axis_size("loop")
    position = lax.axis_index("loop")
    image_count = image_rows * loop_count
    text_rows = text_embeds.shape[0]
    first_image = position * image_rows
    gather = functools.partial(lax.all_gather, axis_name="loop", axis=0, tiled=True)

    text_unit, text_inverse = unit_rows(text_embeds.astype(jnp.float32))
    cell_mean = jnp.mean(features.astype(jnp.float32), axis=(1, 2))

    padded = jnp.pad(
        features.astype(jnp.float32), ((0, 0), (0, 0), (0, ROWS - GRID), (0, 0))
    )
    gain_row = norm_gain[None, :]
    unit, inverse = conv_norm(
        padded,
        depth_kernel.astype(jnp.float32).reshape(cell_count, channels),
        depth_bias[None, :],
    )
    padded_rows = image_rows * GRID * ROWS
    unit_rows_own = unit.reshape(padded_rows, channels)
    unit_share = lax.all_to_all(unit_rows_own, "loop", split_axis=1, concat_axis=0, tiled=True)
    normed_rows = (unit_rows_own * gain_row).astype(jnp.bfloat16)
    pre_act = jnp.dot(normed_rows, w_up, preferred_element_type=jnp.float32)
    hidden_sum = jnp.sum(
        gelu_value(pre_act).reshape(image_rows, GRID * ROWS, hidden_share), axis=1
    )
    slope = gelu_slope(pre_act)
    hidden_own = (hidden_sum / cell_count).astype(jnp.bfloat16)
    mlp_part = lax.dot_general(
        hidden_own, w_down, (((1,), (1,)), ((), ())), preferred_element_type=jnp.float32
    )
    id_row = jnp.pad(image_ids.astype(jnp.float32), (0, LANES - image_rows))[None, :]
    rest = jnp.concatenate([dense_rows(hidden_sum), dense_rows(text_unit), id_row], axis=0)
    hidden_rows = image_rows * hidden_share // LANES
    text_end = hidden_rows + text_unit.size // LANES
    rest = jnp.pad(rest, ((0, -rest.shape[0] % ROWS), (0, 0)))
    pooled_all, rest_all = head_exchange(dense_rows(mlp_part), dense_rows(cell_mean), rest)
    slope_sent, unit_share, pooled_all = lax.optimization_barrier((slope, unit_share, pooled_all))
    slope_all = gather(slope_sent)
    pooled = pooled_all.reshape(image_count, channels).astype(jnp.bfloat16)
    hidden_all = rest_all[:, :hidden_rows].reshape(image_count, hidden_share)
    hidden_all = (hidden_all / cell_count).astype(jnp.bfloat16)
    text_all = rest_all[:, hidden_rows:text_end].reshape(-1, text_embeds.shape[1])
    ids_all = rest_all[:, text_end, :image_rows].reshape(image_count).astype(jnp.int32)
    embedding = jnp.dot(pooled, projection, preferred_element_type=jnp.float32)
    image_unit, image_inverse = unit_rows(embedding)
    logits = (
        logit_scale[0] * jnp.dot(image_unit, text_all.T, precision=full_precision)
        + logit_bias[0]
    )
    labels = jnp.where(ids_all[:, None] == text_ids[None, :], 1.0, -1.0).astype(jnp.float32)
    loss_all = -jnp.sum(jax.nn.log_sigmoid(labels * logits), axis=1)
    row_loss = lax.dynamic_slice_in_dim(loss_all, first_image, image_rows)
    coeffs = -logit_scale[0] * labels * jax.nn.sigmoid(-labels * logits)
    grad_image = jnp.dot(coeffs, text_all, precision=full_precision)
    own_coeffs = lax.dynamic_slice_in_dim(coeffs, position * text_rows, text_rows, 1)
    grad_text = jnp.dot(own_coeffs.T, image_unit, precision=full_precision)
    grad_texts = text_inverse * (
        grad_text - text_unit * jnp.sum(text_unit * grad_text, axis=1, keepdims=True)
    )
    grad_embed = (
        image_inverse
        * (grad_image - image_unit * jnp.sum(image_unit * grad_image, axis=1, keepdims=True))
    ).astype(jnp.bfloat16)
    grad_pooled = lax.dot_general(
        grad_embed, projection, (((1,), (1,)), ((), ())), preferred_element_type=jnp.float32
    ).astype(jnp.bfloat16)
    spread = jnp.dot(grad_pooled, w_down, preferred_element_type=jnp.float32) / cell_count
    own_spread = lax.dynamic_slice_in_dim(spread, first_image, image_rows)
    grad_pre = (
        (slope.reshape(image_rows, GRID * ROWS, hidden_share) * own_spread[:, None, :])
        .reshape(padded_rows, hidden_share)
        .astype(jnp.bfloat16)
    )
    grad_normed = lax.dot_general(
        grad_pre, w_up, (((1,), (1,)), ((), ())), preferred_element_type=jnp.float32
    ).reshape(padded.shape)
    part = conv_grads(padded, unit, inverse, gain_row, grad_normed)
    total = total_sum(part).transpose(1, 0, 2).reshape(TAP_ROWS, channels)
    grad_kernel = total[:cell_count].reshape(GRID, GRID, channels)
    grad_bias = total[cell_count]
    grad_gain = total[cell_count + 1]

    up_share = channels // loop_count
    grad_pooled_share = lax.dynamic_slice_in_dim(grad_pooled, position * up_share, up_share, 1)
    grad_down = lax.dot_general(
        grad_pooled_share, hidden_all, (((0,), (0,)), ((), ())), preferred_element_type=jnp.float32
    )
    proj_share = up_share // lax.axis_size("dp")
    proj_at = (lax.axis_index("dp") * loop_count + position) * proj_share
    pooled_share = lax.dynamic_slice_in_dim(pooled, proj_at, proj_share, 1)
    grad_proj = lax.dot_general(
        pooled_share, grad_embed, (((0,), (0,)), ((), ())), preferred_element_type=jnp.float32
    )
    grad_pre_all = (
        (slope_all.reshape(image_count, GRID * ROWS, hidden_share) * spread[:, None, :])
        .reshape(loop_count * padded_rows, hidden_share)
        .astype(jnp.bfloat16)
    )
    gain_share = lax.dynamic_slice_in_dim(norm_gain, position * up_share, up_share)
    normed_share = (unit_share * gain_share).astype(jnp.bfloat16)
    grad_up = lax.dot_general(
        normed_share,
        grad_pre_all,
        (((0,), (0,)), ((), ())),
        preferred_element_type=jnp.float32,
    )
    return (row_loss, grad_texts, grad_kernel, grad_bias, grad_gain, grad_up, grad_down, grad_proj)


SPLIT = 96
SIDE = 4
CORES = 2
PACKET = 2304
PART_ROWS = 56
MESH = pl.DeviceIdType.MESH
nn = (((1,), (0,)), ((), ()))
nt = (((1,), (1,)), ((), ()))
tn = (((0,), (0,)), ((), ()))


def product(left, right, dims, precision=None):
    return lax.dot_general(
        left, right, dims, preferred_element_type=jnp.float32, precision=precision
    )


def flipped(index, by):
    if by == 1:
        return index + 1 - 2 * lax.rem(index, 2)
    if by == 2:
        return lax.rem(index + 2, SIDE)
    return SIDE - 1 - index


def columns(start, size):
    return pl.ds(pl.multiple_of(start, LANES), size)


def rounded(values):
    return values.astype(jnp.bfloat16).astype(jnp.float32)


def image_of(first, shape, values):
    cells = GRID * GRID
    row = first + lax.broadcasted_iota(jnp.int32, shape, 0)
    out = jnp.broadcast_to(values[-1], shape)
    for n in reversed(range(len(values) - 1)):
        out = jnp.where(row < (n + 1) * cells, values[n], out)
    return jnp.where(row < len(values) * cells, out, 0.0)


def fused_kernel(
    xb,
    kb,
    wu_hbm,
    wd_hbm,
    pj_hbm,
    bias_ref,
    gain_ref,
    text_ref,
    iid_ref,
    tid_ref,
    scale_ref,
    shift_ref,
    o_loss,
    *refs,
):
    (
        o_text,
        o_kernel,
        o_bias,
        o_gain,
        o_up,
        o_down,
        o_proj,
        wu,
        wd,
        pj,
        x,
        kf,
        unit,
        inv,
        nf,
        nb,
        stats,
        stats_out,
        stats_in,
        pre,
        sl,
        gn,
        full,
        thin,
        far,
        nrow,
        gpre,
        fullb,
        packed,
        packets,
        texts_out,
        texts_in,
        texts,
        part_out,
        part_in,
        means,
        small,
        heads,
        gathered,
        work,
        taps_out,
        taps_in,
        taps_sum,
        taps_z,
        taps_all,
        up_out,
        up_in,
        local_sem,
        send_sem,
        recv_sem,
    ) = refs
    count, _, _, channels = xb.shape
    hidden = wu.shape[1]
    width = pj.shape[1]
    split = full.shape[1]
    total_rows = nf.shape[0]
    sent_rows = count * GRID * GRID
    sent_rows += -sent_rows % ROWS
    rest_rows = sent_rows - split
    tiles = channels // LANES
    reach = (GRID - 1) // 2
    taps = GRID * GRID
    chip = channels // SIDE
    half = hidden // 2
    dp = lax.axis_index("dp")
    loop = lax.axis_index("loop")
    z = loop // CORES
    core = lax.rem(loop, CORES)
    rank = dp * CORES + core
    planes = SIDE * CORES
    next_sem = [0]

    def take(number):
        first = next_sem[0]
        next_sem[0] += number
        return first

    def remote(src, dst, device, sem, sent=None):
        return pltpu.make_async_remote_copy(
            src_ref=src,
            dst_ref=dst,
            send_sem=send_sem.at[sem if sent is None else sent],
            recv_sem=recv_sem.at[sem],
            device_id=device,
            device_id_type=MESH,
        )

    def at_z(index):
        return {"dp": dp, "loop": index * CORES + core}

    def at_dp(index):
        return {"dp": index, "loop": loop}

    def at_rank(index):
        return {"dp": index // CORES, "loop": z * CORES + lax.rem(index, CORES)}

    partner = {"dp": dp, "loop": z * CORES + 1 - core}

    barrier = pltpu.get_barrier_semaphore()
    met = 0
    for by in range(1, planes):
        pl.semaphore_signal(
            barrier, inc=1, device_id={"dp": dp, "loop": lax.rem(loop + by, planes)}, device_id_type=MESH
        )
        met += 1
    for by in range(1, SIDE):
        for other in range(CORES):
            pl.semaphore_signal(
                barrier,
                inc=1,
                device_id={"dp": flipped(dp, by), "loop": z * CORES + other},
                device_id_type=MESH,
            )
            met += 1
    loads = []
    for at, (far_ref, near_ref) in enumerate(((wu_hbm, wu), (wd_hbm, wd), (pj_hbm, pj))):
        copy = pltpu.make_async_copy(far_ref, near_ref, local_sem.at[at])
        copy.start()
        loads.append(copy)

    text = text_ref[...].astype(jnp.float32)
    text_unit, text_inverse = unit_rows(text)
    third = width // 3
    texts_out[...] = jnp.zeros(texts_out.shape, jnp.float32)
    for k in range(3):
        texts_out[2 * k : 2 * k + 2, :] = text_unit[:, k * third : (k + 1) * third]

    cell = lax.broadcasted_iota(jnp.int32, (ROWS, LANES), 0)
    zero = jnp.zeros((ROWS, LANES), jnp.float32)
    cells = [(n, p) for n in range(count) for p in range(GRID)]

    edge = total_rows - 2 * ROWS
    nf[edge:total_rows, :] = jnp.zeros((2 * ROWS, channels), jnp.float32)

    def conv_tile(i, sums):
        lanes = lane_tile(lax.rem(dp * (tiles // SIDE) + i, tiles))
        for n, p in cells:
            x[n, p, 0:GRID, lanes] = xb[n, p, :, lanes].astype(jnp.float32)
            x[n, p, GRID:ROWS, lanes] = jnp.zeros((ROWS - GRID, LANES), jnp.float32)
        for a in range(GRID):
            kf[a * GRID : (a + 1) * GRID, lanes] = kb[a, :, lanes].astype(jnp.float32)
        bias = jnp.broadcast_to(bias_ref[:, lanes], (ROWS, LANES))
        out = {at: bias for at in cells}
        for col_off in range(GRID):
            moved = shifted_rows(x, lanes, col_off - reach, cell)
            for row_off in range(GRID):
                tap = row_off * GRID + col_off
                weight = jnp.broadcast_to(kf[tap : tap + 1, lanes], (ROWS, LANES))
                for p in range(GRID):
                    row = p + row_off - reach
                    if 0 <= row < GRID:
                        for n in range(count):
                            out[(n, p)] = out[(n, p)] + moved[row][n] * weight
        for n, p in cells:
            unit[n, p, :, lanes] = out[(n, p)]
            first = n * taps + p * GRID
            nf[first : first + ROWS, lanes] = out[(n, p)]
        return tuple(total + out[at] for total, at in zip(sums, cells))

    zeros = tuple(zero for _ in cells)
    early = tiles // SIDE
    sums = lax.fori_loop(0, early, conv_tile, zeros)

    pl.semaphore_wait(barrier, met)
    text_sem = take(planes)
    text_copies = []
    for by in range(1, planes):
        peer = {"dp": dp, "loop": lax.rem(loop + by, planes)}
        copy = remote(texts_out, texts_in.at[loop], peer, text_sem + by)
        copy.start()
        text_copies.append(copy)

    quarter = channels // SIDE
    slim = chip // SIDE
    own_quarter = columns(dp * quarter, quarter)
    own_slim = columns(dp * slim, slim)
    full_sem = take(SIDE)
    thin_sem = take(SIDE)
    far_sem = take(SIDE)
    relay_sem = take(2)
    inner = z * (SIDE - 1 - z) > 0
    full_copies = {}
    thin_copies = {}
    far_copies = {}
    for by in range(1, SIDE):
        peer = flipped(z, by)
        full_copies[by] = remote(
            nf.at[pl.ds(0, split), own_quarter],
            full.at[z, :, own_quarter],
            at_z(peer),
            full_sem + by,
        )
        thin_copies[by] = remote(
            nf.at[pl.ds(split, rest_rows), columns(peer * chip + dp * slim, slim)],
            thin.at[z, pl.ds(0, rest_rows), own_slim],
            at_z(peer),
            thin_sem + by,
        )
        far_copies[by] = remote(
            sl.at[pl.ds(split, rest_rows), :],
            far.at[z, pl.ds(0, rest_rows), :],
            at_z(peer),
            far_sem + by,
        )
    two_away = flipped(z, 2)
    full_relay = remote(
        full.at[two_away, :, own_quarter],
        full.at[two_away, :, own_quarter],
        at_z(flipped(z, 1)),
        full_sem + 3,
        relay_sem,
    )
    far_relay = remote(
        far.at[two_away, pl.ds(0, rest_rows), :],
        far.at[two_away, pl.ds(0, rest_rows), :],
        at_z(flipped(z, 1)),
        far_sem + 3,
        relay_sem + 1,
    )

    def when_inner(*actions):
        @pl.when(inner)
        def _():
            for action in actions:
                action()

    full_copies[1].start()
    full_copies[2].start()
    when_inner(full_copies[3].start)

    sums = lax.fori_loop(early, tiles, conv_tile, sums)
    for by in range(1, SIDE):
        thin_copies[by].start()
    centers = [jnp.sum(total, axis=1, keepdims=True) / channels for total in sums]
    centers = [jnp.broadcast_to(mean, (ROWS, LANES)) for mean in centers]

    def square_tile(index, sums):
        lanes = lane_tile(index)
        result = []
        for total, mean, (n, p) in zip(sums, centers, cells):
            centered = unit[n, p, :, lanes] - mean
            result.append(total + centered * centered)
        return tuple(result)

    squares = lax.fori_loop(0, tiles, square_tile, zeros)

    inverses = []
    for total, (n, p) in zip(squares, cells):
        variance = jnp.sum(total, axis=1, keepdims=True) / channels
        inverse = jnp.broadcast_to(lax.rsqrt(variance + 1e-06), (ROWS, LANES))
        inverse = jnp.where(cell < GRID, inverse, 0.0)
        inv[n, p, :, :] = inverse
        inverses.append(inverse)
    lane_at = lax.broadcasted_iota(jnp.int32, (ROWS, LANES), 1)
    side_by_side = lane_at < LANES // 2
    stats[edge:total_rows, :] = jnp.zeros((2 * ROWS, LANES), jnp.float32)
    for inverse, mean, (n, p) in zip(inverses, centers, cells):
        first = n * taps + p * GRID
        stats[first : first + ROWS, :] = jnp.where(side_by_side, mean, inverse)
    total = zero
    for k in range(total_rows // ROWS):
        values = stats[k * ROWS : (k + 1) * ROWS, :]
        total = total + jnp.where(lax.rem(lane_at, LANES // 2) == k, values, 0.0)
    stats_out[...] = total
    stats_sem = take(SIDE)
    stats_copies = {}
    for by in range(1, SIDE):
        copy = remote(stats_out, stats_in.at[z], at_z(flipped(z, by)), stats_sem + by)
        copy.start()
        stats_copies[by] = copy

    gn[edge:total_rows, :] = jnp.zeros((2 * ROWS, channels), jnp.float32)

    def norm_tile(index, carry):
        lanes = lane_tile(index)
        gain = jnp.broadcast_to(gain_ref[:, lanes], (ROWS, LANES))
        for inverse, mean, (n, p) in zip(inverses, centers, cells):
            value = (unit[n, p, :, lanes] - mean) * inverse
            unit[n, p, :, lanes] = value
            first = n * taps + p * GRID
            gn[first : first + ROWS, lanes] = value * gain
        return carry

    lax.fori_loop(0, tiles, norm_tile, 0)

    def narrow(i, carry):
        rows = pl.ds(pl.multiple_of(i * 2 * ROWS, 2 * ROWS), 2 * ROWS)
        nb[rows, :] = gn[rows, :].astype(jnp.bfloat16)
        return carry

    lax.fori_loop(0, total_rows // (2 * ROWS), narrow, 0)

    loads[0].wait()
    strip = 2 * LANES

    def expand(rows_ref, rows):
        def step(j, carry):
            lanes = pl.ds(pl.multiple_of(j * strip, strip), strip)
            pre[0:rows, lanes] = product(rows_ref[0:rows, :], wu[:, lanes], nn)
            return carry

        lax.fori_loop(0, hidden // strip, step, 0)

    expand(nb, total_rows)

    def activate(i, carry):
        rows = pl.ds(pl.multiple_of((i // 2) * 2 * ROWS, 2 * ROWS), 2 * ROWS)
        lanes = pl.ds(pl.multiple_of(lax.rem(i, 2) * half, LANES), half)
        values = pre[rows, lanes]
        cumulative = 0.5 * (1.0 + lax.erf(values * half_root))
        sl[rows, lanes] = cumulative + values * jnp.exp(-0.5 * values * values) * density_factor
        pre[rows, lanes] = values * cumulative
        return carry

    lax.fori_loop(0, total_rows // ROWS, activate, 0)

    far_copies[1].start()

    row_wide = lax.broadcasted_iota(jnp.int32, (ROWS, hidden), 0)
    heads[...] = jnp.zeros(heads.shape, jnp.float32)
    for n in range(count):
        begin, end = n * taps, (n + 1) * taps
        total = jnp.zeros((ROWS, hidden), jnp.float32)
        for tile in range(begin // ROWS, -(-end // ROWS)):
            values = pre[tile * ROWS : (tile + 1) * ROWS, :]
            if tile * ROWS < begin:
                values = jnp.where(row_wide >= begin - tile * ROWS, values, 0.0)
            if (tile + 1) * ROWS > end:
                values = jnp.where(row_wide < end - tile * ROWS, values, 0.0)
            total = total + values
        mean = jnp.sum(total, axis=0, keepdims=True) / taps
        heads[n : n + 1, 0:hidden] = rounded(mean)

    loads[1].wait()
    mlp = product(heads[:, 0:hidden].astype(jnp.bfloat16), wd[...], nt)
    part_out[...] = jnp.zeros(part_out.shape, jnp.float32)
    part_out[0:count, :] = mlp[0:count, 0:hidden]
    part_out[count : 2 * count, :] = mlp[0:count, hidden : 2 * hidden]
    part_sem = take(SIDE)
    part_copies = []
    for by in range(1, SIDE):
        copy = remote(part_out, part_in.at[dp], at_dp(flipped(dp, by)), part_sem + by)
        copy.start()
        part_copies.append(copy)
    first_sem = take(3 * SIDE)
    second_sem = take(3 * SIDE)
    slim_sem = take(SIDE * SIDE)
    half_quarter = quarter // 2
    first_hop = {}
    second_hop = {}
    slim_hop = {}

    def hop_one(by):
        peer = flipped(z, by)
        if by == 3:
            full_copies[3].wait_recv()
            when_inner(full_copies[3].wait_send, full_relay.wait_send)
        else:
            full_copies[by].wait()
        if by == 2:
            when_inner(full_relay.start)
        thin_copies[by].wait()
        block = full.at[peer, :, own_quarter]
        first_hop[by] = []
        for to in (1, 2):
            copy = remote(block, block, at_dp(flipped(dp, to)), first_sem + 3 * by + to)
            copy.start()
            first_hop[by].append(copy)
        piece = thin.at[peer, pl.ds(0, rest_rows), own_slim]
        slim_hop[by] = []
        for to in range(1, SIDE):
            copy = remote(piece, piece, at_dp(flipped(dp, to)), slim_sem + SIDE * by + to)
            copy.start()
            slim_hop[by].append(copy)

    def hop_two(by):
        peer = flipped(z, by)
        second_hop[by] = []
        for to in (1, 2):
            first_hop[by][to - 1].wait_recv()
            source = flipped(dp, to)
            block = full.at[peer, :, columns(source * quarter + (to - 1) * half_quarter, half_quarter)]
            copy = remote(block, block, at_dp(flipped(dp, 3 - to)), second_sem + 3 * by + to)
            copy.start()
            second_hop[by].append(copy)

    def arrived(by):
        for copy in second_hop[by]:
            copy.wait()
        for copy in first_hop[by]:
            copy.wait_send()
        for copy in slim_hop[by]:
            copy.wait()
        if by == 3:
            far_copies[3].wait_recv()
            when_inner(far_copies[3].wait_send, far_relay.wait_send)
        elif by == 1:
            far_copies[1].wait()

    hop_one(1)
    part_in[dp] = part_out[...]
    means[...] = jnp.zeros(means.shape, jnp.float32)
    for n in range(count):
        total = x[n, 0]
        for p in range(1, GRID):
            total = total + x[n, p]
        mean = jnp.sum(total, axis=0, keepdims=True) / taps
        means[n : n + 1, :] = mean[:, 0:hidden]
        means[count + n : count + n + 1, :] = mean[:, hidden : 2 * hidden]
    for copy in text_copies:
        copy.wait()
    texts_in[loop] = texts_out[...]
    for l in range(planes):
        for k in range(3):
            texts[2 * l : 2 * l + 2, k * third : (k + 1) * third] = texts_in[l, 2 * k : 2 * k + 2, :]
    loads[2].wait()
    small[...] = jnp.zeros(small.shape, jnp.float32)
    for copy in part_copies:
        copy.wait()
    total = part_in[0]
    for at in range(1, SIDE):
        total = total + part_in[at]
    pooled = rounded(means[...] + total)
    small[0:count, 0:hidden] = pooled[0:count, :]
    small[0:count, hidden : 2 * hidden] = pooled[count : 2 * count, :]

    embedding = product(small[...].astype(jnp.bfloat16), pj[...], nn)[0:ROWS, :]
    image_unit, image_inverse = unit_rows(embedding)
    all_texts = texts[...]
    text_count = all_texts.shape[0]
    scale = scale_ref[...]
    logits = scale * product(image_unit, all_texts, nt, full_precision) + shift_ref[...]
    ids = jnp.broadcast_to(iid_ref[...].astype(jnp.float32), (ROWS, count))
    spot_row = lax.broadcasted_iota(jnp.int32, (ROWS, count), 0)
    spot_col = lax.broadcasted_iota(jnp.int32, (ROWS, count), 1)
    own_ids = jnp.sum(jnp.where(spot_row == spot_col, ids, 0.0), axis=1, keepdims=True)
    same = jnp.broadcast_to(own_ids, (ROWS, text_count)) == jnp.broadcast_to(
        tid_ref[...].astype(jnp.float32), (ROWS, text_count)
    )
    labels = jnp.where(same, 1.0, -1.0)
    signed = labels * logits
    losses = jnp.log1p(jnp.exp(-jnp.abs(signed))) - jnp.minimum(signed, 0.0)
    loss = jnp.broadcast_to(jnp.sum(losses, axis=1, keepdims=True), (ROWS, LANES))
    o_loss[...] = jnp.sum(jnp.where(cell == lane_at, loss, 0.0), axis=0, keepdims=True)
    coeffs = -scale * labels * lax.logistic(-signed)
    grad_image = product(coeffs, all_texts, nn, full_precision)
    own_row = lax.broadcasted_iota(jnp.int32, (ROWS, width), 0)
    grad_embed = image_inverse * (
        grad_image - image_unit * jnp.sum(image_unit * grad_image, axis=1, keepdims=True)
    )
    grad_embed = jnp.where(own_row < count, rounded(grad_embed), 0.0)
    grad_text = product(coeffs, image_unit, tn, full_precision)
    heads[0:ROWS, hidden : hidden + width] = grad_embed
    grad_pooled = product(heads[:, hidden : hidden + width].astype(jnp.bfloat16), pj[...], nt)
    grad_pooled = grad_pooled.astype(jnp.bfloat16)
    spread = product(grad_pooled, wd[...], nn) / taps
    grad_pooled = grad_pooled.astype(jnp.float32)

    for at in range(SIDE):
        packed[at, 0:count, 0:chip] = grad_pooled[0:count, at * chip : (at + 1) * chip]
        packed[at, 0:count, chip : chip + LANES] = small[
            0:count, columns(dp * quarter + at * LANES, LANES)
        ]
        packed[at, 0:count, chip + LANES : chip + LANES + width] = grad_embed[0:count, :]
        packed[at, count : 2 * count, 0:hidden] = heads[0:count, 0:hidden]
        packed[at, count : 2 * count, hidden : 2 * hidden] = spread[0:count, :]
        packed[at, 6:8, 0:width] = grad_text[4 * at : 4 * at + 2, :]
        packed[at, 6:8, width : 2 * width] = grad_text[4 * at + 2 : 4 * at + 4, :]
    packet_sem = take(SIDE)
    packet_copies = {}
    for by in range(1, SIDE):
        peer = flipped(z, by)
        copy = remote(packed.at[peer], packets.at[core, z], at_z(peer), packet_sem + by)
        copy.start()
        packet_copies[by] = copy
    packets[core, z] = packed[z]
    far_copies[2].start()
    when_inner(far_copies[3].start)


    spreads = [spread[n : n + 1, :] for n in range(count)]

    def own_slopes(i, carry):
        first = pl.multiple_of(i * 2 * ROWS, 2 * ROWS)
        rows = pl.ds(first, 2 * ROWS)
        for lanes in (slice(0, half), slice(half, hidden)):
            scaled = image_of(first, (2 * ROWS, half), [s[:, lanes] for s in spreads])
            gpre[rows, lanes] = (sl[rows, lanes] * scaled).astype(jnp.bfloat16)
        return carry

    lax.fori_loop(0, total_rows // (2 * ROWS), own_slopes, 0)
    hop_one(2)
    hop_two(1)

    def contract(j, carry):
        lanes = pl.ds(pl.multiple_of(j * strip, strip), strip)
        gn[:, lanes] = product(gpre[0:total_rows, :], wu[lanes, :], nt)
        return carry

    lax.fori_loop(0, channels // strip, contract, 0)
    own_chip = columns(z * chip, chip)
    nrow[0:total_rows, :] = nb[:, own_chip]

    def first_tile(index, carry):
        plain, crossed = carry
        lanes = lane_tile(index)
        gain = jnp.broadcast_to(gain_ref[:, lanes], (ROWS, LANES))
        gain_sum = zero
        taps_out[index, 48:PART_ROWS, :] = jnp.zeros((PART_ROWS - 48, LANES), jnp.float32)
        plain_out = []
        crossed_out = []
        for at, (n, p) in enumerate(cells):
            first = n * taps + p * GRID
            value = unit[n, p, :, lanes]
            grad = gn[first : first + ROWS, lanes]
            gain_sum = gain_sum + grad * value
            scaled = grad * gain
            plain_out.append(plain[at] + scaled)
            crossed_out.append(crossed[at] + scaled * value)
        taps_out[index, taps + 1 : taps + 2, :] = jnp.sum(gain_sum, axis=0, keepdims=True)
        return (tuple(plain_out), tuple(crossed_out))

    plain, crossed = lax.fori_loop(0, tiles, first_tile, (zeros, zeros))
    for at, (n, p) in enumerate(cells):
        first = jnp.sum(plain[at], axis=1, keepdims=True) / channels
        second = jnp.sum(crossed[at], axis=1, keepdims=True) / channels
        work[0, n, p, :, :] = jnp.broadcast_to(first, (ROWS, LANES))
        work[1, n, p, :, :] = jnp.broadcast_to(second, (ROWS, LANES))

    own_tiles = tiles // planes
    sent_tiles = tiles - own_tiles
    taps_sem = take(sent_tiles)

    def taps_copy(i):
        owner = lax.rem(rank + 1 + i // own_tiles, planes)
        return remote(
            taps_out.at[owner * own_tiles + lax.rem(i, own_tiles)],
            taps_in.at[rank, lax.rem(i, own_tiles)],
            at_rank(owner),
            taps_sem + i,
        )

    def tap_tile(i, carry):
        index = lax.rem(rank * own_tiles + own_tiles + i, tiles)
        lanes = lane_tile(index)
        gain = jnp.broadcast_to(gain_ref[:, lanes], (ROWS, LANES))
        grad_conv = {}
        bias_sum = zero
        for n, p in cells:
            first = n * taps + p * GRID
            value = inv[n, p, :, :] * (
                gn[first : first + ROWS, lanes] * gain
                - work[0, n, p, :, :]
                - unit[n, p, :, lanes] * work[1, n, p, :, :]
            )
            grad_conv[(n, p)] = value
            bias_sum = bias_sum + value
        taps_out[index, taps : taps + 1, :] = jnp.sum(bias_sum, axis=0, keepdims=True)
        for col_off in range(GRID):
            moved = shifted_rows(x, lanes, col_off - reach, cell)
            for row_off in range(GRID):
                tap = row_off * GRID + col_off
                total = zero
                for p in range(GRID):
                    row = p + row_off - reach
                    if 0 <= row < GRID:
                        for n in range(count):
                            total = total + moved[row][n] * grad_conv[(n, p)]
                taps_out[index, tap : tap + 1, :] = jnp.sum(total, axis=0, keepdims=True)

        @pl.when(i < sent_tiles)
        def _():
            taps_copy(i).start()

        return carry

    lax.fori_loop(0, tiles // 2, tap_tile, 0)
    hop_two(2)
    lax.fori_loop(tiles // 2, tiles, tap_tile, 0)
    hop_one(3)

    for by in range(1, SIDE):
        packet_copies[by].wait()
    cross_sem = take(1)
    cross = remote(packets.at[core], packets.at[core], partner, cross_sem)
    cross.start()

    def other_rows(by):
        peer = flipped(z, by)
        base = by * total_rows
        arrived(by)
        stats_copies[by].wait()
        scales = stats_in[peer]

        def spot(k):
            return jnp.sum(jnp.where(lane_at == k, scales, 0.0), axis=1, keepdims=True)

        def normed(values, k, gain):
            parts = []
            for at in range(2):
                part = values[at * ROWS : (at + 1) * ROWS, :] - spot(k + at)
                parts.append(part * spot(k + at + LANES // 2) * gain)
            return jnp.concatenate(parts, axis=0)

        def cast(i, carry):
            first = pl.multiple_of(i * 2 * ROWS, 2 * ROWS)
            rows = pl.ds(first, 2 * ROWS)
            fullb[rows, :] = normed(full[peer, rows, :], 2 * i, gain_ref[...]).astype(jnp.bfloat16)
            nrow[pl.ds(base + first, 2 * ROWS), :] = fullb[rows, own_chip]
            return carry

        lax.fori_loop(0, split // (2 * ROWS), cast, 0)
        expand(fullb, split)
        spreads = [
            packets[core, peer, count + n : count + n + 1, hidden : 2 * hidden] for n in range(count)
        ]

        def slopes(i, carry):
            first = pl.multiple_of(i * 2 * ROWS, 2 * ROWS)
            for lanes in (slice(0, half), slice(half, hidden)):
                scaled = image_of(first, (2 * ROWS, half), [s[:, lanes] for s in spreads])
                values = gelu_slope(pre[pl.ds(first, 2 * ROWS), lanes]) * scaled
                gpre[pl.ds(base + first, 2 * ROWS), lanes] = values.astype(jnp.bfloat16)
            return carry

        lax.fori_loop(0, split // (2 * ROWS), slopes, 0)
        for i in range((total_rows - split) // (2 * ROWS)):
            first = i * 2 * ROWS
            at = split + first
            rows = slice(first, first + 2 * ROWS)
            keep = lax.broadcasted_iota(jnp.int32, (2 * ROWS, chip), 0) + at < count * taps
            values = normed(thin[peer, rows, :], at // ROWS, gain_ref[:, own_chip])
            values = jnp.where(keep, values, 0.0)
            nrow[base + at : base + at + 2 * ROWS, :] = values.astype(jnp.bfloat16)
            for lanes in (slice(0, half), slice(half, hidden)):
                keep = lax.broadcasted_iota(jnp.int32, (2 * ROWS, half), 0) + at < count * taps
                scaled = image_of(at, (2 * ROWS, half), [s[:, lanes] for s in spreads])
                values = jnp.where(keep, far[peer, rows, lanes] * scaled, 0.0)
                gpre[base + at : base + at + 2 * ROWS, lanes] = values.astype(jnp.bfloat16)

    other_rows(1)

    def taps_wait(i, carry):
        taps_copy(i).wait()
        return carry

    lax.fori_loop(0, sent_tiles, taps_wait, 0)
    for k in range(own_tiles):
        total = taps_out[rank * own_tiles + k]
        for by in range(1, planes):
            total = total + taps_in[lax.rem(rank + by, planes), k]
        taps_sum[k] = total
    along_sem = take(SIDE)
    along_copies = []
    for by in range(1, SIDE):
        copy = remote(taps_sum, taps_z.at[z], at_z(flipped(z, by)), along_sem + by)
        copy.start()
        along_copies.append(copy)
    taps_z[z] = taps_sum[...]

    cross.wait()

    def collect(lanes, shift, first_lane):
        for other in range(CORES):
            for at in range(SIDE):
                values = packets[other, at, :, lanes]
                if shift:
                    values = pltpu.roll(values, ROWS - shift, 0)
                keep = lax.broadcasted_iota(jnp.int32, values.shape, 0) < count
                first = (other * SIDE + at) * ROWS
                gathered[first : first + ROWS, first_lane : first_lane + values.shape[1]] = jnp.where(
                    keep, values, 0.0
                )

    share = chip // CORES
    collect(columns(core * share, share), 0, 0)
    collect(slice(chip, chip + LANES + width), 0, share)
    collect(slice(0, hidden), count, share + LANES + width)
    end = share + LANES + width
    o_down[...] = product(
        gathered[:, 0:share].astype(jnp.bfloat16), gathered[:, end : end + hidden].astype(jnp.bfloat16), tn
    )
    proj_two = product(
        gathered[:, share : share + LANES].astype(jnp.bfloat16),
        gathered[:, share + LANES : end].astype(jnp.bfloat16),
        tn,
    )
    proj_rows = LANES // CORES
    gn[0:LANES, 0:width] = proj_two
    o_proj[...] = gn[pl.ds(pl.multiple_of(core * proj_rows, proj_rows), proj_rows), 0:width]
    total = jnp.zeros((ROWS, width), jnp.float32)
    for at in range(SIDE):
        for other in range(CORES):
            total = total + packets[other, at, :, columns(core * width, width)]
    grad_text = total[6:8, :]
    o_text[...] = text_inverse * (
        grad_text - text_unit * jnp.sum(text_unit * grad_text, axis=1, keepdims=True)
    )


    far_copies[2].wait()
    when_inner(far_relay.start)
    hop_two(3)

    for copy in along_copies:
        copy.wait()
    for k in range(own_tiles):
        total = taps_z[0, k]
        for at in range(1, SIDE):
            total = total + taps_z[at, k]
        taps_all[rank * own_tiles + k] = total
    spread_sem = take(2 * SIDE)

    def tiles_of(index):
        return taps_all.at[pl.ds(index * own_tiles, own_tiles)]

    mine = tiles_of(rank)
    spread_copies = [remote(mine, mine, partner, spread_sem)]
    for by in range(1, SIDE):
        spread_copies.append(remote(mine, mine, at_dp(flipped(dp, by)), spread_sem + by))
    for copy in spread_copies:
        copy.start()

    other_rows(2)
    other_rows(3)

    def up_strip(rows_at, j):
        lanes = pl.ds(pl.multiple_of(j * strip, strip), strip)
        return lanes, product(nrow[:, rows_at], gpre[:, lanes], tn)

    theirs = columns((1 - core) * share, share)
    ours = columns(core * share, share)
    steps = hidden // strip
    up_sem = take(steps)

    def up_copy(j):
        return remote(up_out.at[j], up_in.at[j], partner, up_sem + j)

    def up_send(j, carry):
        lanes, values = up_strip(theirs, j)
        up_out[j] = values
        up_copy(j).start()
        return carry

    lax.fori_loop(0, steps, up_send, 0)
    share_copies = []
    for by in range(1, SIDE):
        spread_copies[by].wait()
        theirs_at = flipped(dp, by) * CORES + core
        copy = remote(tiles_of(theirs_at), tiles_of(theirs_at), partner, spread_sem + SIDE + by)
        copy.start()
        share_copies.append(copy)

    def up_own(j, carry):
        lanes, values = up_strip(ours, j)
        o_up[:, lanes] = values
        return carry

    lax.fori_loop(0, steps, up_own, 0)

    spread_copies[0].wait()
    for copy in share_copies:
        copy.wait()
    for index in range(tiles):
        lanes = slice(index * LANES, (index + 1) * LANES)
        for a in range(GRID):
            o_kernel[a, :, lanes] = taps_all[index, a * GRID : (a + 1) * GRID, :]
        o_bias[:, lanes] = taps_all[index, taps : taps + 1, :]
        o_gain[:, lanes] = taps_all[index, taps + 1 : taps + 2, :]


    def up_add(j, carry):
        lanes = pl.ds(pl.multiple_of(j * strip, strip), strip)
        up_copy(j).wait()
        o_up[:, lanes] = o_up[:, lanes] + up_in[j]
        return carry

    lax.fori_loop(0, steps, up_add, 0)


def deliver_kernel(loss, *refs):
    number = (len(refs) - 2) // 2
    held, out_loss, placed, sems = refs[:number], refs[number], refs[number + 1 : -1], refs[-1]
    copies = []
    for at in range(number):
        copy = pltpu.make_async_copy(held[at], placed[at], sems.at[at])
        copy.start()
        copies.append(copy)
    for n in range(out_loss.shape[0]):
        out_loss[n] = loss[0, n]
    wait_all(copies)


def deliver(count, loss, *held):
    outside = pl.BlockSpec(memory_space=pl.ANY)
    return pl.pallas_call(
        deliver_kernel,
        out_shape=(jax.ShapeDtypeStruct((count,), jnp.float32),)
        + tuple(jax.ShapeDtypeStruct(h.shape, h.dtype) for h in held),
        in_specs=[pl.BlockSpec(memory_space=pltpu.VMEM)] * (1 + len(held)),
        out_specs=(pl.BlockSpec(memory_space=pltpu.SMEM),) + (outside,) * len(held),
        scratch_shapes=[pltpu.SemaphoreType.DMA((len(held),))],
        compiler_params=pltpu.CompilerParams(vmem_limit_bytes=8 * 1024 * 1024),
    )(loss, *held)


def fused_device(
    features,
    image_ids,
    text_embeds,
    text_ids,
    depth_kernel,
    depth_bias,
    norm_gain,
    w_up,
    w_down,
    projection,
    logit_scale,
    logit_bias,
):
    count, _, _, channels = features.shape
    hidden = w_up.shape[1]
    width = projection.shape[1]
    texts = text_ids.shape[0]
    text_rows = text_embeds.shape[0]
    cells = count * GRID * GRID
    rows = cells + -cells % (2 * ROWS)
    chip = channels // SIDE
    share = chip // CORES
    strip = 2 * LANES
    planes = SIDE * CORES
    own_tiles = channels // LANES // planes
    whole = pl.BlockSpec(memory_space=pltpu.VMEM)
    outside = pl.BlockSpec(memory_space=pl.ANY)

    def room(*shape):
        return pltpu.VMEM(shape, jnp.float32)

    def narrow(*shape):
        return pltpu.VMEM(shape, jnp.bfloat16)

    def result(*shape):
        return pltpu.VMEM(shape, jnp.float32)

    results = pl.pallas_call(
        fused_kernel,
        out_shape=(
            result(1, LANES),
            result(text_rows, width),
            result(GRID, GRID, channels),
            result(1, channels),
            result(1, channels),
            result(share, hidden),
            result(share, hidden),
            result(LANES // CORES, width),
        ),
        in_specs=[whole] * 2 + [outside] * 3 + [whole] * 7,
        out_specs=(whole,) * 8,
        scratch_shapes=[
            narrow(channels, hidden),
            narrow(channels, hidden),
            narrow(channels, width),
            room(count, GRID, ROWS, channels),
            room(PART_ROWS, channels),
            room(count, GRID, ROWS, channels),
            room(count, GRID, ROWS, LANES),
            room(rows, channels),
            narrow(rows, channels),
            room(rows, LANES),
            room(ROWS, LANES),
            room(SIDE, ROWS, LANES),
            room(rows, hidden),
            room(rows, hidden),
            room(rows, channels),
            room(SIDE, SPLIT, channels),
            room(SIDE, rows - SPLIT, chip),
            room(SIDE, rows - SPLIT, hidden),
            narrow(SIDE * rows, chip),
            narrow(SIDE * rows, hidden),
            narrow(SPLIT, channels),
            room(SIDE, ROWS, PACKET),
            room(CORES, SIDE, ROWS, PACKET),
            room(ROWS, width // 3),
            room(planes, ROWS, width // 3),
            room(texts, width),
            room(ROWS, hidden),
            room(SIDE, ROWS, hidden),
            room(ROWS, hidden),
            room(2 * ROWS, channels),
            room(2 * ROWS, hidden + width),
            room(planes * ROWS, share + LANES + width + hidden),
            room(2, count, GRID, ROWS, LANES),
            room(channels // LANES, PART_ROWS, LANES),
            room(planes, own_tiles, PART_ROWS, LANES),
            room(own_tiles, PART_ROWS, LANES),
            room(SIDE, own_tiles, PART_ROWS, LANES),
            room(channels // LANES, PART_ROWS, LANES),
            room(hidden // strip, share, strip),
            room(hidden // strip, share, strip),
            pltpu.SemaphoreType.DMA((3,)),
            pltpu.SemaphoreType.DMA((128,)),
            pltpu.SemaphoreType.DMA((128,)),
        ],
        compiler_params=pltpu.CompilerParams(
            collective_id=2, has_side_effects=True, vmem_limit_bytes=54 * 1024 * 1024
        ),
    )(
        features,
        depth_kernel,
        w_up,
        w_down,
        projection,
        depth_bias[None, :],
        norm_gain[None, :],
        text_embeds,
        image_ids[None, :],
        text_ids[None, :],
        logit_scale[None, :],
        logit_bias[None, :],
    )
    loss, grad_texts, grad_kernel, grad_bias, grad_gain, grad_up, grad_down, grad_proj = deliver(
        count, *results
    )
    return (
        loss,
        grad_texts,
        grad_kernel,
        grad_bias[0],
        grad_gain[0],
        grad_up,
        grad_down,
        grad_proj,
    )


def fits_fused(mesh):
    return mesh.shape["dp"] == SIDE and mesh.shape["loop"] == SIDE * CORES


def solution(mesh):
    placed = (
        P("loop", None, None, None),
        P("loop"),
        P("loop", None),
        P(),
        P(),
        P(),
        P(),
        P(None, "dp"),
        P(None, "dp"),
        P(),
        P(),
        P(),
    )
    fused = fits_fused(mesh)
    return jax.shard_map(
        fused_device if fused else general_device,
        mesh=mesh,
        in_specs=placed,
        out_specs=(
            P("loop"),
            P("loop", None),
            P(),
            P(),
            P(),
            P("loop", "dp"),
            P("loop", "dp"),
            P(("dp", "loop"), None),
        ),
        check_vma=False,
    )
```
